32 devices in a mesh: dp: 4 (over x, core), ctx: 4 (over z), fsdp: 2 (over y).
Axes of the slice: x: 2, y: 2, z: 4, core: 2. Of those that a mesh axis runs over, the one named last changes fastest.
Arguments:
- tokens: bfloat16 [16, 2048, 768], P(('dp', 'fsdp'), 'ctx'), may hold values from -6 to 6
- cotangent: bfloat16 [16, 2048, 768], P(('dp', 'fsdp'), 'ctx'), may hold values from -6 to 6
- qkv_weight: bfloat16 [768, 2304], P(('dp', 'fsdp')), may hold values from -8 to 8
- out_weight: bfloat16 [768, 768], P(('dp', 'fsdp')), may hold values from -0.75 to 0.75
- up_weight: bfloat16 [768, 2304], P(('dp', 'fsdp')), may hold values from -0.21875 to 0.21875
- down_weight: bfloat16 [1152, 768], P(('dp', 'fsdp')), may hold values from -0.1875 to 0.1875
- attention_gain: bfloat16 [768], P(('dp', 'fsdp')), may hold values from 0.25 to 1.75
- feedforward_gain: bfloat16 [768], P(('dp', 'fsdp')), may hold values from 0.25 to 1.75
Outputs:
- output: bfloat16 [16, 2048, 768], P(('dp', 'fsdp'), 'ctx')
- token_grad: float32 [16, 2048, 768], P(('dp', 'fsdp'), 'ctx')
- grad_qkv: float32 [768, 2304], P(('dp', 'fsdp'))
- grad_out: float32 [768, 768], P(('dp', 'fsdp'))
- grad_up: float32 [768, 2304], P(('dp', 'fsdp'))
- grad_down: float32 [1152, 768], P(('dp', 'fsdp'))
- grad_attention_gain: float32 [768], P(('dp', 'fsdp'))
- grad_feedforward_gain: float32 [768], P(('dp', 'fsdp'))
The draws below stay inside these ranges and needn't reach their ends.
All inputs are finite; a program needn't handle non-finite values.
Results may differ from the reference program's by a relative error of at most 0.02.
Values may be sent and summed in bfloat16 or wider, within the bound.
A program may use at most 320 MiB of HBM per device.

```python
import jax
import jax.numpy as jnp
from jax import lax

D = 768
HEADS = 12
HEAD = 64
FF = 1152
LEN = 2048
SEQS = 16


def draw_qkv_weight(key, part):
    value_key = jax.random.fold_in(jax.random.fold_in(key, 7), 0)
    spread = D ** (-0.5)
    entries = jnp.clip(jax.random.normal(value_key, (D, 3 * D), jnp.float32), -6.0, 6.0) * spread
    return entries.astype(jnp.bfloat16)


def level_of(stream_key, dims, cuts, least, top_value):
    level = 1.0
    for dim, shards_of in cuts:
        heights = jax.random.uniform(jax.random.fold_in(jax.random.fold_in(stream_key, 6), dim), (shards_of,), jnp.float32, least / len(cuts), top_value / len(cuts))
        level = level * jnp.repeat(jnp.exp(heights), dims[dim] // shards_of).reshape((-1,) + (1,) * (len(dims) - 1 - dim))
    return level


def normal_values(key, dims, width, most, shards=(), held_as=jnp.bfloat16):
    array = width * jax.random.normal(key, dims, jnp.float32)
    if shards:
        array = array * level_of(key, dims, shards, -0.22, 0.18)
    return jnp.clip(array, -most, most).astype(held_as)


def setup_inputs(seed: int = 0) -> dict:
    arg_keys = jax.random.split(jax.random.key(seed), 9)
    tokens = normal_values(arg_keys[0], (SEQS, LEN, D), 1.0, 6.0, ((0, 8), (1, 4)))
    cotangent = normal_values(arg_keys[1], (SEQS, LEN, D), 1.0, 6.0, ((0, 8), (1, 4)))
    qkv_weight = draw_qkv_weight(jax.random.fold_in(arg_keys[8], 71), 0)
    out_weight = normal_values(arg_keys[3], (D, D), HEAD ** -0.5, 0.75, ((0, 8),))
    up_weight = normal_values(arg_keys[4], (D, 2 * FF), D ** -0.5, 0.21875, ((0, 8),))
    down_weight = normal_values(arg_keys[5], (FF, D), FF ** -0.5, 0.1875, ((0, 8),))
    attention_gain = jnp.clip(1.0 + 0.15 * jax.random.normal(arg_keys[6], (D,), jnp.float32), 0.25, 1.75).astype(jnp.bfloat16)
    feedforward_gain = jnp.clip(1.0 + 0.15 * jax.random.normal(arg_keys[7], (D,), jnp.float32), 0.25, 1.75).astype(jnp.bfloat16)
    return {"tokens": tokens, "cotangent": cotangent, "qkv_weight": qkv_weight, "out_weight": out_weight, "up_weight": up_weight, "down_weight": down_weight, "attention_gain": attention_gain, "feedforward_gain": feedforward_gain}


norm_eps = 1e-05
rope_base = 160000.0

def layer_norm(values, norm_gain):
    centre = lax.optimization_barrier(jnp.mean(values, -1, keepdims=True))
    centred = values - centre
    inverse = lax.rsqrt(lax.optimization_barrier(jnp.mean(centred * centred, -1, keepdims=True)) + norm_eps)
    normed = centred * inverse
    return (normed, inverse, normed * norm_gain)

def norm_back(upstream, normed, inverse, norm_gain):
    scaled = upstream * norm_gain
    return (scaled - lax.optimization_barrier(jnp.mean(scaled, -1, keepdims=True)) - normed * lax.optimization_barrier(jnp.mean(scaled * normed, -1, keepdims=True))) * inverse

def gated_gelu(inputs, gating):
    return jax.nn.gelu(inputs, approximate=False) * gating

def rope_tables(positions, head_size):
    half_size = head_size // 2
    frequency = rope_base ** (-2.0 * jnp.arange(half_size, dtype=jnp.float32) / head_size)
    angles = positions.astype(jnp.float32)[:, None] * frequency[None, :]
    cosine = jnp.cos(angles)
    sine_half = jnp.sin(angles)
    return (jnp.concatenate([cosine, cosine], -1), jnp.concatenate([sine_half, sine_half], -1))

def rotate_heads(values, cosine_table, sine_table):
    half_size = values.shape[-1] // 2
    turned = jnp.concatenate([-values[..., half_size:], values[..., :half_size]], -1)
    return values * cosine_table[:, None, :] + turned * sine_table[:, None, :]

def rounded(values):
    return lax.optimization_barrier(values.astype(jnp.bfloat16)).astype(jnp.float32)

def attend_forward(query_rows, key_rows, value_rows):
    score_scale = HEAD ** (-0.5)
    scores = jnp.einsum('qhd,khd->hqk', query_rows.astype(jnp.float32), key_rows.astype(jnp.float32)) * score_scale
    highest = lax.optimization_barrier(jnp.max(scores, -1, keepdims=True))
    log_total = highest[..., 0] + jnp.log(lax.optimization_barrier(jnp.sum(jnp.exp(scores - highest), -1)))
    weights = rounded(jnp.exp(scores - log_total[..., None]))
    attended = jnp.einsum('hqk,khd->qhd', weights, value_rows.astype(jnp.float32))
    return (attended.astype(jnp.bfloat16), log_total)

def attend_backward(query_rows, key_rows, value_rows, attended, upstream, log_total):
    score_scale = HEAD ** (-0.5)
    query_wide = query_rows.astype(jnp.float32)
    key_wide = key_rows.astype(jnp.float32)
    value_wide = value_rows.astype(jnp.float32)
    upstream_wide = upstream.astype(jnp.float32)
    scores = jnp.einsum('qhd,khd->hqk', query_wide, key_wide) * score_scale
    weights = jnp.exp(scores - log_total[..., None])
    weight_grad = jnp.einsum('qhd,khd->hqk', upstream_wide, value_wide)
    delta_sum = jnp.transpose(lax.optimization_barrier(jnp.sum(upstream_wide * attended.astype(jnp.float32), -1)))
    score_grad = rounded(weights * (weight_grad - delta_sum[..., None]))
    query_grad = jnp.einsum('hqk,khd->qhd', score_grad, key_wide) * score_scale
    key_grad = jnp.einsum('hqk,qhd->khd', score_grad, query_wide) * score_scale
    value_grad = jnp.einsum('hqk,qhd->khd', rounded(weights), upstream_wide)
    return (query_grad, key_grad, value_grad)

def one_sequence(tokens, cotangent, qkv_weight, out_weight, up_weight, down_weight, attention_gain, feedforward_gain):
    length = tokens.shape[0]
    attn_gain = attention_gain.astype(jnp.float32)
    ffn_gain = feedforward_gain.astype(jnp.float32)
    inputs = tokens.astype(jnp.float32)
    normed_a, inverse_a, scaled_a = layer_norm(inputs, attn_gain)
    normal_a = scaled_a.astype(jnp.bfloat16)
    projected = jnp.dot(normal_a, qkv_weight, preferred_element_type=jnp.float32)
    cosine_table, sine_table = rope_tables(jnp.arange(length, dtype=jnp.int32), HEAD)
    head_shape = (length, HEADS, HEAD)
    query_rows = rotate_heads(projected[:, :D].reshape(head_shape), cosine_table, sine_table).astype(jnp.bfloat16)
    key_rows = rotate_heads(projected[:, D:2 * D].reshape(head_shape), cosine_table, sine_table).astype(jnp.bfloat16)
    value_rows = projected[:, 2 * D:].reshape(head_shape).astype(jnp.bfloat16)
    attended, log_total = attend_forward(query_rows, key_rows, value_rows)
    attended_flat = attended.reshape(length, D)
    residual = inputs + jnp.dot(attended_flat, out_weight, preferred_element_type=jnp.float32)
    normed_b, inverse_b, scaled_b = layer_norm(residual, ffn_gain)
    normal_b = scaled_b.astype(jnp.bfloat16)
    widened = jnp.dot(normal_b, up_weight, preferred_element_type=jnp.float32)
    hidden, hidden_back = jax.vjp(gated_gelu, widened[:, :FF], widened[:, FF:])
    hidden_low = hidden.astype(jnp.bfloat16)
    output = (residual + jnp.dot(hidden_low, down_weight, preferred_element_type=jnp.float32)).astype(jnp.bfloat16)
    down_grad = jnp.dot(hidden_low.T, cotangent, preferred_element_type=jnp.float32)
    hidden_grad = jnp.dot(cotangent, down_weight.T, preferred_element_type=jnp.float32)
    input_grad, gating_grad = hidden_back(hidden_grad)
    widened_grad = jnp.concatenate([input_grad, gating_grad], -1).astype(jnp.bfloat16)
    up_grad = jnp.dot(normal_b.T, widened_grad, preferred_element_type=jnp.float32)
    normal_b_grad = jnp.dot(widened_grad, up_weight.T, preferred_element_type=jnp.float32)
    ffn_gain_grad = lax.optimization_barrier(jnp.sum(normal_b_grad * normed_b, 0))
    residual_grad = cotangent.astype(jnp.float32) + norm_back(normal_b_grad, normed_b, inverse_b, ffn_gain)
    residual_low = residual_grad.astype(jnp.bfloat16)
    out_grad = jnp.dot(attended_flat.T, residual_low, preferred_element_type=jnp.float32)
    attended_grad = jnp.dot(residual_low, out_weight.T, preferred_element_type=jnp.float32).astype(jnp.bfloat16).reshape(head_shape)
    query_grad, key_grad, value_grad = attend_backward(query_rows, key_rows, value_rows, attended, attended_grad, log_total)
    query_grad = rotate_heads(query_grad, cosine_table, -sine_table)
    key_grad = rotate_heads(key_grad, cosine_table, -sine_table)
    projected_grad = jnp.concatenate([query_grad.reshape(length, D), key_grad.reshape(length, D), value_grad.reshape(length, D)], -1).astype(jnp.bfloat16)
    qkv_grad = jnp.dot(normal_a.T, projected_grad, preferred_element_type=jnp.float32)
    normal_a_grad = jnp.dot(projected_grad, qkv_weight.T, preferred_element_type=jnp.float32)
    attn_gain_grad = lax.optimization_barrier(jnp.sum(normal_a_grad * normed_a, 0))
    token_grad = residual_grad + norm_back(normal_a_grad, normed_a, inverse_a, attn_gain)
    return (output, token_grad, (qkv_grad, out_grad, up_grad, down_grad, attn_gain_grad, ffn_gain_grad))

def reference(tokens, cotangent, qkv_weight, out_weight, up_weight, down_weight, attention_gain, feedforward_gain):
    start_grads = (jnp.zeros(qkv_weight.shape, jnp.float32), jnp.zeros(out_weight.shape, jnp.float32), jnp.zeros(up_weight.shape, jnp.float32), jnp.zeros(down_weight.shape, jnp.float32), jnp.zeros((D,), jnp.float32), jnp.zeros((D,), jnp.float32))

    def advance(running, pair_now):
        output, token_grad, fresh = one_sequence(pair_now[0], pair_now[1], qkv_weight, out_weight, up_weight, down_weight, attention_gain, feedforward_gain)
        return (jax.tree.map(jnp.add, running, fresh), (output, token_grad))
    summed, (output, token_grad) = lax.scan(advance, start_grads, (tokens, cotangent))
    return (output, token_grad, summed[0], summed[1], summed[2], summed[3], summed[4], summed[5])
```

```python
from functools import partial
import math

import jax
import jax.numpy as jnp
from jax import lax
from jax.experimental import pallas as pl
from jax.experimental.pallas import tpu as pltpu
from jax.sharding import PartitionSpec as P

D = 768
HEADS = 12
HEAD = 64
FF = 1152
HALF = HEAD // 2

norm_eps = 1e-05
rope_base = 160000.0
score_scale = HEAD ** (-0.5)
score_base2 = score_scale * math.log2(math.e)
WEIGHT_AXES = ("dp", "fsdp")
f32 = jnp.float32
bf16 = jnp.bfloat16


def dot(left, right, left_dim=1, right_dim=0):
    return lax.dot_general(
        left, right, (((left_dim,), (right_dim,)), ((), ())), preferred_element_type=f32
    )


def layer_norm(values, norm_gain):
    centre = jnp.mean(values, -1, keepdims=True)
    centred = values - centre
    inverse = lax.rsqrt(jnp.mean(centred * centred, -1, keepdims=True) + norm_eps)
    normed = centred * inverse
    return (normed, inverse, normed * norm_gain)


def norm_back(upstream, normed, inverse, norm_gain):
    scaled = upstream * norm_gain
    return (
        scaled
        - jnp.mean(scaled, -1, keepdims=True)
        - normed * jnp.mean(scaled * normed, -1, keepdims=True)
    ) * inverse


def gated_gelu(inputs, gating):
    return jax.nn.gelu(inputs, approximate=False) * gating


def rope_rows(length):
    frequency = rope_base ** (-2.0 * jnp.arange(HALF, dtype=f32) / HEAD)
    angles = frequency[:, None] * jnp.arange(length, dtype=jnp.int32).astype(f32)[None, :]
    return (jnp.cos(angles), jnp.sin(angles))


def chunk_of(length, most):
    return most if length % most == 0 else length


def forward_kernel(q_ref, k_ref, v_ref, o_ref, log_ref, k_rows, v_wide):
    length = k_ref.shape[-1]
    chunk = chunk_of(length, 512)

    @pl.when(pl.program_id(1) == 0)
    def _():
        k_rows[...] = k_ref[0, 0].T
        v_wide[:HEAD, :] = v_ref[0, 0]
        v_wide[HEAD:, :] = jnp.ones((v_wide.shape[0] - HEAD, length), bf16)

    query = q_ref[0, 0]
    highest = None
    total = None
    for start in range(0, length, chunk):
        scores = dot(k_rows[start : start + chunk, :], query) * score_base2
        top = jnp.max(scores, 0, keepdims=True)
        new_high = top if highest is None else jnp.maximum(highest, top)
        weights = jnp.exp2(scores - new_high).astype(bf16)
        term = dot(v_wide[:, start : start + chunk], weights)
        total = term if total is None else total * jnp.exp2(highest - new_high) + term
        highest = new_high
    denominator = total[HEAD : HEAD + 1, :]
    o_ref[0, 0] = (total[:HEAD, :] / denominator).astype(bf16)
    log_ref[0] = highest + jnp.log2(denominator)


def attend(heads_t, block_len):
    _, count, _, length = heads_t.shape
    blocks = length // block_len
    return pl.pallas_call(
        forward_kernel,
        grid=(count, blocks),
        in_specs=[
            pl.BlockSpec((1, 1, HEAD, block_len), lambda h, c: (0, h, 0, c)),
            pl.BlockSpec((1, 1, HEAD, length), lambda h, c: (1, h, 0, 0)),
            pl.BlockSpec((1, 1, HEAD, length), lambda h, c: (2, h, 0, 0)),
        ],
        out_specs=[
            pl.BlockSpec((1, 1, HEAD, block_len), lambda h, c: (c, h, 0, 0)),
            pl.BlockSpec((1, 1, block_len), lambda h, c: (h, 0, c)),
        ],
        out_shape=[
            jax.ShapeDtypeStruct((blocks, count, HEAD, block_len), bf16),
            jax.ShapeDtypeStruct((count, 1, length), f32),
        ],
        scratch_shapes=[
            pltpu.VMEM((length, HEAD), bf16),
            pltpu.VMEM((HEAD + 16, length), bf16),
        ],
        compiler_params=pltpu.CompilerParams(vmem_limit_bytes=40 << 20),
        cost_estimate=pl.CostEstimate(
            flops=16 * count * length * length * HEAD,
            bytes_accessed=10 * count * length * HEAD,
            transcendentals=count * length * length,
        ),
    )(heads_t, heads_t, heads_t)


def rope_back(grad_t, cosine, sine):
    first, second = grad_t[:HALF, :], grad_t[HALF:, :]
    return (first * cosine + second * sine, second * cosine - first * sine)


def backward_kernel(
    q_ref, k_ref, v_ref, o_ref, up_ref, log_ref, cos_all, sin_all, cos_ref, sin_ref,
    dq_ref, dk_ref, dv_ref, q_rows, up_rows, up_cols, delta, dq_sum,
):
    step = pl.program_id(1)
    blocks, block_len = up_ref.shape[0], up_ref.shape[-1]
    length = q_ref.shape[-1]
    chunk = chunk_of(length, 512)

    @pl.when(step == 0)
    def _():
        q_rows[...] = q_ref[0, 0].T
        for number in range(blocks):
            place = slice(number * block_len, (number + 1) * block_len)
            upstream = up_ref[number, 0]
            up_cols[:, place] = upstream
            up_rows[place, :] = upstream.T
            delta[:, place] = jnp.sum(
                upstream.astype(f32) * o_ref[number, 0].astype(f32), 0, keepdims=True
            )
        dq_sum[...] = jnp.zeros_like(dq_sum)

    key_t = k_ref[0, 0]
    key = key_t.T
    value = v_ref[0, 0].T
    dk = None
    dv = None
    for start in range(0, length, chunk):
        place = slice(start, start + chunk)
        scores = dot(key, q_ref[0, 0, :, place]) * score_base2
        weights = jnp.exp2(scores - log_ref[0, :, place])
        weight_grad = dot(value, up_cols[:, place])
        score_grad = (weights * (weight_grad - delta[:, place])).astype(bf16)
        dv_term = dot(weights.astype(bf16), up_rows[place, :])
        dk_term = dot(score_grad, q_rows[place, :])
        dv = dv_term if dv is None else dv + dv_term
        dk = dk_term if dk is None else dk + dk_term
        dq_sum[:, place] += dot(key_t, score_grad)
    upper, lower = rope_back((dk * score_scale).T, cos_ref[...], sin_ref[...])
    dk_ref[0, :HALF, :] = upper.astype(bf16)
    dk_ref[0, HALF:, :] = lower.astype(bf16)
    dv_ref[0] = dv.T.astype(bf16)

    @pl.when(step == pl.num_programs(1) - 1)
    def _():
        upper, lower = rope_back(dq_sum[...] * score_scale, cos_all[...], sin_all[...])
        dq_ref[0, :HALF, :] = upper.astype(bf16)
        dq_ref[0, HALF:, :] = lower.astype(bf16)


def attend_back(heads_t, attended, upstream, log_total, cosine, sine):
    _, count, _, length = heads_t.shape
    blocks, _, _, block_len = attended.shape
    rows = chunk_of(length, 256)
    split = pl.BlockSpec((blocks, 1, HEAD, block_len), lambda h, k: (0, h, 0, 0))
    shape = jax.ShapeDtypeStruct((count, HEAD, length), bf16)
    return pl.pallas_call(
        backward_kernel,
        grid=(count, length // rows),
        in_specs=[
            pl.BlockSpec((1, 1, HEAD, length), lambda h, k: (0, h, 0, 0)),
            pl.BlockSpec((1, 1, HEAD, rows), lambda h, k: (1, h, 0, k)),
            pl.BlockSpec((1, 1, HEAD, rows), lambda h, k: (2, h, 0, k)),
            split,
            split,
            pl.BlockSpec((1, 1, length), lambda h, k: (h, 0, 0)),
            pl.BlockSpec((HALF, length), lambda h, k: (0, 0)),
            pl.BlockSpec((HALF, length), lambda h, k: (0, 0)),
            pl.BlockSpec((HALF, rows), lambda h, k: (0, k)),
            pl.BlockSpec((HALF, rows), lambda h, k: (0, k)),
        ],
        out_specs=[
            pl.BlockSpec((1, HEAD, length), lambda h, k: (h, 0, 0)),
            pl.BlockSpec((1, HEAD, rows), lambda h, k: (h, 0, k)),
            pl.BlockSpec((1, HEAD, rows), lambda h, k: (h, 0, k)),
        ],
        out_shape=[shape, shape, shape],
        scratch_shapes=[
            pltpu.VMEM((length, HEAD), bf16),
            pltpu.VMEM((length, HEAD), bf16),
            pltpu.VMEM((HEAD, length), bf16),
            pltpu.VMEM((1, length), f32),
            pltpu.VMEM((HEAD, length), f32),
        ],
        compiler_params=pltpu.CompilerParams(vmem_limit_bytes=40 << 20),
        cost_estimate=pl.CostEstimate(
            flops=40 * count * length * length * HEAD,
            bytes_accessed=16 * count * length * HEAD,
            transcendentals=count * length * length,
        ),
    )(heads_t, heads_t, heads_t, attended, upstream, log_total, cosine, sine, cosine, sine)


def gather_rows(shard):
    return lax.all_gather(shard, WEIGHT_AXES, axis=0, tiled=True)


def exchange(blocks):
    return lax.all_to_all(blocks, "ctx", 0, 0, tiled=True)


def general_body(
    tokens,
    cotangent,
    qkv_weight,
    out_weight,
    up_weight,
    down_weight,
    attention_gain,
    feedforward_gain,
):
    ctx = lax.axis_size("ctx")
    groups = lax.axis_size("dp") * lax.axis_size("fsdp")
    seq_count, block_len = (tokens.shape[0], tokens.shape[1])
    length = block_len * ctx
    sets = math.gcd(seq_count, ctx)
    each = seq_count // sets
    teams = ctx // sets
    own = -(-HEADS // teams)
    width = own * HEAD
    spare = teams * own - HEADS
    halves = 2 if own % 2 == 0 else 1
    part = own // halves
    shard_rows = qkv_weight.shape[0]
    row_count = seq_count * block_len

    moved = [
        exchange(jnp.repeat(tokens[turn::each], teams, axis=0)).reshape(length, D)
        for turn in range(each)
    ]

    by_head = qkv_weight.reshape(shard_rows, 3, D)
    if spare:
        by_head = jnp.pad(by_head, ((0, 0), (0, 0), (0, spare * HEAD)))
    team = lax.rem(lax.axis_index("ctx"), teams)
    own_columns = lax.dynamic_slice_in_dim(by_head, team * width, width, 2)
    gain_columns = jnp.pad(
        jnp.stack([attention_gain, feedforward_gain], -1), ((0, 0), (0, 126))
    )
    first_gather = gather_rows(
        jnp.concatenate([own_columns.reshape(shard_rows, 3 * width), gain_columns], -1)
    )
    qkv_own = first_gather[:, : 3 * width]
    attn_gain = first_gather[:, 3 * width].astype(f32)
    ffn_gain = first_gather[:, 3 * width + 1].astype(f32)
    out_whole = gather_rows(out_weight)
    up_whole = gather_rows(up_weight)
    down_whole = gather_rows(down_weight)
    cosine, sine = rope_rows(length)

    saved = []
    for turn in range(each):
        normal = layer_norm(moved[turn].astype(f32), attn_gain)[2].astype(bf16)
        by_part = qkv_own.reshape(D, 3, halves, part * HEAD)
        pieces = []
        for half in range(halves):
            weight = by_part[:, :, half].reshape(D, 3 * part * HEAD)
            projected = dot(weight, normal, 0, 1).reshape(3, part, 2, HALF, length)
            first, second = (projected[:2, :, 0], projected[:2, :, 1])
            turned = jnp.stack(
                [first * cosine - second * sine, second * cosine + first * sine], 2
            )
            heads_t = (
                jnp.concatenate([turned, projected[2:]], 0)
                .astype(bf16)
                .reshape(3, part, HEAD, length)
            )
            attended, log_total = attend(heads_t, block_len)
            pieces.append((heads_t, attended, log_total, exchange(attended)))
        saved.append((normal, pieces))

    columns = []
    for number in range(seq_count):
        chosen, turn = divmod(number, each)
        got = [
            piece[3].reshape(sets, teams, part, HEAD, block_len)[chosen]
            for piece in saved[turn][1]
        ]
        columns.append(jnp.concatenate(got, 1).reshape(teams * width, block_len)[:D])
    attended_t = jnp.concatenate(columns, 1)

    inputs = tokens.reshape(row_count, D).astype(f32)
    residual = inputs + dot(attended_t, out_whole, 0, 0)
    normed_b, inverse_b, scaled_b = layer_norm(residual, ffn_gain)
    normal_b = scaled_b.astype(bf16)
    widened = dot(normal_b, up_whole)
    hidden, hidden_back = jax.vjp(gated_gelu, widened[:, :FF], widened[:, FF:])
    hidden_low = hidden.astype(bf16)
    output = (residual + dot(hidden_low, down_whole)).astype(bf16)
    upstream = cotangent.reshape(row_count, D)
    hidden_grad = dot(upstream, down_whole, 1, 1)
    input_grad, gating_grad = hidden_back(hidden_grad)
    widened_grad = jnp.concatenate([input_grad, gating_grad], -1).astype(bf16)
    normal_b_grad = dot(widened_grad, up_whole, 1, 1)
    residual_grad = upstream.astype(f32) + norm_back(normal_b_grad, normed_b, inverse_b, ffn_gain)
    residual_low = residual_grad.astype(bf16)

    out_heads = out_whole
    if spare:
        out_heads = jnp.pad(out_heads, ((0, spare * HEAD), (0, 0)))
    out_heads = out_heads.reshape(teams, halves, part * HEAD, D)
    arrived = []
    for turn in range(each):
        for half in range(halves):
            weight = out_heads[:, half].reshape(teams * part * HEAD, D)
            sent = [
                dot(weight, residual_low[start : start + block_len], 1, 1).astype(bf16)
                for start in range(turn * block_len, row_count, each * block_len)
            ]
            arrived.append(exchange(jnp.stack(sent).reshape(ctx, part, HEAD, block_len)))

    down_grad = dot(hidden_low, upstream, 0, 0)
    up_grad = dot(normal_b, widened_grad, 0, 0)
    out_grad = dot(attended_t, residual_low)

    parts = [up_grad[:, start : start + D] for start in range(0, up_grad.shape[1], D)]
    parts += [down_grad, out_grad]
    packed = jnp.concatenate([item.astype(bf16).reshape(groups, -1, D) for item in parts], 1)
    shard = lax.psum_scatter(packed, WEIGHT_AXES, scatter_dimension=0, tiled=True)[0]
    shard = lax.psum(shard, "ctx").astype(f32)
    cuts = []
    offset = 0
    for item in parts:
        rows = item.shape[0] // groups
        cuts.append(shard[offset : offset + rows])
        offset += rows
    up_shard = jnp.concatenate(cuts[:-2], -1)
    down_shard, out_shard = cuts[-2:]

    back = []
    qkv_grad = 0.0
    for turn in range(each):
        normal, pieces = saved[turn]
        grads = []
        for half in range(halves):
            heads_t, attended, log_total, _ = pieces[half]
            grads.append(
                attend_back(
                    heads_t, attended, arrived[turn * halves + half], log_total, cosine, sine
                )
            )
        projected_grad = jnp.concatenate(
            [grads[half][which] for which in range(3) for half in range(halves)], 0
        ).reshape(3 * width, length)
        partial_grad = dot(projected_grad, qkv_own, 0, 1).astype(bf16)
        terms = exchange(partial_grad.reshape(ctx, block_len, D))
        back.append(terms.reshape(sets, teams, block_len, D).astype(f32).sum(1))
        qkv_grad = qkv_grad + dot(normal, projected_grad, 0, 1)
    normal_a_grad = jnp.stack(back, 1).reshape(row_count, D)
    normed_a, inverse_a, _ = layer_norm(inputs, attn_gain)
    token_grad = residual_grad + norm_back(normal_a_grad, normed_a, inverse_a, attn_gain)
    qkv_cut = lax.psum_scatter(
        qkv_grad.astype(bf16), WEIGHT_AXES, scatter_dimension=0, tiled=True
    )
    qkv_all = lax.all_gather(qkv_cut, "ctx", axis=0).astype(f32)
    qkv_all = qkv_all.reshape(sets, teams, shard_rows, 3, width).sum(0)
    qkv_shard = jnp.transpose(qkv_all, (1, 2, 0, 3)).reshape(shard_rows, 3, teams * width)
    qkv_shard = qkv_shard[:, :, :D].reshape(shard_rows, 3 * D)
    attn_gain_grad = jnp.sum(qkv_weight.astype(f32) * qkv_shard, -1) / attention_gain.astype(f32)
    ffn_gain_grad = jnp.sum(up_weight.astype(f32) * up_shard, -1) / feedforward_gain.astype(f32)
    return (
        output.reshape(seq_count, block_len, D),
        token_grad.reshape(seq_count, block_len, D),
        qkv_shard,
        out_shard,
        up_shard,
        down_shard,
        attn_gain_grad,
        ffn_gain_grad,
    )


MESH_ID = pl.DeviceIdType.MESH
VMEM_LIMIT = 60 << 20
vmem_spec = pl.BlockSpec(memory_space=pltpu.VMEM)
any_spec = pl.BlockSpec(memory_space=pl.ANY)


def here():
    dp = lax.axis_index("dp")
    return dp, lax.rem(dp, 2), dp // 2, lax.axis_index("ctx"), lax.axis_index("fsdp")


def params(number):
    return pltpu.CompilerParams(
        collective_id=number, has_side_effects=True, vmem_limit_bytes=VMEM_LIMIT
    )


def greet(partners):
    barrier = pltpu.get_barrier_semaphore()
    for partner in partners:
        pl.semaphore_signal(barrier, inc=1, device_id=partner, device_id_type=MESH_ID)
    pl.semaphore_wait(barrier, len(partners))


def remote(src, dst, send_sem, recv_sem, **device):
    return pltpu.make_async_remote_copy(
        src_ref=src, dst_ref=dst, send_sem=send_sem, recv_sem=recv_sem,
        device_id=device, device_id_type=MESH_ID,
    )


def near_order(place, count):
    def at(turn):
        block = place
        bit = 1
        while bit < count:
            flip = lax.rem(turn // bit, 2)
            block = block + flip * (bit - 2 * bit * lax.rem(place // bit, 2))
            bit *= 2
        return block
    return at


def prologue_kernel(
    ctx, nfsdp, groups, seqs,
    x_ref, w_ref, g_ref, cos_ref, sin_ref,
    heads_ref, normal_ref, half_ref, wt_ref, gain_ref,
    xbuf, wbuf, gbuf,
    send_x, recv_x, fwd_x, local_x, send_w, recv_w, local_w, send_g, recv_g, local_g,
):
    dp, core, x, z, y = here()
    sibling = dp + 1 - 2 * core
    block_len = x_ref.shape[1]
    shard_rows = w_ref.shape[0]
    width = wbuf.shape[1] // 3
    heads = width // HEAD
    me = dp * nfsdp + y
    lead = z // seqs == core
    others = []
    for j in range(1, groups):
        other = lax.rem(me + j, groups)
        others.append((other // nfsdp, lax.rem(other, nfsdp)))
    greet(
        [{"ctx": lax.rem(z + k, ctx)} for k in range(1, ctx)]
        + [{"dp": d, "fsdp": f} for d, f in others]
    )

    def column_copy(s):
        return remote(x_ref.at[s], xbuf.at[z], send_x.at[s], recv_x.at[z], ctx=core * seqs + s)

    def sibling_copy(s):
        return remote(x_ref.at[s], xbuf.at[z], send_x.at[s], recv_x.at[z], dp=sibling)

    for s in range(seqs):
        keep = core * seqs + s == z

        @pl.when(jnp.logical_not(keep))
        def _():
            column_copy(s).start()

        @pl.when(keep)
        def _():
            sibling_copy(s).start()
            own = pltpu.make_async_copy(x_ref.at[s], xbuf.at[z], local_x)
            own.start()
            own.wait()

    def weight_copy(j, part):
        d, f = others[j - 1]
        columns = pl.multiple_of(part * D + lax.rem(d, 2) * width, 128)
        return remote(
            w_ref.at[:, pl.ds(columns, width)],
            wbuf.at[pl.ds(pl.multiple_of(me * shard_rows, 16), shard_rows), pl.ds(part * width, width)],
            send_w.at[j - 1, part], recv_w.at[j - 1, part], dp=d, fsdp=f,
        )

    def gain_copy(j):
        d, f = others[j - 1]
        return remote(g_ref, gbuf.at[me], send_g.at[j - 1], recv_g.at[j - 1], dp=d, fsdp=f)

    for j in range(1, groups):
        gain_copy(j).start()
        for part in range(3):
            weight_copy(j, part).start()
    own = [pltpu.make_async_copy(g_ref, gbuf.at[me], local_g)]
    for part in range(3):
        columns = pl.multiple_of(part * D + core * width, 128)
        own.append(pltpu.make_async_copy(
            w_ref.at[:, pl.ds(columns, width)],
            wbuf.at[pl.ds(pl.multiple_of(me * shard_rows, 16), shard_rows), pl.ds(part * width, width)],
            local_w.at[part],
        ))
    for copy in own:
        copy.start()
    for copy in own:
        copy.wait()
    for j in range(1, groups):
        gain_copy(j).wait_recv()
        for part in range(3):
            weight_copy(j, part).wait_recv()

    gains = gbuf[0].astype(f32)
    for number in range(1, groups):
        gains = gains + gbuf[number].astype(f32)
    gain_ref[...] = gains
    wt_ref[...] = wbuf[...].T
    attn_gain = gains[0:1, :]
    order = near_order(z, ctx)

    def forward_copy(block):
        return remote(xbuf.at[block], xbuf.at[block], fwd_x.at[block], recv_x.at[block], dp=sibling)

    def turn(number, carry):
        block = order(number)

        @pl.when(jnp.logical_or(jnp.logical_not(lead), number > 0))
        def _():
            forward_copy(block).wait_recv()

        @pl.when(jnp.logical_and(lead, number > 0))
        def _():
            forward_copy(block).start()

        place = pl.ds(pl.multiple_of(block * block_len, 128), block_len)
        normal = layer_norm(xbuf[block].astype(f32), attn_gain)[2].astype(bf16)
        normal_ref[:, place] = normal.T
        cosine, sine = cos_ref[:, place], sin_ref[:, place]
        for part in range(3):
            projected = dot(wt_ref[part * width : (part + 1) * width, :], normal, 1, 1)
            for head in range(heads):
                first = projected[head * HEAD : head * HEAD + HALF, :]
                second = projected[head * HEAD + HALF : (head + 1) * HEAD, :]
                if part < 2:
                    first, second = (
                        first * cosine - second * sine, second * cosine + first * sine
                    )
                if part == 0:
                    first, second = first * score_base2, second * score_base2
                heads_ref[part, head, :HALF, place] = first.astype(bf16)
                heads_ref[part, head, HALF:, place] = second.astype(bf16)
        return carry

    lax.fori_loop(0, ctx, turn, 0)
    half_blocks = ctx // 2
    half_ref[...] = xbuf[pl.ds(core * half_blocks, half_blocks)].reshape(half_ref.shape)

    for s in range(seqs):
        sibling_copy(s).wait_send()
    for number in range(1, ctx):
        @pl.when(lead)
        def _():
            forward_copy(order(number)).wait_send()
    for j in range(1, groups):
        gain_copy(j).wait_send()
        for part in range(3):
            weight_copy(j, part).wait_send()


def prologue(tokens, qkv_weight, gains, cosine, sine, ctx, nfsdp, groups):
    seqs, block_len, _ = tokens.shape
    length = block_len * ctx
    width = D // 2
    shard_rows = qkv_weight.shape[0]
    dma = pltpu.SemaphoreType.DMA
    return pl.pallas_call(
        partial(prologue_kernel, ctx, nfsdp, groups, seqs),
        in_specs=[any_spec, any_spec, any_spec, vmem_spec, vmem_spec],
        out_specs=[vmem_spec] * 5,
        out_shape=[
            jax.ShapeDtypeStruct((3, width // HEAD, HEAD, length), bf16),
            jax.ShapeDtypeStruct((D, length), bf16),
            jax.ShapeDtypeStruct((length // 2, D), bf16),
            jax.ShapeDtypeStruct((3 * width, D), bf16),
            jax.ShapeDtypeStruct(gains.shape, f32),
        ],
        scratch_shapes=[
            pltpu.VMEM((ctx, block_len, D), bf16),
            pltpu.VMEM((groups * shard_rows, 3 * width), bf16),
            pltpu.VMEM((groups,) + gains.shape, bf16),
            dma((seqs,)), dma((ctx,)), dma((ctx,)), dma,
            dma((groups - 1, 3)), dma((groups - 1, 3)), dma((3,)),
            dma((groups - 1,)), dma((groups - 1,)), dma,
        ],
        compiler_params=params(1),
        name="prologue",
        cost_estimate=pl.CostEstimate(
            flops=6 * width * D * length, bytes_accessed=16 * length * D, transcendentals=0
        ),
    )(tokens, qkv_weight, gains, cosine, sine)


def column_partners(ctx):
    dp, core, x, z, y = here()
    found = [{"dp": dp + 1 - 2 * core}]
    for k in range(1, ctx):
        for c in range(2):
            found.append({"dp": 2 * x + c, "ctx": lax.rem(z + k, ctx)})
    return found


def to_halves(ctx, seqs, src, dst, send_sem, recv_sem, local_sem):
    dp, core, x, z, y = here()
    half = ctx // 2
    side, slot = z // half, lax.rem(z, half)

    def outgoing(s):
        return remote(
            src.at[s], dst.at[slot], send_sem.at[s], recv_sem.at[slot],
            dp=2 * x + side, ctx=core * seqs + s,
        )

    def stays(s):
        return jnp.logical_and(core * seqs + s == z, side == core)

    def own(s):
        return pltpu.make_async_copy(src.at[s], dst.at[slot], local_sem)

    def start():
        for s in range(seqs):
            @pl.when(stays(s))
            def _():
                own(s).start()

            @pl.when(jnp.logical_not(stays(s)))
            def _():
                outgoing(s).start()

    def finish():
        for s in range(seqs):
            @pl.when(stays(s))
            def _():
                own(s).wait()

            @pl.when(jnp.logical_not(stays(s)))
            def _():
                outgoing(s).wait_send()
        for i in range(half):
            mine = jnp.logical_and(z // seqs == core, core * half + i == z)

            @pl.when(jnp.logical_not(mine))
            def _():
                remote(
                    src.at[0], dst.at[i], send_sem.at[0], recv_sem.at[i], dp=dp
                ).wait_recv()

    return start, finish


def to_blocks(ctx, seqs, src, dst, send_sem, recv_sem, local_sem):
    dp, core, x, z, y = here()
    half = ctx // 2
    side, slot = z // seqs, lax.rem(z, seqs)

    def outgoing(i):
        return remote(
            src.at[i], dst.at[slot], send_sem.at[i], recv_sem.at[slot],
            dp=2 * x + side, ctx=core * half + i,
        )

    def stays(i):
        return jnp.logical_and(core * half + i == z, side == core)

    def own(i):
        return pltpu.make_async_copy(src.at[i], dst.at[slot], local_sem)

    def start_one(i):
        @pl.when(stays(i))
        def _():
            own(i).start()

        @pl.when(jnp.logical_not(stays(i)))
        def _():
            outgoing(i).start()

    def finish():
        for i in range(half):
            @pl.when(stays(i))
            def _():
                own(i).wait()

            @pl.when(jnp.logical_not(stays(i)))
            def _():
                outgoing(i).wait_send()
        for s in range(seqs):
            mine = jnp.logical_and(z // half == core, core * seqs + s == z)

            @pl.when(jnp.logical_not(mine))
            def _():
                remote(
                    src.at[0], dst.at[s], send_sem.at[0], recv_sem.at[s], dp=dp
                ).wait_recv()

    return start_one, finish


def attend_kernel(
    ctx, seqs, q_ref, k_ref, v_ref, cot_ref, o_ref, log_ref, all_ref, half_ref,
    k_rows, v_wide, done,
    send_c, recv_c, local_c, send_o, recv_o, local_o,
):
    head, step = pl.program_id(0), pl.program_id(1)
    heads, steps = pl.num_programs(0), pl.num_programs(1)
    dp, core, x, z, y = here()
    sibling = dp + 1 - 2 * core
    length = k_ref.shape[-1]
    chunk = chunk_of(length, 512)
    block = q_ref.shape[-1]
    half = length // 2
    start, finish = to_halves(ctx, seqs, cot_ref, half_ref, send_c, recv_c, local_c)

    @pl.when(jnp.logical_and(head == 0, step == 0))
    def _():
        greet(column_partners(ctx))
        start()

    @pl.when(step == 0)
    def _():
        k_rows[...] = k_ref[0, 0].T
        v_wide[:HEAD, :] = v_ref[0, 0]
        v_wide[HEAD:, :] = jnp.ones((v_wide.shape[0] - HEAD, length), bf16)

    query = q_ref[0, 0]
    highest = None
    total = None
    for first in range(0, length, chunk):
        scores = dot(k_rows[first : first + chunk, :], query)
        top = jnp.max(scores, 0, keepdims=True)
        new_high = top if highest is None else jnp.maximum(highest, top)
        weights = jnp.exp2(scores - new_high).astype(bf16)
        term = dot(v_wide[:, first : first + chunk], weights)
        total = term if total is None else total * jnp.exp2(highest - new_high) + term
        highest = new_high
    denominator = total[HEAD : HEAD + 1, :]
    result = (total[:HEAD, :] / denominator).astype(bf16)
    o_ref[0] = result
    done[head, :, pl.ds(pl.multiple_of(step * block, 128), block)] = result
    log_ref[0] = highest + jnp.log2(denominator)

    def own_copy(number):
        return pltpu.make_async_copy(
            done.at[number, :, pl.ds(pl.multiple_of(core * half, 128), half)],
            all_ref.at[core * heads + number], local_o.at[number],
        )

    def sibling_copy(number):
        return remote(
            done.at[number, :, pl.ds(pl.multiple_of((1 - core) * half, 128), half)],
            all_ref.at[core * heads + number], send_o.at[number], recv_o.at[number], dp=sibling,
        )

    @pl.when(step == steps - 1)
    def _():
        own_copy(head).start()
        sibling_copy(head).start()

    @pl.when(jnp.logical_and(head == heads - 1, step == steps - 1))
    def _():
        def settle(number, carry):
            own_copy(number).wait()
            sibling_copy(number).wait()
            return carry
        lax.fori_loop(0, heads, settle, 0)
        finish()


def attend_chip(heads_t, cotangent, ctx):
    _, count, _, length = heads_t.shape
    seqs, block_len, _ = cotangent.shape
    block = chunk_of(length, 512)
    dma = pltpu.SemaphoreType.DMA
    return pl.pallas_call(
        partial(attend_kernel, ctx, seqs),
        grid=(count, length // block),
        in_specs=[
            pl.BlockSpec((1, 1, HEAD, block), lambda h, c: (0, h, 0, c)),
            pl.BlockSpec((1, 1, HEAD, length), lambda h, c: (1, h, 0, 0)),
            pl.BlockSpec((1, 1, HEAD, length), lambda h, c: (2, h, 0, 0)),
            any_spec,
        ],
        out_specs=[
            pl.BlockSpec((1, HEAD, block), lambda h, c: (h, 0, c)),
            pl.BlockSpec((1, 1, block), lambda h, c: (h, 0, c)),
            any_spec,
            any_spec,
        ],
        out_shape=[
            jax.ShapeDtypeStruct((count, HEAD, length), bf16),
            jax.ShapeDtypeStruct((count, 1, length), f32),
            jax.ShapeDtypeStruct((2 * count, HEAD, length // 2), bf16),
            jax.ShapeDtypeStruct((ctx // 2, block_len, D), bf16),
        ],
        scratch_shapes=[
            pltpu.VMEM((length, HEAD), bf16),
            pltpu.VMEM((HEAD + 16, length), bf16),
            pltpu.VMEM((count, HEAD, length), bf16),
            dma((seqs,)), dma((ctx // 2,)), dma,
            dma((count,)), dma((count,)), dma((count,)),
        ],
        compiler_params=params(2),
        name="attend",
        cost_estimate=pl.CostEstimate(
            flops=16 * count * length * length * HEAD,
            bytes_accessed=10 * count * length * HEAD,
            transcendentals=count * length * length,
        ),
    )(heads_t, heads_t, heads_t, cotangent)


def ffn_kernel(
    groups, x_ref, att_ref, cot_ref, out_w, up_w, down_w, gain_ref,
    output_ref, rgrad_ref, agrad_ref, packed_ref,
    normal_t, hidden_t, widened, low, cot_all, att_all, agrad,
    send_sem, recv_sem, local_sem,
):
    step, steps = pl.program_id(0), pl.num_programs(0)
    dp, core, x, z, y = here()
    sibling = dp + 1 - 2 * core
    block = x_ref.shape[0]
    half = block * steps
    ff = down_w.shape[0]
    model = x_ref.shape[1]

    @pl.when(step == 0)
    def _():
        greet([{"dp": sibling}])

    place = pl.ds(pl.multiple_of(step * block, 128), block)
    attended = att_ref[...]
    upstream = cot_ref[...]
    gain = gain_ref[1:2, :]
    residual = x_ref[...].astype(f32) + dot(attended.T, out_w[...])
    normed, inverse, scaled = layer_norm(residual, gain)
    normal = scaled.astype(bf16)
    wide = dot(normal, up_w[...])
    inputs, gating = wide[:, :ff], wide[:, ff:]
    phi_sum = 0.5 + 0.5 * lax.erf(inputs * math.sqrt(0.5))
    density = jnp.exp2(inputs * inputs * (-0.5 * math.log2(math.e))) * (1.0 / math.sqrt(2.0 * math.pi))
    gelu = inputs * phi_sum
    hidden = (gelu * gating).astype(bf16)
    output_ref[...] = (residual + dot(hidden, down_w[...])).astype(bf16)
    hidden_grad = dot(upstream, down_w[...], 1, 1)
    input_grad = (hidden_grad * gating * (phi_sum + inputs * density)).astype(bf16)
    gating_grad = (hidden_grad * gelu).astype(bf16)
    widened[place, :ff] = input_grad
    widened[place, ff:] = gating_grad
    normal_grad = dot(input_grad, up_w[:, :ff], 1, 1) + dot(gating_grad, up_w[:, ff:], 1, 1)
    residual_grad = upstream.astype(f32) + norm_back(normal_grad, normed, inverse, gain)
    rgrad_ref[...] = residual_grad
    residual_low = residual_grad.astype(bf16)
    agrad[:, place] = dot(out_w[...], residual_low, 1, 1).astype(bf16)
    normal_t[:, place] = normal.T
    hidden_t[:, place] = hidden.T
    low[place, :] = residual_low
    cot_all[place, :] = upstream
    att_all[:, place] = attended

    def agrad_copies():
        width = agrad.shape[0] // 2
        mine = pl.ds(pl.multiple_of(core * half, 128), half)
        return (
            pltpu.make_async_copy(
                agrad.at[pl.ds(pl.multiple_of(core * width, 16), width), :],
                agrad_ref.at[:, mine], local_sem,
            ),
            remote(
                agrad.at[pl.ds(pl.multiple_of((1 - core) * width, 16), width), :],
                agrad_ref.at[:, mine], send_sem, recv_sem, dp=sibling,
            ),
        )

    @pl.when(step == steps - 1)
    def _():
        for copy in agrad_copies():
            copy.start()
        offset = 0
        for first in range(0, 2 * ff, model):
            grad = dot(normal_t[...], widened[:, first : first + model])
            rows = grad.shape[0] // groups
            packed_ref[:, offset : offset + rows, :] = grad.astype(bf16).reshape(groups, rows, model)
            offset += rows
        for left, right in ((hidden_t, cot_all), (att_all, low)):
            grad = dot(left[...], right[...])
            rows = grad.shape[0] // groups
            packed_ref[:, offset : offset + rows, :] = grad.astype(bf16).reshape(groups, rows, model)
            offset += rows
        for copy in agrad_copies():
            copy.wait()


def feed_forward(x, attended, cotangent, out_w, up_w, down_w, gains, groups):
    half = x.shape[0]
    ff = down_w.shape[0]
    block = chunk_of(half, 256)
    rows = (2 * ff // D * D + ff + D) // groups
    dma = pltpu.SemaphoreType.DMA

    def whole(array):
        return pl.BlockSpec(array.shape, lambda i: (0,) * array.ndim, pipeline_mode=pl.Buffered(1))

    by_rows = pl.BlockSpec((block, D), lambda i: (i, 0))
    return pl.pallas_call(
        partial(ffn_kernel, groups),
        grid=(half // block,),
        in_specs=[
            by_rows,
            pl.BlockSpec((D, block), lambda i: (0, i)),
            by_rows,
            whole(out_w), whole(up_w), whole(down_w), whole(gains),
        ],
        out_specs=[
            by_rows,
            by_rows,
            any_spec,
            pl.BlockSpec((groups, rows, D), lambda i: (0, 0, 0), pipeline_mode=pl.Buffered(1)),
        ],
        out_shape=[
            jax.ShapeDtypeStruct((half, D), bf16),
            jax.ShapeDtypeStruct((half, D), f32),
            jax.ShapeDtypeStruct((D // 2, 2 * half), bf16),
            jax.ShapeDtypeStruct((groups, rows, D), bf16),
        ],
        scratch_shapes=[
            pltpu.VMEM((D, half), bf16),
            pltpu.VMEM((ff, half), bf16),
            pltpu.VMEM((half, 2 * ff), bf16),
            pltpu.VMEM((half, D), bf16),
            pltpu.VMEM((half, D), bf16),
            pltpu.VMEM((D, half), bf16),
            pltpu.VMEM((D, half), bf16),
            dma, dma, dma,
        ],
        compiler_params=params(3),
        name="feed_forward",
        cost_estimate=pl.CostEstimate(
            flops=6 * half * D * (3 * ff + D), bytes_accessed=32 << 20,
            transcendentals=2 * half * ff,
        ),
    )(x, attended, cotangent, out_w, up_w, down_w, gains)


def tail_kernel(
    ctx, nfsdp, groups, seqs,
    dproj, wt_ref, normal_t, x_ref, rgrad_ref, gain_ref,
    token_ref, qkv_ref,
    dn_send, dn_recv, tg_send, gq_send, gq_recv, zq_send, zq_recv, fq,
    send_n, recv_n, send_t, recv_t, local_t,
    send_q, recv_q, local_q, send_z, recv_z, local_z, send_f, recv_f, local_f, send_s, recv_s, local_s,
):
    dp, core, x, z, y = here()
    sibling = dp + 1 - 2 * core
    half = x_ref.shape[0]
    nx = groups // (2 * nfsdp)
    chips = groups // 2
    here_chip = x * nfsdp + y
    shard_rows = normal_t.shape[0] // groups
    width3 = dproj.shape[0]
    blocks = ctx // 2
    block_len = half // blocks
    chip_others = []
    for j in range(1, chips):
        other = lax.rem(here_chip + j, chips)
        chip_others.append((other // nfsdp, lax.rem(other, nfsdp)))
    greet(
        column_partners(ctx)
        + [{"dp": 2 * cx + core, "fsdp": cy} for cx, cy in chip_others]
    )

    def dn_rows(first, size):
        return dot(dproj[:, pl.ds(pl.multiple_of(first, 128), size)], wt_ref[...], 0, 0)

    size = block_len // 2 if block_len % 256 == 0 else block_len

    def sibling_rows(number, carry):
        first = number * size
        dn_send[pl.ds(pl.multiple_of(first, 16), size), :] = dn_rows(
            (1 - core) * half + first, size
        ).astype(bf16)
        return carry

    lax.fori_loop(0, half // size, sibling_rows, 0)
    dn_copy = remote(dn_send, dn_recv, send_n, recv_n, dp=sibling)
    dn_copy.start()

    part = width3 // 3
    for number in range(3):
        columns = slice(number * part, (number + 1) * part)
        grad = dot(normal_t[...], dproj[columns, :], 1, 1)
        gq_send[:, :, columns] = grad.astype(bf16).reshape(groups, shard_rows, part)

    def row_of(cx, cy, c):
        return (2 * cx + c) * nfsdp + cy

    def gq_copy(j, c):
        cx, cy = chip_others[j - 1]
        return remote(
            gq_send.at[row_of(cx, cy, c)], gq_recv.at[j, c], send_q.at[j - 1, c],
            recv_q.at[j - 1, c], dp=2 * cx + core, fsdp=cy,
        )

    for j in range(1, chips):
        for c in range(2):
            gq_copy(j, c).start()
    own_q = [
        pltpu.make_async_copy(gq_send.at[row_of(x, y, c)], gq_recv.at[0, c], local_q.at[c])
        for c in range(2)
    ]
    for copy in own_q:
        copy.start()

    dn_copy.wait()
    gain = gain_ref[0:1, :]
    start_one, finish = to_blocks(ctx, seqs, tg_send, token_ref, send_t, recv_t, local_t)
    for number in range(blocks):
        for part_first in range(0, block_len, size):
            first = number * block_len + part_first
            place = slice(first, first + size)
            grad = dn_rows(core * half + first, size) + dn_recv[place, :].astype(f32)
            normed, inverse, _ = layer_norm(x_ref[place, :].astype(f32), gain)
            token = rgrad_ref[place, :] + norm_back(grad, normed, inverse, gain)
            tg_send[number, part_first : part_first + size, :] = token.astype(bf16)
        start_one(number)

    for copy in own_q:
        copy.wait()
    for j in range(1, chips):
        for c in range(2):
            gq_copy(j, c).wait()
    rows = 2 * shard_rows // ctx
    summed = gq_recv[0].astype(f32)
    for j in range(1, chips):
        summed = summed + gq_recv[j].astype(f32)
    zq_send[...] = summed.astype(bf16).reshape(zq_send.shape)

    def z_copy(k):
        to = lax.rem(z + k, ctx)
        return remote(
            zq_send.at[to], zq_recv.at[k], send_z.at[k - 1], recv_z.at[k - 1], ctx=to
        )

    for k in range(1, ctx):
        z_copy(k).start()
    own = pltpu.make_async_copy(zq_send.at[z], zq_recv.at[0], local_z)
    own.start()
    own.wait()
    for k in range(1, ctx):
        z_copy(k).wait()
    summed = zq_recv[0].astype(f32)
    for k in range(1, ctx):
        summed = summed + zq_recv[k].astype(f32)
    fq[z] = summed.astype(bf16)

    def f_copy(k):
        return remote(
            fq.at[z], fq.at[z], send_f.at[k - 1], recv_f.at[k - 1], ctx=lax.rem(z + k, ctx)
        )

    for k in range(1, ctx):
        f_copy(k).start()
    for k in range(1, ctx):
        f_copy(k).wait()
    per = ctx // 2
    own = pltpu.make_async_copy(
        fq.at[pl.ds(core * per, per)], qkv_ref.at[core], local_s
    )
    other = remote(
        fq.at[pl.ds((1 - core) * per, per)], qkv_ref.at[core], send_s, recv_s, dp=sibling
    )
    own.start()
    other.start()
    own.wait()
    other.wait()
    finish()


def tail(dproj, wt, normal_t, x, rgrad, gains, ctx, nfsdp, groups, seqs):
    half = x.shape[0]
    block_len = 2 * half // ctx
    width3 = dproj.shape[0]
    shard_rows = D // groups
    chips = groups // 2
    rows = 2 * shard_rows // ctx
    dma = pltpu.SemaphoreType.DMA
    return pl.pallas_call(
        partial(tail_kernel, ctx, nfsdp, groups, seqs),
        in_specs=[vmem_spec] * 6,
        out_specs=[any_spec, any_spec],
        out_shape=[
            jax.ShapeDtypeStruct((seqs, block_len, D), bf16),
            jax.ShapeDtypeStruct((2, ctx // 2, rows, width3), bf16),
        ],
        scratch_shapes=[
            pltpu.VMEM((half, D), bf16),
            pltpu.VMEM((half, D), bf16),
            pltpu.VMEM((ctx // 2, block_len, D), bf16),
            pltpu.VMEM((groups, shard_rows, width3), bf16),
            pltpu.VMEM((chips, 2, shard_rows, width3), bf16),
            pltpu.VMEM((ctx, rows, width3), bf16),
            pltpu.VMEM((ctx, rows, width3), bf16),
            pltpu.VMEM((ctx, rows, width3), bf16),
            dma, dma, dma((ctx // 2,)), dma((seqs,)), dma,
            dma((chips - 1, 2)), dma((chips - 1, 2)), dma((2,)),
            dma((ctx - 1,)), dma((ctx - 1,)), dma,
            dma((ctx - 1,)), dma((ctx - 1,)), dma,
            dma, dma, dma,
        ],
        compiler_params=params(5),
        name="tail",
    )(dproj, wt, normal_t, x, rgrad, gains)


def return_kernel(ctx, seqs, src, dst, send_sem, recv_sem, local_sem):
    greet(column_partners(ctx))
    start_one, finish = to_blocks(ctx, seqs, src, dst, send_sem, recv_sem, local_sem)
    for i in range(ctx // 2):
        start_one(i)
    finish()


def return_blocks(values, ctx, seqs):
    _, block_len, width = values.shape
    dma = pltpu.SemaphoreType.DMA
    return pl.pallas_call(
        partial(return_kernel, ctx, seqs),
        in_specs=[any_spec],
        out_specs=any_spec,
        out_shape=jax.ShapeDtypeStruct((seqs, block_len, width), values.dtype),
        scratch_shapes=[dma((ctx // 2,)), dma((seqs,)), dma],
        compiler_params=params(6),
        name="return_blocks",
    )(values)


def chip_backward_kernel(
    q_ref, k_ref, v_ref, o_ref, up_ref, log_ref, cos_all, sin_all, cos_ref, sin_ref,
    dq_ref, dk_ref, dv_ref, q_rows, up_rows, up_cols, delta, dq_sum,
):
    step = pl.program_id(1)
    blocks, block_len = up_ref.shape[0], up_ref.shape[-1]
    length = q_ref.shape[-1]
    chunk = chunk_of(length, 512)

    @pl.when(step == 0)
    def _():
        q_rows[...] = q_ref[0, 0].T
        for number in range(blocks):
            place = slice(number * block_len, (number + 1) * block_len)
            upstream = up_ref[number, 0]
            up_cols[:, place] = upstream
            up_rows[place, :] = upstream.T
            delta[:, place] = jnp.sum(
                upstream.astype(f32) * o_ref[number, 0].astype(f32), 0, keepdims=True
            )
        dq_sum[...] = jnp.zeros_like(dq_sum)

    key_t = k_ref[0, 0]
    key = key_t.T
    value = v_ref[0, 0].T
    dk = None
    dv = None
    for start in range(0, length, chunk):
        place = slice(start, start + chunk)
        scores = dot(key, q_ref[0, 0, :, place])
        weights = jnp.exp2(scores - log_ref[0, :, place])
        weight_grad = dot(value, up_cols[:, place])
        score_grad = (weights * (weight_grad - delta[:, place])).astype(bf16)
        dv_term = dot(weights.astype(bf16), up_rows[place, :])
        dk_term = dot(score_grad, q_rows[place, :])
        dv = dv_term if dv is None else dv + dv_term
        dk = dk_term if dk is None else dk + dk_term
        dq_sum[:, place] += dot(key_t, score_grad)
    upper, lower = rope_back((dk * math.log(2.0)).T, cos_ref[...], sin_ref[...])
    dk_ref[0, :HALF, :] = upper.astype(bf16)
    dk_ref[0, HALF:, :] = lower.astype(bf16)
    dv_ref[0] = dv.T.astype(bf16)

    @pl.when(step == pl.num_programs(1) - 1)
    def _():
        upper, lower = rope_back(dq_sum[...] * score_scale, cos_all[...], sin_all[...])
        dq_ref[0, :HALF, :] = upper.astype(bf16)
        dq_ref[0, HALF:, :] = lower.astype(bf16)


def attend_back_chip(heads_t, attended, upstream, log_total, cosine, sine):
    _, count, _, length = heads_t.shape
    blocks, _, _, block_len = attended.shape
    rows = chunk_of(length, 256)
    split = pl.BlockSpec((blocks, 1, HEAD, block_len), lambda h, k: (0, h, 0, 0))
    shape = jax.ShapeDtypeStruct((count, HEAD, length), bf16)
    return pl.pallas_call(
        chip_backward_kernel,
        grid=(count, length // rows),
        in_specs=[
            pl.BlockSpec((1, 1, HEAD, length), lambda h, k: (0, h, 0, 0)),
            pl.BlockSpec((1, 1, HEAD, rows), lambda h, k: (1, h, 0, k)),
            pl.BlockSpec((1, 1, HEAD, rows), lambda h, k: (2, h, 0, k)),
            split,
            split,
            pl.BlockSpec((1, 1, length), lambda h, k: (h, 0, 0)),
            pl.BlockSpec((HALF, length), lambda h, k: (0, 0)),
            pl.BlockSpec((HALF, length), lambda h, k: (0, 0)),
            pl.BlockSpec((HALF, rows), lambda h, k: (0, k)),
            pl.BlockSpec((HALF, rows), lambda h, k: (0, k)),
        ],
        out_specs=[
            pl.BlockSpec((1, HEAD, length), lambda h, k: (h, 0, 0)),
            pl.BlockSpec((1, HEAD, rows), lambda h, k: (h, 0, k)),
            pl.BlockSpec((1, HEAD, rows), lambda h, k: (h, 0, k)),
        ],
        out_shape=[shape, shape, shape],
        scratch_shapes=[
            pltpu.VMEM((length, HEAD), bf16),
            pltpu.VMEM((length, HEAD), bf16),
            pltpu.VMEM((HEAD, length), bf16),
            pltpu.VMEM((1, length), f32),
            pltpu.VMEM((HEAD, length), f32),
        ],
        compiler_params=pltpu.CompilerParams(vmem_limit_bytes=40 << 20),
        cost_estimate=pl.CostEstimate(
            flops=40 * count * length * length * HEAD,
            bytes_accessed=16 * count * length * HEAD,
            transcendentals=count * length * length,
        ),
    )(heads_t, heads_t, heads_t, attended, upstream, log_total, cosine, sine, cosine, sine)


def chip_body(
    tokens,
    cotangent,
    qkv_weight,
    out_weight,
    up_weight,
    down_weight,
    attention_gain,
    feedforward_gain,
):
    ctx, nfsdp = lax.axis_size("ctx"), lax.axis_size("fsdp")
    groups = lax.axis_size("dp") * nfsdp
    seqs, block_len, _ = tokens.shape
    length = block_len * ctx
    width = D // 2
    shard_rows = qkv_weight.shape[0]
    me = lax.axis_index("dp") * nfsdp + lax.axis_index("fsdp")
    gain_rows = lax.dynamic_update_slice(
        jnp.zeros((16, D), bf16), jnp.stack([attention_gain, feedforward_gain]),
        (0, me * shard_rows),
    )
    cosine, sine = rope_rows(length)
    out_whole = gather_rows(out_weight)
    up_whole = gather_rows(up_weight)
    down_whole = gather_rows(down_weight)
    heads_t, normal_t, x_half, wt, gains = prologue(
        tokens, qkv_weight, gain_rows, cosine, sine, ctx, nfsdp, groups
    )
    attended, log_total, att_all, cot_half = attend_chip(heads_t, cotangent, ctx)
    output, rgrad, agrad, packed = feed_forward(
        x_half, att_all.reshape(D, length // 2), cot_half.reshape(length // 2, D),
        out_whole, up_whole, down_whole, gains, groups,
    )
    output = return_blocks(output.reshape(ctx // 2, block_len, D), ctx, seqs)

    shard = lax.psum_scatter(packed, WEIGHT_AXES, scatter_dimension=0, tiled=True)[0]
    shard = lax.psum(shard, "ctx").astype(f32)
    up_parts = up_weight.shape[1] // D
    cuts = [shard[i * shard_rows : (i + 1) * shard_rows] for i in range(up_parts)]
    up_shard = jnp.concatenate(cuts, -1)
    offset = up_parts * shard_rows
    down_shard = shard[offset : offset + down_weight.shape[0]]
    out_shard = shard[offset + down_weight.shape[0] :]

    grads = attend_back_chip(
        heads_t, attended[None], agrad.reshape(1, width // HEAD, HEAD, length), log_total,
        cosine, sine,
    )
    dproj = jnp.concatenate(grads, 0).reshape(3 * width, length)
    token_low, qkv_low = tail(
        dproj, wt, normal_t, x_half, rgrad, gains, ctx, nfsdp, groups, seqs
    )
    qkv_shard = qkv_low.reshape(2, shard_rows, 3, width).astype(f32)
    qkv_shard = jnp.transpose(qkv_shard, (1, 2, 0, 3)).reshape(shard_rows, 3 * D)
    attn_gain_grad = jnp.sum(qkv_weight.astype(f32) * qkv_shard, -1) / attention_gain.astype(f32)
    ffn_gain_grad = jnp.sum(up_weight.astype(f32) * up_shard, -1) / feedforward_gain.astype(f32)
    return (
        output,
        token_low.astype(f32),
        qkv_shard,
        out_shard,
        up_shard,
        down_shard,
        attn_gain_grad,
        ffn_gain_grad,
    )


def body(tokens, cotangent, qkv_weight, *others):
    ctx, dp = lax.axis_size("ctx"), lax.axis_size("dp")
    one_each = ctx == 2 * tokens.shape[0] and dp % 2 == 0 and ctx & (ctx - 1) == 0
    aligned = tokens.shape[1] % 128 == 0 and 2 * qkv_weight.shape[0] % (16 * ctx) == 0
    chosen = chip_body if one_each and aligned else general_body
    return chosen(tokens, cotangent, qkv_weight, *others)


def solution(mesh):
    rows = P(("dp", "fsdp"), "ctx", None)
    weight = P(("dp", "fsdp"), None)
    gain = P(("dp", "fsdp"))
    return jax.shard_map(
        body,
        mesh=mesh,
        in_specs=(rows, rows, weight, weight, weight, weight, gain, gain),
        out_specs=(rows, rows, weight, weight, weight, weight, gain, gain),
        check_vma=False,
    )
```

```python
from functools import partial
import math

import jax
import jax.numpy as jnp
from jax import lax
from jax.experimental import pallas as pl
from jax.experimental.pallas import tpu as pltpu
from jax.sharding import PartitionSpec as P

D = 768
HEADS = 12
HEAD = 64
FF = 1152
HALF = HEAD // 2

norm_eps = 1e-05
rope_base = 160000.0
score_scale = HEAD ** (-0.5)
score_base2 = score_scale * math.log2(math.e)
WEIGHT_AXES = ("dp", "fsdp")
f32 = jnp.float32
bf16 = jnp.bfloat16


def dot(left, right, left_dim=1, right_dim=0):
    return lax.dot_general(
        left, right, (((left_dim,), (right_dim,)), ((), ())), preferred_element_type=f32
    )


def layer_norm(values, norm_gain):
    centre = jnp.mean(values, -1, keepdims=True)
    centred = values - centre
    inverse = lax.rsqrt(jnp.mean(centred * centred, -1, keepdims=True) + norm_eps)
    normed = centred * inverse
    return (normed, inverse, normed * norm_gain)


def norm_back(upstream, normed, inverse, norm_gain):
    scaled = upstream * norm_gain
    return (
        scaled
        - jnp.mean(scaled, -1, keepdims=True)
        - normed * jnp.mean(scaled * normed, -1, keepdims=True)
    ) * inverse


def gated_gelu(inputs, gating):
    return jax.nn.gelu(inputs, approximate=False) * gating


def rope_rows(length):
    frequency = rope_base ** (-2.0 * jnp.arange(HALF, dtype=f32) / HEAD)
    angles = frequency[:, None] * jnp.arange(length, dtype=jnp.int32).astype(f32)[None, :]
    return (jnp.cos(angles), jnp.sin(angles))


def chunk_of(length, most):
    return most if length % most == 0 else length


def forward_kernel(q_ref, k_ref, v_ref, o_ref, log_ref, k_rows, v_wide):
    length = k_ref.shape[-1]
    chunk = chunk_of(length, 512)

    @pl.when(pl.program_id(1) == 0)
    def _():
        k_rows[...] = k_ref[0, 0].T
        v_wide[:HEAD, :] = v_ref[0, 0]
        v_wide[HEAD:, :] = jnp.ones((v_wide.shape[0] - HEAD, length), bf16)

    query = q_ref[0, 0]
    highest = None
    total = None
    for start in range(0, length, chunk):
        scores = dot(k_rows[start : start + chunk, :], query) * score_base2
        top = jnp.max(scores, 0, keepdims=True)
        new_high = top if highest is None else jnp.maximum(highest, top)
        weights = jnp.exp2(scores - new_high).astype(bf16)
        term = dot(v_wide[:, start : start + chunk], weights)
        total = term if total is None else total * jnp.exp2(highest - new_high) + term
        highest = new_high
    denominator = total[HEAD : HEAD + 1, :]
    o_ref[0, 0] = (total[:HEAD, :] / denominator).astype(bf16)
    log_ref[0] = highest + jnp.log2(denominator)


def attend(heads_t, block_len):
    _, count, _, length = heads_t.shape
    blocks = length // block_len
    return pl.pallas_call(
        forward_kernel,
        grid=(count, blocks),
        in_specs=[
            pl.BlockSpec((1, 1, HEAD, block_len), lambda h, c: (0, h, 0, c)),
            pl.BlockSpec((1, 1, HEAD, length), lambda h, c: (1, h, 0, 0)),
            pl.BlockSpec((1, 1, HEAD, length), lambda h, c: (2, h, 0, 0)),
        ],
        out_specs=[
            pl.BlockSpec((1, 1, HEAD, block_len), lambda h, c: (c, h, 0, 0)),
            pl.BlockSpec((1, 1, block_len), lambda h, c: (h, 0, c)),
        ],
        out_shape=[
            jax.ShapeDtypeStruct((blocks, count, HEAD, block_len), bf16),
            jax.ShapeDtypeStruct((count, 1, length), f32),
        ],
        scratch_shapes=[
            pltpu.VMEM((length, HEAD), bf16),
            pltpu.VMEM((HEAD + 16, length), bf16),
        ],
        compiler_params=pltpu.CompilerParams(vmem_limit_bytes=40 << 20),
        cost_estimate=pl.CostEstimate(
            flops=16 * count * length * length * HEAD,
            bytes_accessed=10 * count * length * HEAD,
            transcendentals=count * length * length,
        ),
    )(heads_t, heads_t, heads_t)


def rope_back(grad_t, cosine, sine):
    first, second = grad_t[:HALF, :], grad_t[HALF:, :]
    return (first * cosine + second * sine, second * cosine - first * sine)


def backward_kernel(
    q_ref, k_ref, v_ref, o_ref, up_ref, log_ref, cos_all, sin_all, cos_ref, sin_ref,
    dq_ref, dk_ref, dv_ref, q_rows, up_rows, up_cols, delta, dq_sum,
):
    step = pl.program_id(1)
    blocks, block_len = up_ref.shape[0], up_ref.shape[-1]
    length = q_ref.shape[-1]
    chunk = chunk_of(length, 512)

    @pl.when(step == 0)
    def _():
        q_rows[...] = q_ref[0, 0].T
        for number in range(blocks):
            place = slice(number * block_len, (number + 1) * block_len)
            upstream = up_ref[number, 0]
            up_cols[:, place] = upstream
            up_rows[place, :] = upstream.T
            delta[:, place] = jnp.sum(
                upstream.astype(f32) * o_ref[number, 0].astype(f32), 0, keepdims=True
            )
        dq_sum[...] = jnp.zeros_like(dq_sum)

    key_t = k_ref[0, 0]
    key = key_t.T
    value = v_ref[0, 0].T
    dk = None
    dv = None
    for start in range(0, length, chunk):
        place = slice(start, start + chunk)
        scores = dot(key, q_ref[0, 0, :, place]) * score_base2
        weights = jnp.exp2(scores - log_ref[0, :, place])
        weight_grad = dot(value, up_cols[:, place])
        score_grad = (weights * (weight_grad - delta[:, place])).astype(bf16)
        dv_term = dot(weights.astype(bf16), up_rows[place, :])
        dk_term = dot(score_grad, q_rows[place, :])
        dv = dv_term if dv is None else dv + dv_term
        dk = dk_term if dk is None else dk + dk_term
        dq_sum[:, place] += dot(key_t, score_grad)
    upper, lower = rope_back((dk * score_scale).T, cos_ref[...], sin_ref[...])
    dk_ref[0, :HALF, :] = upper.astype(bf16)
    dk_ref[0, HALF:, :] = lower.astype(bf16)
    dv_ref[0] = dv.T.astype(bf16)

    @pl.when(step == pl.num_programs(1) - 1)
    def _():
        upper, lower = rope_back(dq_sum[...] * score_scale, cos_all[...], sin_all[...])
        dq_ref[0, :HALF, :] = upper.astype(bf16)
        dq_ref[0, HALF:, :] = lower.astype(bf16)


def attend_back(heads_t, attended, upstream, log_total, cosine, sine):
    _, count, _, length = heads_t.shape
    blocks, _, _, block_len = attended.shape
    rows = chunk_of(length, 256)
    split = pl.BlockSpec((blocks, 1, HEAD, block_len), lambda h, k: (0, h, 0, 0))
    shape = jax.ShapeDtypeStruct((count, HEAD, length), bf16)
    return pl.pallas_call(
        backward_kernel,
        grid=(count, length // rows),
        in_specs=[
            pl.BlockSpec((1, 1, HEAD, length), lambda h, k: (0, h, 0, 0)),
            pl.BlockSpec((1, 1, HEAD, rows), lambda h, k: (1, h, 0, k)),
            pl.BlockSpec((1, 1, HEAD, rows), lambda h, k: (2, h, 0, k)),
            split,
            split,
            pl.BlockSpec((1, 1, length), lambda h, k: (h, 0, 0)),
            pl.BlockSpec((HALF, length), lambda h, k: (0, 0)),
            pl.BlockSpec((HALF, length), lambda h, k: (0, 0)),
            pl.BlockSpec((HALF, rows), lambda h, k: (0, k)),
            pl.BlockSpec((HALF, rows), lambda h, k: (0, k)),
        ],
        out_specs=[
            pl.BlockSpec((1, HEAD, length), lambda h, k: (h, 0, 0)),
            pl.BlockSpec((1, HEAD, rows), lambda h, k: (h, 0, k)),
            pl.BlockSpec((1, HEAD, rows), lambda h, k: (h, 0, k)),
        ],
        out_shape=[shape, shape, shape],
        scratch_shapes=[
            pltpu.VMEM((length, HEAD), bf16),
            pltpu.VMEM((length, HEAD), bf16),
            pltpu.VMEM((HEAD, length), bf16),
            pltpu.VMEM((1, length), f32),
            pltpu.VMEM((HEAD, length), f32),
        ],
        compiler_params=pltpu.CompilerParams(vmem_limit_bytes=40 << 20),
        cost_estimate=pl.CostEstimate(
            flops=40 * count * length * length * HEAD,
            bytes_accessed=16 * count * length * HEAD,
            transcendentals=count * length * length,
        ),
    )(heads_t, heads_t, heads_t, attended, upstream, log_total, cosine, sine, cosine, sine)


def gather_rows(shard):
    return lax.all_gather(shard, WEIGHT_AXES, axis=0, tiled=True)


def exchange(blocks):
    return lax.all_to_all(blocks, "ctx", 0, 0, tiled=True)


def general_body(
    tokens,
    cotangent,
    qkv_weight,
    out_weight,
    up_weight,
    down_weight,
    attention_gain,
    feedforward_gain,
):
    ctx = lax.axis_size("ctx")
    groups = lax.axis_size("dp") * lax.axis_size("fsdp")
    seq_count, block_len = (tokens.shape[0], tokens.shape[1])
    length = block_len * ctx
    sets = math.gcd(seq_count, ctx)
    each = seq_count // sets
    teams = ctx // sets
    own = -(-HEADS // teams)
    width = own * HEAD
    spare = teams * own - HEADS
    halves = 2 if own % 2 == 0 else 1
    part = own // halves
    shard_rows = qkv_weight.shape[0]
    row_count = seq_count * block_len

    moved = [
        exchange(jnp.repeat(tokens[turn::each], teams, axis=0)).reshape(length, D)
        for turn in range(each)
    ]

    by_head = qkv_weight.reshape(shard_rows, 3, D)
    if spare:
        by_head = jnp.pad(by_head, ((0, 0), (0, 0), (0, spare * HEAD)))
    team = lax.rem(lax.axis_index("ctx"), teams)
    own_columns = lax.dynamic_slice_in_dim(by_head, team * width, width, 2)
    gain_columns = jnp.pad(
        jnp.stack([attention_gain, feedforward_gain], -1), ((0, 0), (0, 126))
    )
    first_gather = gather_rows(
        jnp.concatenate([own_columns.reshape(shard_rows, 3 * width), gain_columns], -1)
    )
    qkv_own = first_gather[:, : 3 * width]
    attn_gain = first_gather[:, 3 * width].astype(f32)
    ffn_gain = first_gather[:, 3 * width + 1].astype(f32)
    out_whole = gather_rows(out_weight)
    up_whole = gather_rows(up_weight)
    down_whole = gather_rows(down_weight)
    cosine, sine = rope_rows(length)

    saved = []
    for turn in range(each):
        normal = layer_norm(moved[turn].astype(f32), attn_gain)[2].astype(bf16)
        by_part = qkv_own.reshape(D, 3, halves, part * HEAD)
        pieces = []
        for half in range(halves):
            weight = by_part[:, :, half].reshape(D, 3 * part * HEAD)
            projected = dot(weight, normal, 0, 1).reshape(3, part, 2, HALF, length)
            first, second = (projected[:2, :, 0], projected[:2, :, 1])
            turned = jnp.stack(
                [first * cosine - second * sine, second * cosine + first * sine], 2
            )
            heads_t = (
                jnp.concatenate([turned, projected[2:]], 0)
                .astype(bf16)
                .reshape(3, part, HEAD, length)
            )
            attended, log_total = attend(heads_t, block_len)
            pieces.append((heads_t, attended, log_total, exchange(attended)))
        saved.append((normal, pieces))

    columns = []
    for number in range(seq_count):
        chosen, turn = divmod(number, each)
        got = [
            piece[3].reshape(sets, teams, part, HEAD, block_len)[chosen]
            for piece in saved[turn][1]
        ]
        columns.append(jnp.concatenate(got, 1).reshape(teams * width, block_len)[:D])
    attended_t = jnp.concatenate(columns, 1)

    inputs = tokens.reshape(row_count, D).astype(f32)
    residual = inputs + dot(attended_t, out_whole, 0, 0)
    normed_b, inverse_b, scaled_b = layer_norm(residual, ffn_gain)
    normal_b = scaled_b.astype(bf16)
    widened = dot(normal_b, up_whole)
    hidden, hidden_back = jax.vjp(gated_gelu, widened[:, :FF], widened[:, FF:])
    hidden_low = hidden.astype(bf16)
    output = (residual + dot(hidden_low, down_whole)).astype(bf16)
    upstream = cotangent.reshape(row_count, D)
    hidden_grad = dot(upstream, down_whole, 1, 1)
    input_grad, gating_grad = hidden_back(hidden_grad)
    widened_grad = jnp.concatenate([input_grad, gating_grad], -1).astype(bf16)
    normal_b_grad = dot(widened_grad, up_whole, 1, 1)
    residual_grad = upstream.astype(f32) + norm_back(normal_b_grad, normed_b, inverse_b, ffn_gain)
    residual_low = residual_grad.astype(bf16)

    out_heads = out_whole
    if spare:
        out_heads = jnp.pad(out_heads, ((0, spare * HEAD), (0, 0)))
    out_heads = out_heads.reshape(teams, halves, part * HEAD, D)
    arrived = []
    for turn in range(each):
        for half in range(halves):
            weight = out_heads[:, half].reshape(teams * part * HEAD, D)
            sent = [
                dot(weight, residual_low[start : start + block_len], 1, 1).astype(bf16)
                for start in range(turn * block_len, row_count, each * block_len)
            ]
            arrived.append(exchange(jnp.stack(sent).reshape(ctx, part, HEAD, block_len)))

    down_grad = dot(hidden_low, upstream, 0, 0)
    up_grad = dot(normal_b, widened_grad, 0, 0)
    out_grad = dot(attended_t, residual_low)

    parts = [up_grad[:, start : start + D] for start in range(0, up_grad.shape[1], D)]
    parts += [down_grad, out_grad]
    packed = jnp.concatenate([item.astype(bf16).reshape(groups, -1, D) for item in parts], 1)
    shard = lax.psum_scatter(packed, WEIGHT_AXES, scatter_dimension=0, tiled=True)[0]
    shard = lax.psum(shard, "ctx").astype(f32)
    cuts = []
    offset = 0
    for item in parts:
        rows = item.shape[0] // groups
        cuts.append(shard[offset : offset + rows])
        offset += rows
    up_shard = jnp.concatenate(cuts[:-2], -1)
    down_shard, out_shard = cuts[-2:]

    back = []
    qkv_grad = 0.0
    for turn in range(each):
        normal, pieces = saved[turn]
        grads = []
        for half in range(halves):
            heads_t, attended, log_total, _ = pieces[half]
            grads.append(
                attend_back(
                    heads_t, attended, arrived[turn * halves + half], log_total, cosine, sine
                )
            )
        projected_grad = jnp.concatenate(
            [grads[half][which] for which in range(3) for half in range(halves)], 0
        ).reshape(3 * width, length)
        partial_grad = dot(projected_grad, qkv_own, 0, 1).astype(bf16)
        terms = exchange(partial_grad.reshape(ctx, block_len, D))
        back.append(terms.reshape(sets, teams, block_len, D).astype(f32).sum(1))
        qkv_grad = qkv_grad + dot(normal, projected_grad, 0, 1)
    normal_a_grad = jnp.stack(back, 1).reshape(row_count, D)
    normed_a, inverse_a, _ = layer_norm(inputs, attn_gain)
    token_grad = residual_grad + norm_back(normal_a_grad, normed_a, inverse_a, attn_gain)
    qkv_cut = lax.psum_scatter(
        qkv_grad.astype(bf16), WEIGHT_AXES, scatter_dimension=0, tiled=True
    )
    qkv_all = lax.all_gather(qkv_cut, "ctx", axis=0).astype(f32)
    qkv_all = qkv_all.reshape(sets, teams, shard_rows, 3, width).sum(0)
    qkv_shard = jnp.transpose(qkv_all, (1, 2, 0, 3)).reshape(shard_rows, 3, teams * width)
    qkv_shard = qkv_shard[:, :, :D].reshape(shard_rows, 3 * D)
    attn_gain_grad = jnp.sum(qkv_weight.astype(f32) * qkv_shard, -1) / attention_gain.astype(f32)
    ffn_gain_grad = jnp.sum(up_weight.astype(f32) * up_shard, -1) / feedforward_gain.astype(f32)
    return (
        output.reshape(seq_count, block_len, D),
        token_grad.reshape(seq_count, block_len, D),
        qkv_shard,
        out_shard,
        up_shard,
        down_shard,
        attn_gain_grad,
        ffn_gain_grad,
    )


MESH_ID = pl.DeviceIdType.MESH
VMEM_LIMIT = 60 << 20
vmem_spec = pl.BlockSpec(memory_space=pltpu.VMEM)
any_spec = pl.BlockSpec(memory_space=pl.ANY)


def here():
    dp = lax.axis_index("dp")
    return dp, lax.rem(dp, 2), dp // 2, lax.axis_index("ctx"), lax.axis_index("fsdp")


def params(number):
    return pltpu.CompilerParams(
        collective_id=number, has_side_effects=True, vmem_limit_bytes=VMEM_LIMIT
    )


def greet(partners):
    barrier = pltpu.get_barrier_semaphore()
    for partner in partners:
        pl.semaphore_signal(barrier, inc=1, device_id=partner, device_id_type=MESH_ID)
    pl.semaphore_wait(barrier, len(partners))


def remote(src, dst, send_sem, recv_sem, **device):
    return pltpu.make_async_remote_copy(
        src_ref=src, dst_ref=dst, send_sem=send_sem, recv_sem=recv_sem,
        device_id=device, device_id_type=MESH_ID,
    )


def near_order(place, count):
    def at(turn):
        block = place
        bit = 1
        while bit < count:
            flip = lax.rem(turn // bit, 2)
            block = block + flip * (bit - 2 * bit * lax.rem(place // bit, 2))
            bit *= 2
        return block
    return at


def prologue_kernel(
    ctx, nfsdp, groups, seqs,
    x_ref, w_ref, g_ref, cos_ref, sin_ref,
    heads_ref, normal_ref, half_ref, wt_ref, gain_ref,
    xbuf, wbuf, gbuf,
    send_x, recv_x, fwd_x, local_x, send_w, recv_w, local_w, send_g, recv_g, local_g,
):
    dp, core, x, z, y = here()
    sibling = dp + 1 - 2 * core
    block_len = x_ref.shape[1]
    shard_rows = w_ref.shape[0]
    width = wbuf.shape[1] // 3
    heads = width // HEAD
    me = dp * nfsdp + y
    lead = z // seqs == core
    others = []
    for j in range(1, groups):
        other = lax.rem(me + j, groups)
        others.append((other // nfsdp, lax.rem(other, nfsdp)))
    greet(
        [{"ctx": lax.rem(z + k, ctx)} for k in range(1, ctx)]
        + [{"dp": d, "fsdp": f} for d, f in others]
    )

    def column_copy(s):
        return remote(x_ref.at[s], xbuf.at[z], send_x.at[s], recv_x.at[z], ctx=core * seqs + s)

    def sibling_copy(s):
        return remote(x_ref.at[s], xbuf.at[z], send_x.at[s], recv_x.at[z], dp=sibling)

    for s in range(seqs):
        keep = core * seqs + s == z

        @pl.when(jnp.logical_not(keep))
        def _():
            column_copy(s).start()

        @pl.when(keep)
        def _():
            sibling_copy(s).start()
            own = pltpu.make_async_copy(x_ref.at[s], xbuf.at[z], local_x)
            own.start()
            own.wait()

    def weight_copy(j, part):
        d, f = others[j - 1]
        columns = pl.multiple_of(part * D + lax.rem(d, 2) * width, 128)
        return remote(
            w_ref.at[:, pl.ds(columns, width)],
            wbuf.at[pl.ds(pl.multiple_of(me * shard_rows, 16), shard_rows), pl.ds(part * width, width)],
            send_w.at[j - 1, part], recv_w.at[j - 1, part], dp=d, fsdp=f,
        )

    def gain_copy(j):
        d, f = others[j - 1]
        return remote(g_ref, gbuf.at[me], send_g.at[j - 1], recv_g.at[j - 1], dp=d, fsdp=f)

    for j in range(1, groups):
        gain_copy(j).start()
        for part in range(3):
            weight_copy(j, part).start()
    own = [pltpu.make_async_copy(g_ref, gbuf.at[me], local_g)]
    for part in range(3):
        columns = pl.multiple_of(part * D + core * width, 128)
        own.append(pltpu.make_async_copy(
            w_ref.at[:, pl.ds(columns, width)],
            wbuf.at[pl.ds(pl.multiple_of(me * shard_rows, 16), shard_rows), pl.ds(part * width, width)],
            local_w.at[part],
        ))
    for copy in own:
        copy.start()
    for copy in own:
        copy.wait()
    for j in range(1, groups):
        gain_copy(j).wait_recv()
        for part in range(3):
            weight_copy(j, part).wait_recv()

    gains = gbuf[0].astype(f32)
    for number in range(1, groups):
        gains = gains + gbuf[number].astype(f32)
    gain_ref[...] = gains
    wt_ref[...] = wbuf[...].T
    attn_gain = gains[0:1, :]
    order = near_order(z, ctx)

    def forward_copy(block):
        return remote(xbuf.at[block], xbuf.at[block], fwd_x.at[block], recv_x.at[block], dp=sibling)

    def turn(number, carry):
        block = order(number)

        @pl.when(jnp.logical_or(jnp.logical_not(lead), number > 0))
        def _():
            forward_copy(block).wait_recv()

        @pl.when(jnp.logical_and(lead, number > 0))
        def _():
            forward_copy(block).start()

        place = pl.ds(pl.multiple_of(block * block_len, 128), block_len)
        normal = layer_norm(xbuf[block].astype(f32), attn_gain)[2].astype(bf16)
        normal_ref[:, place] = normal.T
        cosine, sine = cos_ref[:, place], sin_ref[:, place]
        for part in range(3):
            projected = dot(wt_ref[part * width : (part + 1) * width, :], normal, 1, 1)
            for head in range(heads):
                first = projected[head * HEAD : head * HEAD + HALF, :]
                second = projected[head * HEAD + HALF : (head + 1) * HEAD, :]
                if part < 2:
                    first, second = (
                        first * cosine - second * sine, second * cosine + first * sine
                    )
                if part == 0:
                    first, second = first * score_base2, second * score_base2
                heads_ref[part, head, :HALF, place] = first.astype(bf16)
                heads_ref[part, head, HALF:, place] = second.astype(bf16)
        return carry

    lax.fori_loop(0, ctx, turn, 0)
    half_blocks = ctx // 2
    half_ref[...] = xbuf[pl.ds(core * half_blocks, half_blocks)].reshape(half_ref.shape)

    for s in range(seqs):
        sibling_copy(s).wait_send()
    for number in range(1, ctx):
        @pl.when(lead)
        def _():
            forward_copy(order(number)).wait_send()
    for j in range(1, groups):
        gain_copy(j).wait_send()
        for part in range(3):
            weight_copy(j, part).wait_send()


def prologue(tokens, qkv_weight, gains, cosine, sine, ctx, nfsdp, groups):
    seqs, block_len, _ = tokens.shape
    length = block_len * ctx
    width = D // 2
    shard_rows = qkv_weight.shape[0]
    dma = pltpu.SemaphoreType.DMA
    return pl.pallas_call(
        partial(prologue_kernel, ctx, nfsdp, groups, seqs),
        in_specs=[any_spec, any_spec, any_spec, vmem_spec, vmem_spec],
        out_specs=[vmem_spec] * 5,
        out_shape=[
            jax.ShapeDtypeStruct((3, width // HEAD, HEAD, length), bf16),
            jax.ShapeDtypeStruct((D, length), bf16),
            jax.ShapeDtypeStruct((length // 2, D), bf16),
            jax.ShapeDtypeStruct((3 * width, D), bf16),
            jax.ShapeDtypeStruct(gains.shape, f32),
        ],
        scratch_shapes=[
            pltpu.VMEM((ctx, block_len, D), bf16),
            pltpu.VMEM((groups * shard_rows, 3 * width), bf16),
            pltpu.VMEM((groups,) + gains.shape, bf16),
            dma((seqs,)), dma((ctx,)), dma((ctx,)), dma,
            dma((groups - 1, 3)), dma((groups - 1, 3)), dma((3,)),
            dma((groups - 1,)), dma((groups - 1,)), dma,
        ],
        compiler_params=params(1),
        name="prologue",
        cost_estimate=pl.CostEstimate(
            flops=6 * width * D * length, bytes_accessed=16 * length * D, transcendentals=0
        ),
    )(tokens, qkv_weight, gains, cosine, sine)


def column_partners(ctx):
    dp, core, x, z, y = here()
    found = [{"dp": dp + 1 - 2 * core}]
    for k in range(1, ctx):
        for c in range(2):
            found.append({"dp": 2 * x + c, "ctx": lax.rem(z + k, ctx)})
    return found


def to_halves(ctx, seqs, src, dst, send_sem, recv_sem, local_sem):
    dp, core, x, z, y = here()
    half = ctx // 2
    side, slot = z // half, lax.rem(z, half)

    def outgoing(s):
        return remote(
            src.at[s], dst.at[slot], send_sem.at[s], recv_sem.at[slot],
            dp=2 * x + side, ctx=core * seqs + s,
        )

    def stays(s):
        return jnp.logical_and(core * seqs + s == z, side == core)

    def own(s):
        return pltpu.make_async_copy(src.at[s], dst.at[slot], local_sem)

    def start():
        for s in range(seqs):
            @pl.when(stays(s))
            def _():
                own(s).start()

            @pl.when(jnp.logical_not(stays(s)))
            def _():
                outgoing(s).start()

    def finish():
        for s in range(seqs):
            @pl.when(stays(s))
            def _():
                own(s).wait()

            @pl.when(jnp.logical_not(stays(s)))
            def _():
                outgoing(s).wait_send()
        for i in range(half):
            mine = jnp.logical_and(z // seqs == core, core * half + i == z)

            @pl.when(jnp.logical_not(mine))
            def _():
                remote(
                    src.at[0], dst.at[i], send_sem.at[0], recv_sem.at[i], dp=dp
                ).wait_recv()

    return start, finish


def to_blocks(ctx, seqs, parts, src, dst, send_sem, recv_sem, local_sem):
    dp, core, x, z, y = here()
    half = ctx // 2
    side, slot = z // seqs, lax.rem(z, seqs)
    size = src.shape[1] // parts

    def outgoing(i, part):
        rows = slice(part * size, (part + 1) * size)
        return remote(
            src.at[i, rows], dst.at[slot, rows], send_sem.at[i, part], recv_sem.at[slot, part],
            dp=2 * x + side, ctx=core * half + i,
        )

    def stays(i):
        return jnp.logical_and(core * half + i == z, side == core)

    def own(i, part):
        rows = slice(part * size, (part + 1) * size)
        return pltpu.make_async_copy(src.at[i, rows], dst.at[slot, rows], local_sem.at[part])

    def start_one(i, part):
        @pl.when(stays(i))
        def _():
            own(i, part).start()

        @pl.when(jnp.logical_not(stays(i)))
        def _():
            outgoing(i, part).start()

    def finish():
        for part in range(parts):
            rows = slice(part * size, (part + 1) * size)
            for i in range(half):
                @pl.when(stays(i))
                def _():
                    own(i, part).wait()

                @pl.when(jnp.logical_not(stays(i)))
                def _():
                    outgoing(i, part).wait_send()
            for s in range(seqs):
                mine = jnp.logical_and(z // half == core, core * seqs + s == z)

                @pl.when(jnp.logical_not(mine))
                def _():
                    remote(
                        src.at[0, rows], dst.at[s, rows], send_sem.at[0, part],
                        recv_sem.at[s, part], dp=dp,
                    ).wait_recv()

    return start_one, finish


def block_sems(ctx, seqs, parts):
    dma = pltpu.SemaphoreType.DMA
    return [dma((ctx // 2, parts)), dma((seqs, parts)), dma((parts,))]


def attend_kernel(
    ctx, seqs, q_ref, k_ref, v_ref, cot_ref, o_ref, log_ref, all_ref, half_ref,
    k_rows, v_wide, done,
    send_c, recv_c, local_c, send_o, recv_o, local_o,
):
    head, step = pl.program_id(0), pl.program_id(1)
    heads, steps = pl.num_programs(0), pl.num_programs(1)
    dp, core, x, z, y = here()
    sibling = dp + 1 - 2 * core
    length = k_ref.shape[-1]
    chunk = chunk_of(length, 512)
    block = q_ref.shape[-1]
    half = length // 2
    start, finish = to_halves(ctx, seqs, cot_ref, half_ref, send_c, recv_c, local_c)

    @pl.when(jnp.logical_and(head == 0, step == 0))
    def _():
        greet(column_partners(ctx))
        start()

    @pl.when(step == 0)
    def _():
        k_rows[...] = k_ref[0, 0].T
        v_wide[:HEAD, :] = v_ref[0, 0]
        v_wide[HEAD:, :] = jnp.ones((v_wide.shape[0] - HEAD, length), bf16)

    query = q_ref[0, 0]
    highest = None
    total = None
    for first in range(0, length, chunk):
        scores = dot(k_rows[first : first + chunk, :], query)
        top = jnp.max(scores, 0, keepdims=True)
        new_high = top if highest is None else jnp.maximum(highest, top)
        weights = jnp.exp2(scores - new_high).astype(bf16)
        term = dot(v_wide[:, first : first + chunk], weights)
        total = term if total is None else total * jnp.exp2(highest - new_high) + term
        highest = new_high
    denominator = total[HEAD : HEAD + 1, :]
    result = (total[:HEAD, :] / denominator).astype(bf16)
    o_ref[0] = result
    done[head, :, pl.ds(pl.multiple_of(step * block, 128), block)] = result
    log_ref[0] = highest + jnp.log2(denominator)

    def own_copy(number):
        return pltpu.make_async_copy(
            done.at[number, :, pl.ds(pl.multiple_of(core * half, 128), half)],
            all_ref.at[core * heads + number], local_o.at[number],
        )

    def sibling_copy(number):
        return remote(
            done.at[number, :, pl.ds(pl.multiple_of((1 - core) * half, 128), half)],
            all_ref.at[core * heads + number], send_o.at[number], recv_o.at[number], dp=sibling,
        )

    @pl.when(step == steps - 1)
    def _():
        own_copy(head).start()
        sibling_copy(head).start()

    @pl.when(jnp.logical_and(head == heads - 1, step == steps - 1))
    def _():
        def settle(number, carry):
            own_copy(number).wait()
            sibling_copy(number).wait()
            return carry
        lax.fori_loop(0, heads, settle, 0)
        finish()


def attend_chip(heads_t, cotangent, ctx):
    _, count, _, length = heads_t.shape
    seqs, block_len, _ = cotangent.shape
    block = chunk_of(length, 512)
    dma = pltpu.SemaphoreType.DMA
    return pl.pallas_call(
        partial(attend_kernel, ctx, seqs),
        grid=(count, length // block),
        in_specs=[
            pl.BlockSpec((1, 1, HEAD, block), lambda h, c: (0, h, 0, c)),
            pl.BlockSpec((1, 1, HEAD, length), lambda h, c: (1, h, 0, 0)),
            pl.BlockSpec((1, 1, HEAD, length), lambda h, c: (2, h, 0, 0)),
            any_spec,
        ],
        out_specs=[
            pl.BlockSpec((1, HEAD, block), lambda h, c: (h, 0, c)),
            pl.BlockSpec((1, 1, block), lambda h, c: (h, 0, c)),
            any_spec,
            any_spec,
        ],
        out_shape=[
            jax.ShapeDtypeStruct((count, HEAD, length), bf16),
            jax.ShapeDtypeStruct((count, 1, length), f32),
            jax.ShapeDtypeStruct((2 * count, HEAD, length // 2), bf16),
            jax.ShapeDtypeStruct((ctx // 2, block_len, D), bf16),
        ],
        scratch_shapes=[
            pltpu.VMEM((length, HEAD), bf16),
            pltpu.VMEM((HEAD + 16, length), bf16),
            pltpu.VMEM((count, HEAD, length), bf16),
            dma((seqs,)), dma((ctx // 2,)), dma,
            dma((count,)), dma((count,)), dma((count,)),
        ],
        compiler_params=params(2),
        name="attend",
        cost_estimate=pl.CostEstimate(
            flops=16 * count * length * length * HEAD,
            bytes_accessed=10 * count * length * HEAD,
            transcendentals=count * length * length,
        ),
    )(heads_t, heads_t, heads_t, cotangent)


def ffn_kernel(
    nfsdp, groups, x_ref, att_ref, cot_ref, out_w, up_w, down_w, gain_ref,
    output_ref, rgrad_ref, agrad_ref, shard_ref,
    normal_t, hidden_t, widened, low, cot_all, att_all, agrad, packed, twin,
    send_sem, recv_sem, local_sem, send_t, recv_t,
):
    step, steps = pl.program_id(0), pl.num_programs(0)
    dp, core, x, z, y = here()
    sibling = dp + 1 - 2 * core
    block = x_ref.shape[0]
    half = block * steps
    ff = down_w.shape[0]
    model = x_ref.shape[1]

    @pl.when(step == 0)
    def _():
        greet([{"dp": sibling}])

    place = pl.ds(pl.multiple_of(step * block, 128), block)
    attended = att_ref[...]
    upstream = cot_ref[...]
    gain = gain_ref[1:2, :]
    residual = x_ref[...].astype(f32) + dot(attended.T, out_w[...])
    normed, inverse, scaled = layer_norm(residual, gain)
    normal = scaled.astype(bf16)
    wide = dot(normal, up_w[...])
    inputs, gating = wide[:, :ff], wide[:, ff:]
    phi_sum = 0.5 + 0.5 * lax.erf(inputs * math.sqrt(0.5))
    density = jnp.exp2(inputs * inputs * (-0.5 * math.log2(math.e))) * (1.0 / math.sqrt(2.0 * math.pi))
    gelu = inputs * phi_sum
    hidden = (gelu * gating).astype(bf16)
    output_ref[...] = (residual + dot(hidden, down_w[...])).astype(bf16)
    hidden_grad = dot(upstream, down_w[...], 1, 1)
    input_grad = (hidden_grad * gating * (phi_sum + inputs * density)).astype(bf16)
    gating_grad = (hidden_grad * gelu).astype(bf16)
    widened[place, :ff] = input_grad
    widened[place, ff:] = gating_grad
    normal_grad = dot(input_grad, up_w[:, :ff], 1, 1) + dot(gating_grad, up_w[:, ff:], 1, 1)
    residual_grad = upstream.astype(f32) + norm_back(normal_grad, normed, inverse, gain)
    rgrad_ref[...] = residual_grad
    residual_low = residual_grad.astype(bf16)
    agrad[:, place] = dot(out_w[...], residual_low, 1, 1).astype(bf16)
    normal_t[:, place] = normal.T
    hidden_t[:, place] = hidden.T
    low[place, :] = residual_low
    cot_all[place, :] = upstream
    att_all[:, place] = attended

    def agrad_copies():
        width = agrad.shape[0] // 2
        mine = pl.ds(pl.multiple_of(core * half, 128), half)
        return (
            pltpu.make_async_copy(
                agrad.at[pl.ds(pl.multiple_of(core * width, 16), width), :],
                agrad_ref.at[:, mine], local_sem,
            ),
            remote(
                agrad.at[pl.ds(pl.multiple_of((1 - core) * width, 16), width), :],
                agrad_ref.at[:, mine], send_sem, recv_sem, dp=sibling,
            ),
        )

    @pl.when(step == steps - 1)
    def _():
        for copy in agrad_copies():
            copy.start()
        chips = groups // 2
        pieces = [
            (normal_t, widened.at[:, pl.ds(first, model)]) for first in range(0, 2 * ff, model)
        ]
        pieces += [(att_all, low), (hidden_t, cot_all)]
        spans = []
        offset = 0

        def group_of(chip, c):
            return (2 * (chip // nfsdp) + c) * nfsdp + chip % nfsdp

        def twin_copy(number, chip):
            rows = spans[number]
            return remote(
                packed.at[group_of(chip, 0) + (1 - core) * nfsdp, rows], twin.at[chip, rows],
                send_t.at[number, chip], recv_t.at[number, chip], dp=sibling,
            )

        for number, (left, right) in enumerate(pieces):
            grad = dot(left[...], right[...])
            rows = grad.shape[0] // groups
            spans.append(slice(offset, offset + rows))
            packed[:, spans[-1], :] = grad.astype(bf16).reshape(groups, rows, model)
            offset += rows
            for chip in range(chips):
                twin_copy(number, chip).start()
        for number, rows in enumerate(spans):
            for chip in range(chips):
                twin_copy(number, chip).wait()
                mine = packed[group_of(chip, 0) + core * nfsdp, rows].astype(f32)
                shard_ref[chip, rows] = (mine + twin[chip, rows].astype(f32)).astype(bf16)
        for copy in agrad_copies():
            copy.wait()


def feed_forward(x, attended, cotangent, out_w, up_w, down_w, gains, nfsdp, groups):
    half = x.shape[0]
    ff = down_w.shape[0]
    block = chunk_of(half, 256)
    chips, pieces = groups // 2, 2 * ff // D + 2
    rows = (2 * ff // D * D + ff + D) // groups
    dma = pltpu.SemaphoreType.DMA

    def whole(array):
        return pl.BlockSpec(array.shape, lambda i: (0,) * array.ndim, pipeline_mode=pl.Buffered(1))

    by_rows = pl.BlockSpec((block, D), lambda i: (i, 0))
    return pl.pallas_call(
        partial(ffn_kernel, nfsdp, groups),
        grid=(half // block,),
        in_specs=[
            by_rows,
            pl.BlockSpec((D, block), lambda i: (0, i)),
            by_rows,
            whole(out_w), whole(up_w), whole(down_w), whole(gains),
        ],
        out_specs=[
            by_rows,
            by_rows,
            any_spec,
            vmem_spec,
        ],
        out_shape=[
            jax.ShapeDtypeStruct((half, D), bf16),
            jax.ShapeDtypeStruct((half, D), f32),
            jax.ShapeDtypeStruct((D // 2, 2 * half), bf16),
            jax.ShapeDtypeStruct((chips, rows, D), bf16),
        ],
        scratch_shapes=[
            pltpu.VMEM((D, half), bf16),
            pltpu.VMEM((ff, half), bf16),
            pltpu.VMEM((half, 2 * ff), bf16),
            pltpu.VMEM((half, D), bf16),
            pltpu.VMEM((half, D), bf16),
            pltpu.VMEM((D, half), bf16),
            pltpu.VMEM((D, half), bf16),
            pltpu.VMEM((groups, rows, D), bf16),
            pltpu.VMEM((chips, rows, D), bf16),
            dma, dma, dma, dma((pieces, chips)), dma((pieces, chips)),
        ],
        compiler_params=params(3),
        name="feed_forward",
        cost_estimate=pl.CostEstimate(
            flops=6 * half * D * (3 * ff + D), bytes_accessed=32 << 20,
            transcendentals=2 * half * ff,
        ),
    )(x, attended, cotangent, out_w, up_w, down_w, gains)


def chips_of(nfsdp, groups):
    dp, core, x, z, y = here()
    chips = groups // 2
    mine = x * nfsdp + y
    found = []
    for j in range(1, chips):
        other = lax.rem(mine + j, chips)
        found.append((other, other // nfsdp, lax.rem(other, nfsdp)))
    return mine, found


def plane_partners(nfsdp, groups):
    dp, core, x, z, y = here()
    return [{"dp": 2 * cx + core, "fsdp": cy} for _, cx, cy in chips_of(nfsdp, groups)[1]]


def z_sum(ctx, sent, got, final, sems):
    z = lax.axis_index("ctx")
    send_a, recv_a, send_b, recv_b = sems

    def piece(k):
        to = lax.rem(z + k, ctx)
        return remote(sent.at[to], got.at[k - 1], send_a.at[k - 1], recv_a.at[k - 1], ctx=to)

    def result(k):
        to = lax.rem(z + k, ctx)
        return remote(final.at[z], final.at[z], send_b.at[k - 1], recv_b.at[k - 1], ctx=to)

    def start():
        for k in range(1, ctx):
            piece(k).start()

    def middle():
        for k in range(1, ctx):
            piece(k).wait()
        total = sent[z].astype(f32)
        for k in range(1, ctx):
            total = total + got[k - 1].astype(f32)
        final[z] = total.astype(bf16)
        for k in range(1, ctx):
            result(k).start()

    def finish():
        for k in range(1, ctx):
            result(k).wait()

    return start, middle, finish


def z_sems(ctx):
    return [pltpu.SemaphoreType.DMA((ctx - 1,))] * 4


def column_sum(ctx, nfsdp, groups, src, got, zsent, zgot, final, out, sems):
    dp, core, x, z, y = here()
    sibling = dp + 1 - 2 * core
    mine, others = chips_of(nfsdp, groups)
    send_q, recv_q, send_s, recv_s, local_s = sems[:5]
    z_start, z_middle, z_finish = z_sum(ctx, zsent, zgot, final, sems[5:])
    per = ctx // 2

    def row_of(cx, cy, c):
        return (2 * cx + c) * nfsdp + cy

    def copy(j, c):
        _, cx, cy = others[j]
        return remote(
            src.at[row_of(cx, cy, c)], got.at[j, c], send_q.at[j, c], recv_q.at[j, c],
            dp=2 * cx + core, fsdp=cy,
        )

    def send():
        for j in range(len(others)):
            for c in range(2):
                copy(j, c).start()

    def plane():
        for j in range(len(others)):
            for c in range(2):
                copy(j, c).wait()
        rows, columns = src.shape[1], src.shape[2]
        for c in range(2):
            total = src[row_of(x, y, c)].astype(f32)
            for j in range(len(others)):
                total = total + got[j, c].astype(f32)
            zsent[c * per : (c + 1) * per] = total.astype(bf16).reshape(per, rows // per, columns)
        z_start()

    def swaps():
        return (
            pltpu.make_async_copy(final.at[pl.ds(core * per, per)], out.at[core], local_s),
            remote(
                final.at[pl.ds((1 - core) * per, per)], out.at[core], send_s, recv_s, dp=sibling
            ),
        )

    def swap():
        z_finish()
        for each in swaps():
            each.start()

    def finish():
        for each in swaps():
            each.wait()

    return send, plane, z_middle, swap, finish


def column_scratch(ctx, groups, rows, columns):
    chips, per = groups // 2, 2 * rows // ctx
    dma = pltpu.SemaphoreType.DMA
    buffers = [
        pltpu.VMEM((chips - 1, 2, rows, columns), bf16),
        pltpu.VMEM((ctx, per, columns), bf16),
        pltpu.VMEM((ctx - 1, per, columns), bf16),
        pltpu.VMEM((ctx, per, columns), bf16),
    ]
    return buffers, [dma((chips - 1, 2)), dma((chips - 1, 2)), dma, dma, dma] + z_sems(ctx)


def plane_sum(ctx, nfsdp, groups, spans, own, got, zsent, zgot, final, sems):
    dp, core, x, z, y = here()
    mine, others = chips_of(nfsdp, groups)
    send_q, recv_q = sems[:2]
    per = zsent.shape[2]
    z_stages = [
        z_sum(
            ctx, zsent.at[n], zgot.at[n], final.at[n],
            [sems[k].at[n] for k in range(2, 6)],
        )
        for n in range(len(spans))
    ]

    def copy(number, j):
        chip, cx, cy = others[j]
        rows = spans[number]
        return remote(
            own.at[chip, rows], got.at[j, rows], send_q.at[number, j], recv_q.at[number, j],
            dp=2 * cx + core, fsdp=cy,
        )

    def begin():
        for number in range(len(spans)):
            for j in range(len(others)):
                copy(number, j).start()

    def plane(number):
        rows = spans[number]
        for j in range(len(others)):
            copy(number, j).wait()
        total = own[mine, rows].astype(f32)
        for j in range(len(others)):
            total = total + got[j, rows].astype(f32)
        low = total.astype(bf16)
        count = low.shape[0]
        for k in range(ctx):
            first, last = min(k * per, count), min((k + 1) * per, count)
            if last > first:
                zsent[number, k, : last - first, :] = low[first:last, :]
            if last - first < per:
                zsent[number, k, last - first :, :] = jnp.zeros(
                    (per - last + first, low.shape[1]), bf16
                )
        z_stages[number][0]()

    def middle(number):
        z_stages[number][1]()

    def finish():
        for stage in z_stages:
            stage[2]()

    return begin, plane, middle, finish


def plane_scratch(ctx, groups, spans):
    chips, count = groups // 2, len(spans)
    most = max(span.stop - span.start for span in spans)
    per = -(-most // (16 * ctx)) * 16
    dma = pltpu.SemaphoreType.DMA
    buffers = [
        pltpu.VMEM((chips - 1, spans[-1].stop, D), bf16),
        pltpu.VMEM((count, ctx, per, D), bf16),
        pltpu.VMEM((count, ctx - 1, per, D), bf16),
        pltpu.VMEM((count, ctx, per, D), bf16),
    ]
    return buffers, [dma((count, chips - 1))] * 2 + [dma((count, ctx - 1))] * 4


def attend_back_kernel(
    ctx, nfsdp, groups, seqs, spans, parts,
    q_ref, k_ref, v_ref, o_ref, up_ref, log_ref, cos_all, sin_all, cos_ref, sin_ref,
    normal_ref, shard_ref, out_ref, wt_ref, x_ref, rgrad_ref, gain_ref,
    sums_ref, qkv_ref, output_ref, token_ref,
    q_rows, up_rows, up_cols, delta, dq_sum, dproj, pair_proj, fresh,
    dn_send, dn_recv, tg_send, *scratch,
):
    head, step = pl.program_id(0), pl.program_id(1)
    heads, steps = pl.num_programs(0), pl.num_programs(1)
    dp, core, x, z, y = here()
    sibling = dp + 1 - 2 * core
    length = q_ref.shape[-1]
    rows = k_ref.shape[-1]
    chunk = chunk_of(length, 512)
    pairs = fresh.shape[0]
    total_steps = pairs * 2 * (length // rows)
    last = total_steps - 1
    now = head * steps + step

    def take(count):
        nonlocal scratch
        taken, scratch = scratch[:count], scratch[count:]
        return taken

    send_n, recv_n = take(2)
    begin, plane, middle, plane_finish = plane_sum(
        ctx, nfsdp, groups, spans, shard_ref, *(bufs := take(4)), take(6)
    )
    out_start, out_finish = to_blocks(ctx, seqs, 1, out_ref, output_ref, *take(3))
    token_start, token_finish = to_blocks(ctx, seqs, parts, tg_send, token_ref, *take(3))
    columns = []
    for p in range(pairs):
        columns.append(column_sum(
            ctx, nfsdp, groups, fresh.at[p], *take(4), qkv_ref.at[p], take(9)
        ))

    @pl.when(now == 0)
    def _():
        greet(column_partners(ctx) + plane_partners(nfsdp, groups))
        begin()
        for i in range(ctx // 2):
            out_start(i, 0)

    @pl.when(step == 0)
    def _():
        q_rows[...] = q_ref[0, 0].T
        upstream = up_ref[0]
        up_cols[...] = upstream
        up_rows[...] = upstream.T
        delta[...] = jnp.sum(
            upstream.astype(f32) * o_ref[0].astype(f32), 0, keepdims=True
        )
        dq_sum[...] = jnp.zeros_like(dq_sum)

    key_t = k_ref[0, 0]
    key = key_t.T
    value = v_ref[0, 0].T
    dk = None
    dv = None
    for start in range(0, length, chunk):
        place = slice(start, start + chunk)
        scores = dot(key, q_ref[0, 0, :, place])
        weights = jnp.exp2(scores - log_ref[0, :, place])
        weight_grad = dot(value, up_cols[:, place])
        score_grad = (weights * (weight_grad - delta[:, place])).astype(bf16)
        dv_term = dot(weights.astype(bf16), up_rows[place, :])
        dk_term = dot(score_grad, q_rows[place, :])
        dv = dv_term if dv is None else dv + dv_term
        dk = dk_term if dk is None else dk + dk_term
        dq_sum[:, place] += dot(key_t, score_grad)
    block = pl.ds(pl.multiple_of(step * rows, 128), rows)
    upper, lower = rope_back((dk * math.log(2.0)).T, cos_ref[...], sin_ref[...])
    dproj[1, head, :HALF, block] = upper.astype(bf16)
    dproj[1, head, HALF:, block] = lower.astype(bf16)
    dproj[2, head, :, block] = dv.T.astype(bf16)

    @pl.when(step == steps - 1)
    def _():
        upper, lower = rope_back(dq_sum[...] * score_scale, cos_all[...], sin_all[...])
        dproj[0, head, :HALF, :] = upper.astype(bf16)
        dproj[0, head, HALF:, :] = lower.astype(bf16)
        for part in range(3):
            first = pl.multiple_of(part * 2 * HEAD + lax.rem(head, 2) * HEAD, HEAD)
            pair_proj[pl.ds(first, HEAD), :] = dproj[part, head]

    @pl.when(jnp.logical_and(step == steps - 1, lax.rem(head, 2) == 1))
    def _():
        grad = dot(normal_ref[...], pair_proj[...], 1, 1).astype(bf16)
        fresh[head // 2] = grad.reshape(fresh.shape[1:])

    def at(turn, what, *args):
        @pl.when(now == total_steps * turn // 48)
        def _():
            what(*args)

    for number in range(len(spans)):
        at(11 + 27 * number // len(spans), plane, number)
    for number in range(len(spans)):
        at(21 + 25 * number // len(spans), middle, number)
    each = total_steps // pairs
    for p in range(pairs - 1):
        done = (p + 1) * each - 1
        gap = min(each, total_steps - 1 - done) * 5 // 16
        for number, what in enumerate(columns[p][: 4 if p < pairs - 2 else 3]):
            @pl.when(now == done + gap * number)
            def _():
                what()

    half = x_ref.shape[0]
    blocks = tg_send.shape[0]
    block_len = half // blocks
    size = block_len // parts

    def dn_rows(first):
        place = pl.ds(pl.multiple_of(first, 128), size)
        grads = dproj[:, :, :, place].reshape(wt_ref.shape[0], size)
        return dot(grads, wt_ref[...], 0, 0)

    def sibling_copy(number):
        return remote(
            dn_send.at[number], dn_recv.at[number], send_n.at[number], recv_n.at[number],
            dp=sibling,
        )

    def sibling_part(number):
        dn_send[number] = dn_rows((1 - core) * half + number * size).astype(bf16)
        sibling_copy(number).start()

    def own_part(number):
        first = number * size
        place = slice(first, first + size)
        gain = gain_ref[0:1, :]
        grad = dn_rows(core * half + first)
        sibling_copy(number).wait()
        grad = grad + dn_recv[number].astype(f32)
        normed, inverse, _ = layer_norm(x_ref[place, :].astype(f32), gain)
        token = rgrad_ref[place, :] + norm_back(grad, normed, inverse, gain)
        i, part = number // parts, number % parts
        tg_send[i, part * size : (part + 1) * size, :] = token.astype(bf16)
        token_start(i, part)

    @pl.when(now == last)
    def _():
        ending = columns[pairs - 1]
        ending[0]()
        count = blocks * parts
        for number in range(count + 1):
            if number < count:
                sibling_part(number)
            if number > 0:
                own_part(number - 1)
            if number == 2:
                ending[1]()
        if pairs > 1:
            columns[pairs - 2][3]()
        ending[2]()
        out_finish()
        plane_finish()
        ending[3]()
        for each_sum in columns:
            each_sum[4]()
        sums_ref[...] = bufs[3][...]
        token_finish()


def attend_back_chip(
    heads_t, attended, upstream, log_total, cosine, sine, normal_t, shards, spans, output,
    wt, x, rgrad, gains, ctx, nfsdp, groups, seqs,
):
    _, count, _, length = heads_t.shape
    rows = chunk_of(length, 256)
    pairs = count // 2
    half = length // 2
    block_len = length // ctx
    parts = 2 if block_len % 256 == 0 else 1
    size = block_len // parts
    shard_rows = normal_t.shape[0] // groups
    plane_bufs, plane_signals = plane_scratch(ctx, groups, spans)
    column_bufs, column_signals = column_scratch(ctx, groups, shard_rows, 6 * HEAD)
    full = pl.BlockSpec((1, HEAD, length), lambda h, k: (h, 0, 0))
    table = pl.BlockSpec((HALF, length), lambda h, k: (0, 0), pipeline_mode=pl.Buffered(1))
    table_part = pl.BlockSpec((HALF, rows), lambda h, k: (0, k))
    dma = pltpu.SemaphoreType.DMA

    def whole(array):
        return pl.BlockSpec(
            array.shape, lambda h, k: (0,) * array.ndim, pipeline_mode=pl.Buffered(1)
        )

    return pl.pallas_call(
        partial(attend_back_kernel, ctx, nfsdp, groups, seqs, spans, parts),
        grid=(count, length // rows),
        in_specs=[
            pl.BlockSpec((1, 1, HEAD, length), lambda h, k: (0, h, 0, 0)),
            pl.BlockSpec((1, 1, HEAD, rows), lambda h, k: (1, h, 0, k)),
            pl.BlockSpec((1, 1, HEAD, rows), lambda h, k: (2, h, 0, k)),
            full,
            full,
            pl.BlockSpec((1, 1, length), lambda h, k: (h, 0, 0)),
            table,
            table,
            table_part,
            table_part,
            whole(normal_t), whole(shards), any_spec, whole(wt), whole(x), whole(rgrad),
            whole(gains),
        ],
        out_specs=[vmem_spec, any_spec, any_spec, any_spec],
        out_shape=[
            jax.ShapeDtypeStruct(plane_bufs[3].shape, bf16),
            jax.ShapeDtypeStruct(
                (pairs, 2, ctx // 2, 2 * shard_rows // ctx, 6 * HEAD), bf16
            ),
            jax.ShapeDtypeStruct((seqs, block_len, D), bf16),
            jax.ShapeDtypeStruct((seqs, block_len, D), bf16),
        ],
        scratch_shapes=[
            pltpu.VMEM((length, HEAD), bf16),
            pltpu.VMEM((length, HEAD), bf16),
            pltpu.VMEM((HEAD, length), bf16),
            pltpu.VMEM((1, length), f32),
            pltpu.VMEM((HEAD, length), f32),
            pltpu.VMEM((3, count, HEAD, length), bf16),
            pltpu.VMEM((6 * HEAD, length), bf16),
            pltpu.VMEM((pairs, groups, shard_rows, 6 * HEAD), bf16),
            pltpu.VMEM((half // size, size, D), bf16),
            pltpu.VMEM((half // size, size, D), bf16),
            pltpu.VMEM((ctx // 2, block_len, D), bf16),
            dma((half // size,)), dma((half // size,)),
            *plane_bufs, *plane_signals,
            *block_sems(ctx, seqs, 1), *block_sems(ctx, seqs, parts),
            *(column_bufs + column_signals) * pairs,
        ],
        compiler_params=params(4),
        name="attend_back",
        cost_estimate=pl.CostEstimate(
            flops=40 * count * length * length * HEAD,
            bytes_accessed=16 * count * length * HEAD,
            transcendentals=count * length * length,
        ),
    )(
        heads_t, heads_t, heads_t, attended, upstream, log_total,
        cosine, sine, cosine, sine, normal_t, shards, output, wt, x, rgrad, gains,
    )


def chip_body(
    tokens,
    cotangent,
    qkv_weight,
    out_weight,
    up_weight,
    down_weight,
    attention_gain,
    feedforward_gain,
):
    ctx, nfsdp = lax.axis_size("ctx"), lax.axis_size("fsdp")
    groups = lax.axis_size("dp") * nfsdp
    seqs, block_len, _ = tokens.shape
    length = block_len * ctx
    width = D // 2
    shard_rows = qkv_weight.shape[0]
    me = lax.axis_index("dp") * nfsdp + lax.axis_index("fsdp")
    gain_rows = lax.dynamic_update_slice(
        jnp.zeros((16, D), bf16), jnp.stack([attention_gain, feedforward_gain]),
        (0, me * shard_rows),
    )
    cosine, sine = rope_rows(length)
    out_whole = gather_rows(out_weight)
    up_whole = gather_rows(up_weight)
    down_whole = gather_rows(down_weight)
    heads_t, normal_t, x_half, wt, gains = prologue(
        tokens, qkv_weight, gain_rows, cosine, sine, ctx, nfsdp, groups
    )
    attended, log_total, att_all, cot_half = attend_chip(heads_t, cotangent, ctx)
    output, rgrad, agrad, shards = feed_forward(
        x_half, att_all.reshape(D, length // 2), cot_half.reshape(length // 2, D),
        out_whole, up_whole, down_whole, gains, nfsdp, groups,
    )
    up_parts = up_weight.shape[1] // D
    rows = [shard_rows] * (up_parts - 1) + [
        shard_rows + out_weight.shape[0], down_weight.shape[0]
    ]
    if up_parts == 3:
        rows = [2 * shard_rows] + rows[2:]
    spans, first = [], 0
    for count in rows:
        spans.append(slice(first, first + count))
        first += count
    sums, pieces, output, token_low = attend_back_chip(
        heads_t, attended, agrad.reshape(width // HEAD, HEAD, length), log_total,
        cosine, sine, normal_t, shards, spans, output.reshape(ctx // 2, block_len, D),
        wt, x_half, rgrad, gains, ctx, nfsdp, groups, seqs,
    )

    shard = [
        sums[n].reshape(-1, D)[: span.stop - span.start].astype(f32)
        for n, span in enumerate(spans)
    ]
    shard = jnp.concatenate(shard, 0)
    cuts = [shard[i * shard_rows : (i + 1) * shard_rows] for i in range(up_parts)]
    up_shard = jnp.concatenate(cuts, -1)
    offset = up_parts * shard_rows
    out_shard = shard[offset : offset + out_weight.shape[0]]
    down_shard = shard[offset + out_weight.shape[0] :]
    pieces = pieces.reshape(-1, 2, shard_rows, 3, 2 * HEAD)
    qkv_shard = jnp.transpose(pieces, (2, 3, 1, 0, 4)).reshape(shard_rows, 3 * D).astype(f32)
    attn_gain_grad = jnp.sum(qkv_weight.astype(f32) * qkv_shard, -1) / attention_gain.astype(f32)
    ffn_gain_grad = jnp.sum(up_weight.astype(f32) * up_shard, -1) / feedforward_gain.astype(f32)
    return (
        output,
        token_low.astype(f32),
        qkv_shard,
        out_shard,
        up_shard,
        down_shard,
        attn_gain_grad,
        ffn_gain_grad,
    )


def body(tokens, cotangent, qkv_weight, *others):
    ctx, dp = lax.axis_size("ctx"), lax.axis_size("dp")
    one_each = ctx == 2 * tokens.shape[0] and dp % 2 == 0 and ctx & (ctx - 1) == 0 and HEADS % 4 == 0
    aligned = tokens.shape[1] % 128 == 0 and 2 * qkv_weight.shape[0] % (16 * ctx) == 0
    chosen = chip_body if one_each and aligned else general_body
    return chosen(tokens, cotangent, qkv_weight, *others)


def solution(mesh):
    rows = P(("dp", "fsdp"), "ctx", None)
    weight = P(("dp", "fsdp"), None)
    gain = P(("dp", "fsdp"))
    return jax.shard_map(
        body,
        mesh=mesh,
        in_specs=(rows, rows, weight, weight, weight, weight, gain, gain),
        out_specs=(rows, rows, weight, weight, weight, weight, gain, gain),
        check_vma=False,
    )
```

```python
from functools import partial
import math

import jax
import jax.numpy as jnp
import numpy as np
from jax import lax
from jax.experimental import pallas as pl
from jax.experimental.pallas import tpu as pltpu
from jax.sharding import PartitionSpec as P

D = 768
HEADS = 12
HEAD = 64
FF = 1152
HALF = HEAD // 2

norm_eps = 1e-05
rope_base = 160000.0
score_scale = HEAD ** (-0.5)
score_base2 = score_scale * math.log2(math.e)
WEIGHT_AXES = ("dp", "fsdp")
f32 = jnp.float32
bf16 = jnp.bfloat16


def dot(left, right, left_dim=1, right_dim=0):
    return lax.dot_general(
        left, right, (((left_dim,), (right_dim,)), ((), ())), preferred_element_type=f32
    )


def layer_norm(values, norm_gain):
    centre = jnp.mean(values, -1, keepdims=True)
    centred = values - centre
    inverse = lax.rsqrt(jnp.mean(centred * centred, -1, keepdims=True) + norm_eps)
    normed = centred * inverse
    return (normed, inverse, normed * norm_gain)


def norm_back(upstream, normed, inverse, norm_gain):
    scaled = upstream * norm_gain
    return (
        scaled
        - jnp.mean(scaled, -1, keepdims=True)
        - normed * jnp.mean(scaled * normed, -1, keepdims=True)
    ) * inverse


def gated_gelu(inputs, gating):
    return jax.nn.gelu(inputs, approximate=False) * gating


def rope_rows(length):
    frequency = rope_base ** (-2.0 * jnp.arange(HALF, dtype=f32) / HEAD)
    angles = frequency[:, None] * jnp.arange(length, dtype=jnp.int32).astype(f32)[None, :]
    return (jnp.cos(angles), jnp.sin(angles))


def chunk_of(length, most):
    return most if length % most == 0 else length


def forward_kernel(q_ref, k_ref, v_ref, o_ref, log_ref, k_rows, v_wide):
    length = k_ref.shape[-1]
    chunk = chunk_of(length, 512)

    @pl.when(pl.program_id(1) == 0)
    def _():
        k_rows[...] = k_ref[0, 0].T
        v_wide[:HEAD, :] = v_ref[0, 0]
        v_wide[HEAD:, :] = jnp.ones((v_wide.shape[0] - HEAD, length), bf16)

    query = q_ref[0, 0]
    highest = None
    total = None
    for start in range(0, length, chunk):
        scores = dot(k_rows[start : start + chunk, :], query) * score_base2
        top = jnp.max(scores, 0, keepdims=True)
        new_high = top if highest is None else jnp.maximum(highest, top)
        weights = jnp.exp2(scores - new_high).astype(bf16)
        term = dot(v_wide[:, start : start + chunk], weights)
        total = term if total is None else total * jnp.exp2(highest - new_high) + term
        highest = new_high
    denominator = total[HEAD : HEAD + 1, :]
    o_ref[0, 0] = (total[:HEAD, :] / denominator).astype(bf16)
    log_ref[0] = highest + jnp.log2(denominator)


def attend(heads_t, block_len):
    _, count, _, length = heads_t.shape
    blocks = length // block_len
    return pl.pallas_call(
        forward_kernel,
        grid=(count, blocks),
        in_specs=[
            pl.BlockSpec((1, 1, HEAD, block_len), lambda h, c: (0, h, 0, c)),
            pl.BlockSpec((1, 1, HEAD, length), lambda h, c: (1, h, 0, 0)),
            pl.BlockSpec((1, 1, HEAD, length), lambda h, c: (2, h, 0, 0)),
        ],
        out_specs=[
            pl.BlockSpec((1, 1, HEAD, block_len), lambda h, c: (c, h, 0, 0)),
            pl.BlockSpec((1, 1, block_len), lambda h, c: (h, 0, c)),
        ],
        out_shape=[
            jax.ShapeDtypeStruct((blocks, count, HEAD, block_len), bf16),
            jax.ShapeDtypeStruct((count, 1, length), f32),
        ],
        scratch_shapes=[
            pltpu.VMEM((length, HEAD), bf16),
            pltpu.VMEM((HEAD + 16, length), bf16),
        ],
        compiler_params=pltpu.CompilerParams(vmem_limit_bytes=40 << 20),
        cost_estimate=pl.CostEstimate(
            flops=16 * count * length * length * HEAD,
            bytes_accessed=10 * count * length * HEAD,
            transcendentals=count * length * length,
        ),
    )(heads_t, heads_t, heads_t)


def rope_back(grad_t, cosine, sine):
    first, second = grad_t[:HALF, :], grad_t[HALF:, :]
    return (first * cosine + second * sine, second * cosine - first * sine)


def backward_kernel(
    q_ref, k_ref, v_ref, o_ref, up_ref, log_ref, cos_all, sin_all, cos_ref, sin_ref,
    dq_ref, dk_ref, dv_ref, q_rows, up_rows, up_cols, delta, dq_sum,
):
    step = pl.program_id(1)
    blocks, block_len = up_ref.shape[0], up_ref.shape[-1]
    length = q_ref.shape[-1]
    chunk = chunk_of(length, 512)

    @pl.when(step == 0)
    def _():
        q_rows[...] = q_ref[0, 0].T
        for number in range(blocks):
            place = slice(number * block_len, (number + 1) * block_len)
            upstream = up_ref[number, 0]
            up_cols[:, place] = upstream
            up_rows[place, :] = upstream.T
            delta[:, place] = jnp.sum(
                upstream.astype(f32) * o_ref[number, 0].astype(f32), 0, keepdims=True
            )
        dq_sum[...] = jnp.zeros_like(dq_sum)

    key_t = k_ref[0, 0]
    key = key_t.T
    value = v_ref[0, 0].T
    dk = None
    dv = None
    for start in range(0, length, chunk):
        place = slice(start, start + chunk)
        scores = dot(key, q_ref[0, 0, :, place]) * score_base2
        weights = jnp.exp2(scores - log_ref[0, :, place])
        weight_grad = dot(value, up_cols[:, place])
        score_grad = (weights * (weight_grad - delta[:, place])).astype(bf16)
        dv_term = dot(weights.astype(bf16), up_rows[place, :])
        dk_term = dot(score_grad, q_rows[place, :])
        dv = dv_term if dv is None else dv + dv_term
        dk = dk_term if dk is None else dk + dk_term
        dq_sum[:, place] += dot(key_t, score_grad)
    upper, lower = rope_back((dk * score_scale).T, cos_ref[...], sin_ref[...])
    dk_ref[0, :HALF, :] = upper.astype(bf16)
    dk_ref[0, HALF:, :] = lower.astype(bf16)
    dv_ref[0] = dv.T.astype(bf16)

    @pl.when(step == pl.num_programs(1) - 1)
    def _():
        upper, lower = rope_back(dq_sum[...] * score_scale, cos_all[...], sin_all[...])
        dq_ref[0, :HALF, :] = upper.astype(bf16)
        dq_ref[0, HALF:, :] = lower.astype(bf16)


def attend_back(heads_t, attended, upstream, log_total, cosine, sine):
    _, count, _, length = heads_t.shape
    blocks, _, _, block_len = attended.shape
    rows = chunk_of(length, 256)
    split = pl.BlockSpec((blocks, 1, HEAD, block_len), lambda h, k: (0, h, 0, 0))
    shape = jax.ShapeDtypeStruct((count, HEAD, length), bf16)
    return pl.pallas_call(
        backward_kernel,
        grid=(count, length // rows),
        in_specs=[
            pl.BlockSpec((1, 1, HEAD, length), lambda h, k: (0, h, 0, 0)),
            pl.BlockSpec((1, 1, HEAD, rows), lambda h, k: (1, h, 0, k)),
            pl.BlockSpec((1, 1, HEAD, rows), lambda h, k: (2, h, 0, k)),
            split,
            split,
            pl.BlockSpec((1, 1, length), lambda h, k: (h, 0, 0)),
            pl.BlockSpec((HALF, length), lambda h, k: (0, 0)),
            pl.BlockSpec((HALF, length), lambda h, k: (0, 0)),
            pl.BlockSpec((HALF, rows), lambda h, k: (0, k)),
            pl.BlockSpec((HALF, rows), lambda h, k: (0, k)),
        ],
        out_specs=[
            pl.BlockSpec((1, HEAD, length), lambda h, k: (h, 0, 0)),
            pl.BlockSpec((1, HEAD, rows), lambda h, k: (h, 0, k)),
            pl.BlockSpec((1, HEAD, rows), lambda h, k: (h, 0, k)),
        ],
        out_shape=[shape, shape, shape],
        scratch_shapes=[
            pltpu.VMEM((length, HEAD), bf16),
            pltpu.VMEM((length, HEAD), bf16),
            pltpu.VMEM((HEAD, length), bf16),
            pltpu.VMEM((1, length), f32),
            pltpu.VMEM((HEAD, length), f32),
        ],
        compiler_params=pltpu.CompilerParams(vmem_limit_bytes=40 << 20),
        cost_estimate=pl.CostEstimate(
            flops=40 * count * length * length * HEAD,
            bytes_accessed=16 * count * length * HEAD,
            transcendentals=count * length * length,
        ),
    )(heads_t, heads_t, heads_t, attended, upstream, log_total, cosine, sine, cosine, sine)


def gather_rows(shard):
    return lax.all_gather(shard, WEIGHT_AXES, axis=0, tiled=True)


def exchange(blocks):
    return lax.all_to_all(blocks, "ctx", 0, 0, tiled=True)


def general_body(
    tokens,
    cotangent,
    qkv_weight,
    out_weight,
    up_weight,
    down_weight,
    attention_gain,
    feedforward_gain,
):
    ctx = lax.axis_size("ctx")
    groups = lax.axis_size("dp") * lax.axis_size("fsdp")
    seq_count, block_len = (tokens.shape[0], tokens.shape[1])
    length = block_len * ctx
    sets = math.gcd(seq_count, ctx)
    each = seq_count // sets
    teams = ctx // sets
    own = -(-HEADS // teams)
    width = own * HEAD
    spare = teams * own - HEADS
    halves = 2 if own % 2 == 0 else 1
    part = own // halves
    shard_rows = qkv_weight.shape[0]
    row_count = seq_count * block_len

    moved = [
        exchange(jnp.repeat(tokens[turn::each], teams, axis=0)).reshape(length, D)
        for turn in range(each)
    ]

    by_head = qkv_weight.reshape(shard_rows, 3, D)
    if spare:
        by_head = jnp.pad(by_head, ((0, 0), (0, 0), (0, spare * HEAD)))
    team = lax.rem(lax.axis_index("ctx"), teams)
    own_columns = lax.dynamic_slice_in_dim(by_head, team * width, width, 2)
    gain_columns = jnp.pad(
        jnp.stack([attention_gain, feedforward_gain], -1), ((0, 0), (0, 126))
    )
    first_gather = gather_rows(
        jnp.concatenate([own_columns.reshape(shard_rows, 3 * width), gain_columns], -1)
    )
    qkv_own = first_gather[:, : 3 * width]
    attn_gain = first_gather[:, 3 * width].astype(f32)
    ffn_gain = first_gather[:, 3 * width + 1].astype(f32)
    out_whole = gather_rows(out_weight)
    up_whole = gather_rows(up_weight)
    down_whole = gather_rows(down_weight)
    cosine, sine = rope_rows(length)

    saved = []
    for turn in range(each):
        normal = layer_norm(moved[turn].astype(f32), attn_gain)[2].astype(bf16)
        by_part = qkv_own.reshape(D, 3, halves, part * HEAD)
        pieces = []
        for half in range(halves):
            weight = by_part[:, :, half].reshape(D, 3 * part * HEAD)
            projected = dot(weight, normal, 0, 1).reshape(3, part, 2, HALF, length)
            first, second = (projected[:2, :, 0], projected[:2, :, 1])
            turned = jnp.stack(
                [first * cosine - second * sine, second * cosine + first * sine], 2
            )
            heads_t = (
                jnp.concatenate([turned, projected[2:]], 0)
                .astype(bf16)
                .reshape(3, part, HEAD, length)
            )
            attended, log_total = attend(heads_t, block_len)
            pieces.append((heads_t, attended, log_total, exchange(attended)))
        saved.append((normal, pieces))

    columns = []
    for number in range(seq_count):
        chosen, turn = divmod(number, each)
        got = [
            piece[3].reshape(sets, teams, part, HEAD, block_len)[chosen]
            for piece in saved[turn][1]
        ]
        columns.append(jnp.concatenate(got, 1).reshape(teams * width, block_len)[:D])
    attended_t = jnp.concatenate(columns, 1)

    inputs = tokens.reshape(row_count, D).astype(f32)
    residual = inputs + dot(attended_t, out_whole, 0, 0)
    normed_b, inverse_b, scaled_b = layer_norm(residual, ffn_gain)
    normal_b = scaled_b.astype(bf16)
    widened = dot(normal_b, up_whole)
    hidden, hidden_back = jax.vjp(gated_gelu, widened[:, :FF], widened[:, FF:])
    hidden_low = hidden.astype(bf16)
    output = (residual + dot(hidden_low, down_whole)).astype(bf16)
    upstream = cotangent.reshape(row_count, D)
    hidden_grad = dot(upstream, down_whole, 1, 1)
    input_grad, gating_grad = hidden_back(hidden_grad)
    widened_grad = jnp.concatenate([input_grad, gating_grad], -1).astype(bf16)
    normal_b_grad = dot(widened_grad, up_whole, 1, 1)
    residual_grad = upstream.astype(f32) + norm_back(normal_b_grad, normed_b, inverse_b, ffn_gain)
    residual_low = residual_grad.astype(bf16)

    out_heads = out_whole
    if spare:
        out_heads = jnp.pad(out_heads, ((0, spare * HEAD), (0, 0)))
    out_heads = out_heads.reshape(teams, halves, part * HEAD, D)
    arrived = []
    for turn in range(each):
        for half in range(halves):
            weight = out_heads[:, half].reshape(teams * part * HEAD, D)
            sent = [
                dot(weight, residual_low[start : start + block_len], 1, 1).astype(bf16)
                for start in range(turn * block_len, row_count, each * block_len)
            ]
            arrived.append(exchange(jnp.stack(sent).reshape(ctx, part, HEAD, block_len)))

    down_grad = dot(hidden_low, upstream, 0, 0)
    up_grad = dot(normal_b, widened_grad, 0, 0)
    out_grad = dot(attended_t, residual_low)

    parts = [up_grad[:, start : start + D] for start in range(0, up_grad.shape[1], D)]
    parts += [down_grad, out_grad]
    packed = jnp.concatenate([item.astype(bf16).reshape(groups, -1, D) for item in parts], 1)
    shard = lax.psum_scatter(packed, WEIGHT_AXES, scatter_dimension=0, tiled=True)[0]
    shard = lax.psum(shard, "ctx").astype(f32)
    cuts = []
    offset = 0
    for item in parts:
        rows = item.shape[0] // groups
        cuts.append(shard[offset : offset + rows])
        offset += rows
    up_shard = jnp.concatenate(cuts[:-2], -1)
    down_shard, out_shard = cuts[-2:]

    back = []
    qkv_grad = 0.0
    for turn in range(each):
        normal, pieces = saved[turn]
        grads = []
        for half in range(halves):
            heads_t, attended, log_total, _ = pieces[half]
            grads.append(
                attend_back(
                    heads_t, attended, arrived[turn * halves + half], log_total, cosine, sine
                )
            )
        projected_grad = jnp.concatenate(
            [grads[half][which] for which in range(3) for half in range(halves)], 0
        ).reshape(3 * width, length)
        partial_grad = dot(projected_grad, qkv_own, 0, 1).astype(bf16)
        terms = exchange(partial_grad.reshape(ctx, block_len, D))
        back.append(terms.reshape(sets, teams, block_len, D).astype(f32).sum(1))
        qkv_grad = qkv_grad + dot(normal, projected_grad, 0, 1)
    normal_a_grad = jnp.stack(back, 1).reshape(row_count, D)
    normed_a, inverse_a, _ = layer_norm(inputs, attn_gain)
    token_grad = residual_grad + norm_back(normal_a_grad, normed_a, inverse_a, attn_gain)
    qkv_cut = lax.psum_scatter(
        qkv_grad.astype(bf16), WEIGHT_AXES, scatter_dimension=0, tiled=True
    )
    qkv_all = lax.all_gather(qkv_cut, "ctx", axis=0).astype(f32)
    qkv_all = qkv_all.reshape(sets, teams, shard_rows, 3, width).sum(0)
    qkv_shard = jnp.transpose(qkv_all, (1, 2, 0, 3)).reshape(shard_rows, 3, teams * width)
    qkv_shard = qkv_shard[:, :, :D].reshape(shard_rows, 3 * D)
    attn_gain_grad = jnp.sum(qkv_weight.astype(f32) * qkv_shard, -1) / attention_gain.astype(f32)
    ffn_gain_grad = jnp.sum(up_weight.astype(f32) * up_shard, -1) / feedforward_gain.astype(f32)
    return (
        output.reshape(seq_count, block_len, D),
        token_grad.reshape(seq_count, block_len, D),
        qkv_shard,
        out_shard,
        up_shard,
        down_shard,
        attn_gain_grad,
        ffn_gain_grad,
    )


MESH_ID = pl.DeviceIdType.MESH
VMEM_LIMIT = 60 << 20
vmem_spec = pl.BlockSpec(memory_space=pltpu.VMEM)
any_spec = pl.BlockSpec(memory_space=pl.ANY)


def here():
    dp = lax.axis_index("dp")
    return dp, lax.rem(dp, 2), dp // 2, lax.axis_index("ctx"), lax.axis_index("fsdp")


def params(number):
    return pltpu.CompilerParams(
        collective_id=number, has_side_effects=True, vmem_limit_bytes=VMEM_LIMIT
    )


def greet(partners):
    barrier = pltpu.get_barrier_semaphore()
    for partner in partners:
        pl.semaphore_signal(barrier, inc=1, device_id=partner, device_id_type=MESH_ID)
    pl.semaphore_wait(barrier, len(partners))


def remote(src, dst, send_sem, recv_sem, **device):
    return pltpu.make_async_remote_copy(
        src_ref=src, dst_ref=dst, send_sem=send_sem, recv_sem=recv_sem,
        device_id=device, device_id_type=MESH_ID,
    )


def near_order(place, count):
    def at(turn):
        block = place
        bit = 1
        while bit < count:
            flip = lax.rem(turn // bit, 2)
            block = block + flip * (bit - 2 * bit * lax.rem(place // bit, 2))
            bit *= 2
        return block
    return at


def prologue_kernel(
    ctx, nfsdp, groups, seqs,
    x_ref, w_ref, g_ref, cos_ref, sin_ref,
    heads_ref, normal_ref, half_ref, wt_ref, gain_ref,
    xbuf, wbuf, gbuf,
    send_x, recv_x, fwd_x, local_x, send_w, recv_w, local_w, send_g, recv_g, local_g,
):
    dp, core, x, z, y = here()
    sibling = dp + 1 - 2 * core
    block_len = x_ref.shape[1]
    shard_rows = w_ref.shape[0]
    width = wbuf.shape[1] // 3
    heads = width // HEAD
    me = dp * nfsdp + y
    lead = z // seqs == core
    others = []
    for j in range(1, groups):
        other = lax.rem(me + j, groups)
        others.append((other // nfsdp, lax.rem(other, nfsdp)))
    greet(
        [{"ctx": lax.rem(z + k, ctx)} for k in range(1, ctx)]
        + [{"dp": d, "fsdp": f} for d, f in others]
    )

    def column_copy(s):
        return remote(x_ref.at[s], xbuf.at[z], send_x.at[s], recv_x.at[z], ctx=core * seqs + s)

    def sibling_copy(s):
        return remote(x_ref.at[s], xbuf.at[z], send_x.at[s], recv_x.at[z], dp=sibling)

    for s in range(seqs):
        keep = core * seqs + s == z

        @pl.when(jnp.logical_not(keep))
        def _():
            column_copy(s).start()

        @pl.when(keep)
        def _():
            sibling_copy(s).start()
            own = pltpu.make_async_copy(x_ref.at[s], xbuf.at[z], local_x)
            own.start()
            own.wait()

    def weight_copy(j, part):
        d, f = others[j - 1]
        columns = pl.multiple_of(part * D + lax.rem(d, 2) * width, 128)
        return remote(
            w_ref.at[:, pl.ds(columns, width)],
            wbuf.at[pl.ds(pl.multiple_of(me * shard_rows, 16), shard_rows), pl.ds(part * width, width)],
            send_w.at[j - 1, part], recv_w.at[j - 1, part], dp=d, fsdp=f,
        )

    def gain_copy(j):
        d, f = others[j - 1]
        return remote(g_ref, gbuf.at[me], send_g.at[j - 1], recv_g.at[j - 1], dp=d, fsdp=f)

    for j in range(1, groups):
        gain_copy(j).start()
        for part in range(3):
            weight_copy(j, part).start()
    own = [pltpu.make_async_copy(g_ref, gbuf.at[me], local_g)]
    for part in range(3):
        columns = pl.multiple_of(part * D + core * width, 128)
        own.append(pltpu.make_async_copy(
            w_ref.at[:, pl.ds(columns, width)],
            wbuf.at[pl.ds(pl.multiple_of(me * shard_rows, 16), shard_rows), pl.ds(part * width, width)],
            local_w.at[part],
        ))
    for copy in own:
        copy.start()
    for copy in own:
        copy.wait()
    for j in range(1, groups):
        gain_copy(j).wait_recv()
        for part in range(3):
            weight_copy(j, part).wait_recv()

    gains = gbuf[0].astype(f32)
    for number in range(1, groups):
        gains = gains + gbuf[number].astype(f32)
    gain_ref[...] = gains
    wt_ref[...] = wbuf[...].T
    attn_gain = gains[0:1, :]
    order = near_order(z, ctx)

    def forward_copy(block):
        return remote(xbuf.at[block], xbuf.at[block], fwd_x.at[block], recv_x.at[block], dp=sibling)

    def turn(number, carry):
        block = order(number)

        @pl.when(jnp.logical_or(jnp.logical_not(lead), number > 0))
        def _():
            forward_copy(block).wait_recv()

        @pl.when(jnp.logical_and(lead, number > 0))
        def _():
            forward_copy(block).start()

        place = pl.ds(pl.multiple_of(block * block_len, 128), block_len)
        normal = layer_norm(xbuf[block].astype(f32), attn_gain)[2].astype(bf16)
        normal_ref[:, place] = normal.T
        cosine, sine = cos_ref[:, place], sin_ref[:, place]
        for part in range(3):
            projected = dot(wt_ref[part * width : (part + 1) * width, :], normal, 1, 1)
            for head in range(heads):
                first = projected[head * HEAD : head * HEAD + HALF, :]
                second = projected[head * HEAD + HALF : (head + 1) * HEAD, :]
                if part < 2:
                    first, second = (
                        first * cosine - second * sine, second * cosine + first * sine
                    )
                if part == 0:
                    first, second = first * score_base2, second * score_base2
                heads_ref[part, head, :HALF, place] = first.astype(bf16)
                heads_ref[part, head, HALF:, place] = second.astype(bf16)
        return carry

    lax.fori_loop(0, ctx, turn, 0)
    half_blocks = ctx // 2
    half_ref[...] = xbuf[pl.ds(core * half_blocks, half_blocks)].reshape(half_ref.shape)

    for s in range(seqs):
        sibling_copy(s).wait_send()
    for number in range(1, ctx):
        @pl.when(lead)
        def _():
            forward_copy(order(number)).wait_send()
    for j in range(1, groups):
        gain_copy(j).wait_send()
        for part in range(3):
            weight_copy(j, part).wait_send()


def prologue(tokens, qkv_weight, gains, cosine, sine, ctx, nfsdp, groups):
    seqs, block_len, _ = tokens.shape
    length = block_len * ctx
    width = D // 2
    shard_rows = qkv_weight.shape[0]
    dma = pltpu.SemaphoreType.DMA
    return pl.pallas_call(
        partial(prologue_kernel, ctx, nfsdp, groups, seqs),
        in_specs=[any_spec, any_spec, any_spec, vmem_spec, vmem_spec],
        out_specs=[vmem_spec] * 5,
        out_shape=[
            jax.ShapeDtypeStruct((3, width // HEAD, HEAD, length), bf16),
            jax.ShapeDtypeStruct((D, length), bf16),
            jax.ShapeDtypeStruct((length // 2, D), bf16),
            jax.ShapeDtypeStruct((3 * width, D), bf16),
            jax.ShapeDtypeStruct(gains.shape, f32),
        ],
        scratch_shapes=[
            pltpu.VMEM((ctx, block_len, D), bf16),
            pltpu.VMEM((groups * shard_rows, 3 * width), bf16),
            pltpu.VMEM((groups,) + gains.shape, bf16),
            dma((seqs,)), dma((ctx,)), dma((ctx,)), dma,
            dma((groups - 1, 3)), dma((groups - 1, 3)), dma((3,)),
            dma((groups - 1,)), dma((groups - 1,)), dma,
        ],
        compiler_params=params(1),
        name="prologue",
        cost_estimate=pl.CostEstimate(
            flops=6 * width * D * length, bytes_accessed=16 * length * D, transcendentals=0
        ),
    )(tokens, qkv_weight, gains, cosine, sine)


def column_partners(ctx):
    dp, core, x, z, y = here()
    found = [{"dp": dp + 1 - 2 * core}]
    for k in range(1, ctx):
        for c in range(2):
            found.append({"dp": 2 * x + c, "ctx": lax.rem(z + k, ctx)})
    return found


def to_halves(ctx, seqs, src, dst, send_sem, recv_sem, local_sem):
    dp, core, x, z, y = here()
    half = ctx // 2
    side, slot = z // half, lax.rem(z, half)

    def outgoing(s):
        return remote(
            src.at[s], dst.at[slot], send_sem.at[s], recv_sem.at[slot],
            dp=2 * x + side, ctx=core * seqs + s,
        )

    def stays(s):
        return jnp.logical_and(core * seqs + s == z, side == core)

    def own(s):
        return pltpu.make_async_copy(src.at[s], dst.at[slot], local_sem)

    def start():
        for s in range(seqs):
            @pl.when(stays(s))
            def _():
                own(s).start()

            @pl.when(jnp.logical_not(stays(s)))
            def _():
                outgoing(s).start()

    def finish():
        for s in range(seqs):
            @pl.when(stays(s))
            def _():
                own(s).wait()

            @pl.when(jnp.logical_not(stays(s)))
            def _():
                outgoing(s).wait_send()
        for i in range(half):
            mine = jnp.logical_and(z // seqs == core, core * half + i == z)

            @pl.when(jnp.logical_not(mine))
            def _():
                remote(
                    src.at[0], dst.at[i], send_sem.at[0], recv_sem.at[i], dp=dp
                ).wait_recv()

    return start, finish


def to_blocks(ctx, seqs, parts, src, dst, send_sem, recv_sem, local_sem):
    dp, core, x, z, y = here()
    half = ctx // 2
    side, slot = z // seqs, lax.rem(z, seqs)
    size = src.shape[1] // parts

    def outgoing(i, part):
        rows = slice(part * size, (part + 1) * size)
        return remote(
            src.at[i, rows], dst.at[slot, rows], send_sem.at[i, part], recv_sem.at[slot, part],
            dp=2 * x + side, ctx=core * half + i,
        )

    def stays(i):
        return jnp.logical_and(core * half + i == z, side == core)

    def own(i, part):
        rows = slice(part * size, (part + 1) * size)
        return pltpu.make_async_copy(src.at[i, rows], dst.at[slot, rows], local_sem.at[part])

    def start_one(i, part):
        @pl.when(stays(i))
        def _():
            own(i, part).start()

        @pl.when(jnp.logical_not(stays(i)))
        def _():
            outgoing(i, part).start()

    def finish():
        for part in range(parts):
            rows = slice(part * size, (part + 1) * size)
            for i in range(half):
                @pl.when(stays(i))
                def _():
                    own(i, part).wait()

                @pl.when(jnp.logical_not(stays(i)))
                def _():
                    outgoing(i, part).wait_send()
            for s in range(seqs):
                mine = jnp.logical_and(z // half == core, core * seqs + s == z)

                @pl.when(jnp.logical_not(mine))
                def _():
                    remote(
                        src.at[0, rows], dst.at[s, rows], send_sem.at[0, part],
                        recv_sem.at[s, part], dp=dp,
                    ).wait_recv()

    return start_one, finish


def block_sems(ctx, seqs, parts):
    dma = pltpu.SemaphoreType.DMA
    return [dma((ctx // 2, parts)), dma((seqs, parts)), dma((parts,))]


def attend_kernel(
    ctx, seqs, nfsdp, groups,
    q_ref, k_ref, v_ref, cot_ref, up_ref, o_ref, log_ref, all_ref, half_ref, whole_ref,
    k_rows, v_wide, done,
    send_c, recv_c, local_c, send_o, recv_o, local_o, send_u, recv_u, send_f, recv_f, local_u,
):
    head, step = pl.program_id(0), pl.program_id(1)
    heads, steps = pl.num_programs(0), pl.num_programs(1)
    dp, core, x, z, y = here()
    sibling = dp + 1 - 2 * core
    length = k_ref.shape[-1]
    chunk = chunk_of(length, 128)
    block = q_ref.shape[-1]
    half = length // 2
    start, finish = to_halves(ctx, seqs, cot_ref, half_ref, send_c, recv_c, local_c)
    mine, others = chips_of(nfsdp, groups)
    shard_rows = up_ref.shape[0]

    def rows_of(group):
        return pl.ds(pl.multiple_of(group * shard_rows, 16), shard_rows)

    own_rows = rows_of(dp * nfsdp + y)
    own_shard = pltpu.make_async_copy(up_ref, whole_ref.at[own_rows], local_u)
    shard_copies = [
        remote(up_ref, whole_ref.at[own_rows], send_u.at[j], recv_u.at[j], dp=2 * cx + core, fsdp=cy)
        for j, (_, cx, cy) in enumerate(others)
    ]
    twin_copy = remote(
        up_ref, whole_ref.at[own_rows], send_u.at[len(others)], recv_u.at[len(others)], dp=sibling
    )
    passed_on = []
    for j in range(len(others)):
        source = lax.rem(mine + len(others) - j, groups // 2)
        got = whole_ref.at[rows_of((2 * (source // nfsdp) + core) * nfsdp + lax.rem(source, nfsdp))]
        passed_on.append(remote(got, got, send_f.at[j], recv_f.at[j], dp=sibling))

    @pl.when(jnp.logical_and(head == 0, step == 0))
    def _():
        greet(column_partners(ctx) + plane_partners(nfsdp, groups))
        for each in shard_copies:
            each.start()
        start()
        own_shard.start()
        twin_copy.start()

    @pl.when(step == 0)
    def _():
        k_rows[...] = k_ref[0, 0].T
        v_wide[:HEAD, :] = v_ref[0, 0]
        v_wide[HEAD:, :] = jnp.ones((v_wide.shape[0] - HEAD, length), bf16)

    query = q_ref[0, 0]
    highest = None
    total = None
    coming = dot(k_rows[:chunk, :], query)
    for first in range(0, length, chunk):
        scores = coming
        after = first + chunk
        if after < length:
            coming = dot(k_rows[after : after + chunk, :], query)
        top = jnp.max(scores, 0, keepdims=True)
        new_high = top if highest is None else jnp.maximum(highest, top)
        weights = jnp.exp2(scores - new_high).astype(bf16)
        term = dot(v_wide[:, first:after], weights)
        total = term if total is None else total * jnp.exp2(highest - new_high) + term
        highest = new_high
    denominator = total[HEAD : HEAD + 1, :]
    result = (total[:HEAD, :] / denominator).astype(bf16)
    o_ref[0] = result
    done[head, :, pl.ds(pl.multiple_of(step * block, 128), block)] = result
    log_ref[0] = highest + jnp.log2(denominator)

    def own_copy(number):
        return pltpu.make_async_copy(
            done.at[number, :, pl.ds(pl.multiple_of(core * half, 128), half)],
            all_ref.at[core * heads + number], local_o.at[number],
        )

    def sibling_copy(number):
        return remote(
            done.at[number, :, pl.ds(pl.multiple_of((1 - core) * half, 128), half)],
            all_ref.at[core * heads + number], send_o.at[number], recv_o.at[number], dp=sibling,
        )

    @pl.when(step == steps - 1)
    def _():
        own_copy(head).start()
        sibling_copy(head).start()

    @pl.when(jnp.logical_and(head == heads - 1, step == steps - 1))
    def _():
        for each, further in zip(shard_copies, passed_on):
            each.wait()
            further.start()

        def settle(number, carry):
            own_copy(number).wait()
            sibling_copy(number).wait()
            return carry
        lax.fori_loop(0, heads, settle, 0)
        own_shard.wait()
        twin_copy.wait()
        for further in passed_on:
            further.wait()
        finish()


def attend_chip(heads_t, cotangent, up_weight, ctx, nfsdp, groups):
    _, count, _, length = heads_t.shape
    seqs, block_len, _ = cotangent.shape
    block = length
    dma = pltpu.SemaphoreType.DMA
    return pl.pallas_call(
        partial(attend_kernel, ctx, seqs, nfsdp, groups),
        grid=(count, length // block),
        in_specs=[
            pl.BlockSpec((1, 1, HEAD, block), lambda h, c: (0, h, 0, c)),
            pl.BlockSpec((1, 1, HEAD, length), lambda h, c: (1, h, 0, 0)),
            pl.BlockSpec((1, 1, HEAD, length), lambda h, c: (2, h, 0, 0)),
            any_spec,
            any_spec,
        ],
        out_specs=[
            pl.BlockSpec((1, HEAD, block), lambda h, c: (h, 0, c)),
            pl.BlockSpec((1, 1, block), lambda h, c: (h, 0, c)),
            any_spec,
            any_spec,
            any_spec,
        ],
        out_shape=[
            jax.ShapeDtypeStruct((count, HEAD, length), bf16),
            jax.ShapeDtypeStruct((count, 1, length), f32),
            jax.ShapeDtypeStruct((2 * count, HEAD, length // 2), bf16),
            jax.ShapeDtypeStruct((ctx // 2, block_len, D), bf16),
            jax.ShapeDtypeStruct((groups * up_weight.shape[0], up_weight.shape[1]), bf16),
        ],
        scratch_shapes=[
            pltpu.VMEM((length, HEAD), bf16),
            pltpu.VMEM((HEAD + 16, length), bf16),
            pltpu.VMEM((count, HEAD, length), bf16),
            dma((seqs,)), dma((ctx // 2,)), dma,
            dma((count,)), dma((count,)), dma((count,)),
            dma((groups // 2,)), dma((groups // 2,)),
            dma((groups // 2 - 1,)), dma((groups // 2 - 1,)), dma,
        ],
        compiler_params=params(2),
        name="attend",
        cost_estimate=pl.CostEstimate(
            flops=16 * count * length * length * HEAD,
            bytes_accessed=10 * count * length * HEAD,
            transcendentals=count * length * length,
        ),
    )(heads_t, heads_t, heads_t, cotangent, up_weight)


def ffn_kernel(
    ctx, seqs, nfsdp, groups, x_ref, att_ref, cot_ref, out_w, up_w, down_w, gain_ref,
    output_ref, rgrad_ref, agrad_ref, shard_ref, first_ref,
    normal_t, hidden_t, widened, low, cot_all, att_all, agrad, packed, twin, first_out,
    send_sem, recv_sem, local_sem, send_t, recv_t, *block_signals,
):
    step, steps = pl.program_id(0), pl.num_programs(0)
    dp, core, x, z, y = here()
    sibling = dp + 1 - 2 * core
    block = x_ref.shape[0]
    half = block * steps
    ff = down_w.shape[0]
    model = x_ref.shape[1]

    blocks = ctx // 2
    start_one, finish = to_blocks(ctx, seqs, 1, first_out, first_ref, *block_signals)

    @pl.when(step == 0)
    def _():
        greet(column_partners(ctx))

    row_block = lax.rem(step, blocks) * (steps // blocks) + step // blocks
    place = pl.ds(pl.multiple_of(row_block * block, 128), block)
    attended = att_ref[...]
    upstream = cot_ref[...]
    gain = gain_ref[1:2, :]
    residual = x_ref[...].astype(f32) + dot(attended.T, out_w[...])
    normed, inverse, scaled = layer_norm(residual, gain)
    normal = scaled.astype(bf16)
    wide = dot(normal, up_w[...])
    inputs, gating = wide[:, :ff], wide[:, ff:]
    phi_sum = 0.5 + 0.5 * lax.erf(inputs * math.sqrt(0.5))
    density = jnp.exp2(inputs * inputs * (-0.5 * math.log2(math.e))) * (1.0 / math.sqrt(2.0 * math.pi))
    gelu = inputs * phi_sum
    hidden = (gelu * gating).astype(bf16)
    result = (residual + dot(hidden, down_w[...])).astype(bf16)
    output_ref[0] = result
    for number in range(blocks):
        @pl.when(step == number)
        def _():
            first_out[number] = result
            start_one(number, 0)

    hidden_grad = dot(upstream, down_w[...], 1, 1)
    input_grad = (hidden_grad * gating * (phi_sum + inputs * density)).astype(bf16)
    gating_grad = (hidden_grad * gelu).astype(bf16)
    widened[place, :ff] = input_grad
    widened[place, ff:] = gating_grad
    normal_grad = dot(input_grad, up_w[:, :ff], 1, 1) + dot(gating_grad, up_w[:, ff:], 1, 1)
    residual_grad = upstream.astype(f32) + norm_back(normal_grad, normed, inverse, gain)
    rgrad_ref[...] = residual_grad
    residual_low = residual_grad.astype(bf16)
    agrad[:, place] = dot(out_w[...], residual_low, 1, 1).astype(bf16)
    normal_t[:, place] = normal.T
    hidden_t[:, place] = hidden.T
    low[place, :] = residual_low
    cot_all[place, :] = upstream
    att_all[:, place] = attended

    def agrad_copies():
        width = agrad.shape[0] // 2
        mine = pl.ds(pl.multiple_of(core * half, 128), half)
        return (
            pltpu.make_async_copy(
                agrad.at[pl.ds(pl.multiple_of(core * width, 16), width), :],
                agrad_ref.at[:, mine], local_sem,
            ),
            remote(
                agrad.at[pl.ds(pl.multiple_of((1 - core) * width, 16), width), :],
                agrad_ref.at[:, mine], send_sem, recv_sem, dp=sibling,
            ),
        )

    @pl.when(step == steps - 1)
    def _():
        for copy in agrad_copies():
            copy.start()
        chips = groups // 2
        pieces = [
            (normal_t, widened.at[:, pl.ds(first, model)]) for first in range(0, 2 * ff, model)
        ]
        pieces += [(att_all, low), (hidden_t, cot_all)]
        spans = []
        offset = 0

        def group_of(chip, c):
            return (2 * (chip // nfsdp) + c) * nfsdp + chip % nfsdp

        def twin_copy(number, chip):
            rows = spans[number]
            return remote(
                packed.at[group_of(chip, 0) + (1 - core) * nfsdp, rows], twin.at[chip, rows],
                send_t.at[number, chip], recv_t.at[number, chip], dp=sibling,
            )

        for number, (left, right) in enumerate(pieces):
            grad = dot(left[...], right[...])
            rows = grad.shape[0] // groups
            spans.append(slice(offset, offset + rows))
            packed[:, spans[-1], :] = grad.astype(bf16).reshape(groups, rows, model)
            offset += rows
            for chip in range(chips):
                twin_copy(number, chip).start()
        for number, rows in enumerate(spans):
            for chip in range(chips):
                twin_copy(number, chip).wait()
                mine = packed[group_of(chip, 0) + core * nfsdp, rows].astype(f32)
                shard_ref[chip, rows] = (mine + twin[chip, rows].astype(f32)).astype(bf16)
        for copy in agrad_copies():
            copy.wait()
        finish()


def feed_forward(x, attended, cotangent, out_w, up_w, down_w, gains, nfsdp, groups, ctx, seqs):
    half = x.shape[0]
    ff = down_w.shape[0]
    blocks = ctx // 2
    block = half // blocks // 2
    chips, pieces = groups // 2, 2 * ff // D + 2
    rows = (2 * ff // D * D + ff + D) // groups
    dma = pltpu.SemaphoreType.DMA

    def whole(array):
        return pl.BlockSpec(array.shape, lambda i: (0,) * array.ndim, pipeline_mode=pl.Buffered(1))

    def turned(i):
        return i % blocks * 2 + i // blocks

    by_rows = pl.BlockSpec((block, D), lambda i: (turned(i), 0))
    return pl.pallas_call(
        partial(ffn_kernel, ctx, seqs, nfsdp, groups),
        grid=(half // block,),
        in_specs=[
            by_rows,
            pl.BlockSpec((D, block), lambda i: (0, turned(i))),
            by_rows,
            whole(out_w), whole(up_w), whole(down_w), whole(gains),
        ],
        out_specs=[
            pl.BlockSpec((1, block, D), lambda i: (jnp.maximum(i - blocks, 0), 0, 0)),
            by_rows,
            any_spec,
            vmem_spec,
            any_spec,
        ],
        out_shape=[
            jax.ShapeDtypeStruct((blocks, block, D), bf16),
            jax.ShapeDtypeStruct((half, D), f32),
            jax.ShapeDtypeStruct((D // 2, 2 * half), bf16),
            jax.ShapeDtypeStruct((chips, rows, D), bf16),
            jax.ShapeDtypeStruct((seqs, block, D), bf16),
        ],
        scratch_shapes=[
            pltpu.VMEM((D, half), bf16),
            pltpu.VMEM((ff, half), bf16),
            pltpu.VMEM((half, 2 * ff), bf16),
            pltpu.VMEM((half, D), bf16),
            pltpu.VMEM((half, D), bf16),
            pltpu.VMEM((D, half), bf16),
            pltpu.VMEM((D, half), bf16),
            pltpu.VMEM((groups, rows, D), bf16),
            pltpu.VMEM((chips, rows, D), bf16),
            pltpu.VMEM((blocks, block, D), bf16),
            dma, dma, dma, dma((pieces, chips)), dma((pieces, chips)),
            *block_sems(ctx, seqs, 1),
        ],
        compiler_params=params(3),
        name="feed_forward",
        cost_estimate=pl.CostEstimate(
            flops=6 * half * D * (3 * ff + D), bytes_accessed=32 << 20,
            transcendentals=2 * half * ff,
        ),
    )(x, attended, cotangent, out_w, up_w, down_w, gains)


def chips_of(nfsdp, groups):
    dp, core, x, z, y = here()
    chips = groups // 2
    mine = x * nfsdp + y
    found = []
    for j in range(1, chips):
        other = lax.rem(mine + j, chips)
        found.append((other, other // nfsdp, lax.rem(other, nfsdp)))
    return mine, found


def plane_partners(nfsdp, groups):
    dp, core, x, z, y = here()
    return [
        {"dp": 2 * cx + c, "fsdp": cy}
        for _, cx, cy in chips_of(nfsdp, groups)[1] for c in range(2)
    ]


def z_sum(ctx, sent, got, final, sems):
    z = lax.axis_index("ctx")
    send_a, recv_a, send_b, recv_b = sems

    def piece(k):
        to = lax.rem(z + k, ctx)
        return remote(sent.at[to], got.at[k - 1], send_a.at[k - 1], recv_a.at[k - 1], ctx=to)

    def result(k):
        to = lax.rem(z + k, ctx)
        return remote(final.at[z], final.at[z], send_b.at[k - 1], recv_b.at[k - 1], ctx=to)

    def start():
        for k in range(1, ctx):
            piece(k).start()

    def middle():
        for k in range(1, ctx):
            piece(k).wait()
        total = sent[z].astype(f32)
        for k in range(1, ctx):
            total = total + got[k - 1].astype(f32)
        final[z] = total.astype(bf16)
        for k in range(1, ctx):
            result(k).start()

    def finish():
        for k in range(1, ctx):
            result(k).wait()

    return start, middle, finish


def z_sems(ctx):
    return [pltpu.SemaphoreType.DMA((ctx - 1,))] * 4


def column_sum(ctx, nfsdp, groups, src, got, zsent, zgot, final, sems):
    dp, core, x, z, y = here()
    mine, others = chips_of(nfsdp, groups)
    send_q, recv_q = sems[:2]
    z_start, z_middle, z_finish = z_sum(ctx, zsent, zgot, final, sems[2:])
    places = [(x, y)] + [(cx, cy) for _, cx, cy in others]
    chips = len(places)

    def copy(j, way):
        cx, cy = places[j]
        c = core if way == 0 else 1 - core
        return remote(
            src.at[(2 * cx + c) * nfsdp + cy], got.at[way, j],
            send_q.at[way, j], recv_q.at[way, j], dp=2 * cx + c, fsdp=cy,
        )

    pairs = [(j, way) for way in range(2) for j in range(chips) if (j, way) != (0, 0)]

    def send():
        for pair in pairs:
            copy(*pair).start()

    def plane():
        for pair in pairs:
            copy(*pair).wait()
        rows, columns = src.shape[1], src.shape[2]
        per = ctx // 2
        for way in range(2):
            owner = core if way == 0 else 1 - core
            total = (src[dp * nfsdp + y] if way == 0 else got[1, 0]).astype(f32)
            for j in range(1, chips):
                total = total + got[way, j].astype(f32)
            zsent[pl.ds(owner * per, per)] = total.astype(bf16).reshape(per, rows // per, columns)
        z_start()

    return send, plane, z_middle, z_finish


def column_scratch(ctx, groups, rows, columns):
    chips, per = groups // 2, 2 * rows // ctx
    dma = pltpu.SemaphoreType.DMA
    buffers = [
        pltpu.VMEM((2, chips, rows, columns), bf16),
        pltpu.VMEM((ctx, per, columns), bf16),
        pltpu.VMEM((ctx - 1, per, columns), bf16),
        pltpu.VMEM((ctx, per, columns), bf16),
    ]
    return buffers, [dma((2, chips))] * 2 + z_sems(ctx)


def plane_sum(ctx, nfsdp, groups, spans, own, got, zsent, zgot, final, sems):
    dp, core, x, z, y = here()
    mine, others = chips_of(nfsdp, groups)
    send_q, recv_q = sems[:2]
    per = zsent.shape[2]
    z_stages = [
        z_sum(
            ctx, zsent.at[n], zgot.at[n], final.at[n],
            [sems[k].at[n] for k in range(2, 6)],
        )
        for n in range(len(spans))
    ]

    def copy(number, j):
        chip, cx, cy = others[j]
        rows = spans[number]
        return remote(
            own.at[chip, rows], got.at[j, rows], send_q.at[number, j], recv_q.at[number, j],
            dp=2 * cx + core, fsdp=cy,
        )

    def begin(number):
        for j in range(len(others)):
            copy(number, j).start()

    def plane(number):
        rows = spans[number]
        for j in range(len(others)):
            copy(number, j).wait()
        total = own[mine, rows].astype(f32)
        for j in range(len(others)):
            total = total + got[j, rows].astype(f32)
        low = total.astype(bf16)
        count = low.shape[0]
        for k in range(ctx):
            first, last = min(k * per, count), min((k + 1) * per, count)
            if last > first:
                zsent[number, k, : last - first, :] = low[first:last, :]
            if last - first < per:
                zsent[number, k, last - first :, :] = jnp.zeros(
                    (per - last + first, low.shape[1]), bf16
                )
        z_stages[number][0]()

    def middle(number):
        z_stages[number][1]()

    def finish():
        for stage in z_stages:
            stage[2]()

    return begin, plane, middle, finish


def plane_scratch(ctx, groups, spans):
    chips, count = groups // 2, len(spans)
    most = max(span.stop - span.start for span in spans)
    per = -(-most // (16 * ctx)) * 16
    dma = pltpu.SemaphoreType.DMA
    buffers = [
        pltpu.VMEM((chips - 1, spans[-1].stop, D), bf16),
        pltpu.VMEM((count, ctx, per, D), bf16),
        pltpu.VMEM((count, ctx - 1, per, D), bf16),
        pltpu.VMEM((count, ctx, per, D), bf16),
    ]
    return buffers, [dma((count, chips - 1))] * 2 + [dma((count, ctx - 1))] * 4


def attend_back_kernel(
    ctx, nfsdp, groups, seqs, spans, parts,
    q_ref, k_ref, v_ref, o_ref, up_ref, log_ref, cos_all, sin_all, cos_ref, sin_ref,
    normal_ref, shard_ref, out_ref, wt_ref, x_ref, rgrad_ref, gain_ref,
    sums_ref, qkv_ref, output_ref, token_ref,
    q_rows, up_rows, up_cols, delta, dq_sum, dproj, pair_proj, fresh,
    dn_send, dn_recv, tg_send, *scratch,
):
    head, step = pl.program_id(0), pl.program_id(1)
    heads, steps = pl.num_programs(0), pl.num_programs(1)
    dp, core, x, z, y = here()
    sibling = dp + 1 - 2 * core
    length = q_ref.shape[-1]
    rows = k_ref.shape[-1]
    chunk = chunk_of(length, 256)
    pairs = fresh.shape[0]
    total_steps = pairs * 2 * (length // rows)
    last = total_steps - 1
    now = head * steps + step

    def take(count):
        nonlocal scratch
        taken, scratch = scratch[:count], scratch[count:]
        return taken

    send_n, recv_n = take(2)
    begin, plane, middle, plane_finish = plane_sum(
        ctx, nfsdp, groups, spans, shard_ref, *(bufs := take(4)), take(6)
    )
    out_start, out_finish = to_blocks(ctx, seqs, 1, out_ref, output_ref, *take(3))
    token_start, token_finish = to_blocks(ctx, seqs, parts, tg_send, token_ref, *take(3))
    columns, finals = [], []
    for p in range(pairs):
        column_bufs = take(4)
        finals.append(column_bufs[3])
        columns.append(column_sum(
            ctx, nfsdp, groups, fresh.at[p], *column_bufs, take(6)
        ))

    @pl.when(now == 0)
    def _():
        greet(column_partners(ctx) + plane_partners(nfsdp, groups))
        begin(0)
        for i in range(ctx // 2):
            out_start(i, 0)

    @pl.when(step == 0)
    def _():
        q_rows[...] = q_ref[0, 0].T
        upstream = up_ref[0]
        up_cols[...] = upstream
        up_rows[...] = upstream.T
        delta[...] = jnp.sum(
            upstream.astype(f32) * o_ref[0].astype(f32), 0, keepdims=True
        )
        dq_sum[...] = jnp.zeros_like(dq_sum)

    key_t = k_ref[0, 0]
    key = key_t.T
    value = v_ref[0, 0].T
    dk = None
    dv = None
    for start in range(0, length, chunk):
        place = slice(start, start + chunk)
        scores = dot(key, q_ref[0, 0, :, place])
        weights = jnp.exp2(scores - log_ref[0, :, place])
        weight_grad = dot(value, up_cols[:, place])
        score_grad = (weights * (weight_grad - delta[:, place])).astype(bf16)
        dv_term = dot(weights.astype(bf16), up_rows[place, :])
        dk_term = dot(score_grad, q_rows[place, :])
        dv = dv_term if dv is None else dv + dv_term
        dk = dk_term if dk is None else dk + dk_term
        dq_sum[:, place] += dot(key_t, score_grad)
    block = pl.ds(pl.multiple_of(step * rows, 128), rows)
    upper, lower = rope_back((dk * math.log(2.0)).T, cos_ref[...], sin_ref[...])
    dproj[1, head, :HALF, block] = upper.astype(bf16)
    dproj[1, head, HALF:, block] = lower.astype(bf16)
    dproj[2, head, :, block] = dv.T.astype(bf16)

    @pl.when(step == steps - 1)
    def _():
        upper, lower = rope_back(dq_sum[...] * score_scale, cos_all[...], sin_all[...])
        dproj[0, head, :HALF, :] = upper.astype(bf16)
        dproj[0, head, HALF:, :] = lower.astype(bf16)
        for part in range(3):
            first = pl.multiple_of(part * 2 * HEAD + lax.rem(head, 2) * HEAD, HEAD)
            pair_proj[pl.ds(first, HEAD), :] = dproj[part, head]

    @pl.when(jnp.logical_and(step == steps - 1, lax.rem(head, 2) == 1))
    def _():
        grad = dot(normal_ref[...], pair_proj[...], 1, 1).astype(bf16)
        fresh[head // 2] = grad.reshape(fresh.shape[1:])

    events = {}

    def at(turn, what, *args):
        events.setdefault(total_steps * turn // 12, []).append(partial(what, *args))

    count = len(spans)
    for number in range(1, count):
        at(number * 5 // count, begin, number)
    for number in range(count):
        at(2 + 6 * number // count, plane, number)
    for number in range(count):
        at(5 + 6 * number // count, middle, number)
    for p in range(pairs - 1):
        done = 12 * (p + 1) // pairs - 1
        for number, what in enumerate(columns[p][:3]):
            at(min(done + (0, 3 - (p > 0), 5 - 2 * (p > 0))[number], 10), what)
    for when, things in sorted(events.items()):
        @pl.when(now == when)
        def _():
            for thing in things:
                thing()

    half = x_ref.shape[0]
    blocks = tg_send.shape[0]
    block_len = half // blocks
    size = block_len // parts

    def dn_rows(first):
        place = pl.ds(pl.multiple_of(first, 128), size)
        grads = dproj[:, :, :, place].reshape(wt_ref.shape[0], size)
        return dot(grads, wt_ref[...], 0, 0)

    def sibling_copy(number):
        return remote(
            dn_send.at[number], dn_recv.at[number], send_n.at[number], recv_n.at[number],
            dp=sibling,
        )

    def sibling_part(number):
        dn_send[number] = dn_rows((1 - core) * half + number * size).astype(bf16)
        sibling_copy(number).start()

    def own_part(number):
        first = number * size
        place = slice(first, first + size)
        gain = gain_ref[0:1, :]
        grad = dn_rows(core * half + first)
        sibling_copy(number).wait()
        grad = grad + dn_recv[number].astype(f32)
        normed, inverse, _ = layer_norm(x_ref[place, :].astype(f32), gain)
        token = rgrad_ref[place, :] + norm_back(grad, normed, inverse, gain)
        i, part = number // parts, number % parts
        tg_send[i, part * size : (part + 1) * size, :] = token.astype(bf16)
        token_start(i, part)

    @pl.when(now == last)
    def _():
        ending = columns[pairs - 1]
        ending[0]()
        parts_all = blocks * parts
        for number in range(parts_all + 1):
            if number < parts_all:
                sibling_part(number)
            if number > 0:
                own_part(number - 1)
        ending[1]()
        ending[2]()
        out_finish()
        plane_finish()
        sums_ref[...] = bufs[3][...]
        for p in range(pairs):
            columns[p][3]()
            qkv_ref[p] = finals[p][...]
        token_finish()


def attend_back_chip(
    heads_t, attended, upstream, log_total, cosine, sine, normal_t, shards, spans, output,
    wt, x, rgrad, gains, ctx, nfsdp, groups, seqs,
):
    _, count, _, length = heads_t.shape
    rows = chunk_of(length, 1024)
    pairs = count // 2
    half = length // 2
    block_len = length // ctx
    parts = 2 if block_len % 256 == 0 else 1
    size = block_len // parts
    shard_rows = normal_t.shape[0] // groups
    plane_bufs, plane_signals = plane_scratch(ctx, groups, spans)
    column_bufs, column_signals = column_scratch(ctx, groups, shard_rows, 6 * HEAD)
    full = pl.BlockSpec((1, HEAD, length), lambda h, k: (h, 0, 0))
    table = pl.BlockSpec((HALF, length), lambda h, k: (0, 0), pipeline_mode=pl.Buffered(1))
    table_part = pl.BlockSpec((HALF, rows), lambda h, k: (0, k))
    dma = pltpu.SemaphoreType.DMA

    def whole(array):
        return pl.BlockSpec(
            array.shape, lambda h, k: (0,) * array.ndim, pipeline_mode=pl.Buffered(1)
        )

    return pl.pallas_call(
        partial(attend_back_kernel, ctx, nfsdp, groups, seqs, spans, parts),
        grid=(count, length // rows),
        in_specs=[
            pl.BlockSpec((1, 1, HEAD, length), lambda h, k: (0, h, 0, 0)),
            pl.BlockSpec((1, 1, HEAD, rows), lambda h, k: (1, h, 0, k)),
            pl.BlockSpec((1, 1, HEAD, rows), lambda h, k: (2, h, 0, k)),
            full,
            full,
            pl.BlockSpec((1, 1, length), lambda h, k: (h, 0, 0)),
            table,
            table,
            table_part,
            table_part,
            whole(normal_t), whole(shards), any_spec, whole(wt), whole(x), whole(rgrad),
            whole(gains),
        ],
        out_specs=[vmem_spec, vmem_spec, any_spec, any_spec],
        out_shape=[
            jax.ShapeDtypeStruct(plane_bufs[3].shape, bf16),
            jax.ShapeDtypeStruct((pairs, ctx, 2 * shard_rows // ctx, 6 * HEAD), bf16),
            jax.ShapeDtypeStruct((seqs,) + output.shape[1:], bf16),
            jax.ShapeDtypeStruct((seqs, block_len, D), bf16),
        ],
        scratch_shapes=[
            pltpu.VMEM((length, HEAD), bf16),
            pltpu.VMEM((length, HEAD), bf16),
            pltpu.VMEM((HEAD, length), bf16),
            pltpu.VMEM((1, length), f32),
            pltpu.VMEM((HEAD, length), f32),
            pltpu.VMEM((3, count, HEAD, length), bf16),
            pltpu.VMEM((6 * HEAD, length), bf16),
            pltpu.VMEM((pairs, groups, shard_rows, 6 * HEAD), bf16),
            pltpu.VMEM((half // size, size, D), bf16),
            pltpu.VMEM((half // size, size, D), bf16),
            pltpu.VMEM((ctx // 2, block_len, D), bf16),
            dma((half // size,)), dma((half // size,)),
            *plane_bufs, *plane_signals,
            *block_sems(ctx, seqs, 1), *block_sems(ctx, seqs, parts),
            *(column_bufs + column_signals) * pairs,
        ],
        compiler_params=params(4),
        name="attend_back",
        cost_estimate=pl.CostEstimate(
            flops=40 * count * length * length * HEAD,
            bytes_accessed=16 * count * length * HEAD,
            transcendentals=count * length * length,
        ),
    )(
        heads_t, heads_t, heads_t, attended, upstream, log_total,
        cosine, sine, cosine, sine, normal_t, shards, output, wt, x, rgrad, gains,
    )


def chip_body(
    tokens,
    cotangent,
    qkv_weight,
    out_weight,
    up_weight,
    down_weight,
    attention_gain,
    feedforward_gain,
):
    ctx, nfsdp = lax.axis_size("ctx"), lax.axis_size("fsdp")
    groups = lax.axis_size("dp") * nfsdp
    seqs, block_len, _ = tokens.shape
    length = block_len * ctx
    width = D // 2
    shard_rows = qkv_weight.shape[0]
    me = lax.axis_index("dp") * nfsdp + lax.axis_index("fsdp")
    gain_rows = lax.dynamic_update_slice(
        jnp.zeros((16, D), bf16), jnp.stack([attention_gain, feedforward_gain]),
        (0, me * shard_rows),
    )
    frequency = np.float32(rope_base) ** (np.arange(HALF, dtype=np.float32) * np.float32(-2 / HEAD))
    angles = frequency[:, None] * np.arange(length, dtype=np.float32)[None, :]
    cosine, sine = jnp.asarray(np.cos(angles)), jnp.asarray(np.sin(angles))
    out_whole = gather_rows(out_weight)
    down_whole = gather_rows(down_weight)
    heads_t, normal_t, x_half, wt, gains = prologue(
        tokens, qkv_weight, gain_rows, cosine, sine, ctx, nfsdp, groups
    )
    attended, log_total, att_all, cot_half, up_whole = attend_chip(
        heads_t, cotangent, up_weight, ctx, nfsdp, groups
    )
    output, rgrad, agrad, shards, first_rows = feed_forward(
        x_half, att_all.reshape(D, length // 2), cot_half.reshape(length // 2, D),
        out_whole, up_whole, down_whole, gains, nfsdp, groups, ctx, seqs,
    )
    up_parts = up_weight.shape[1] // D
    rows = [shard_rows] * (up_parts - 1) + [
        shard_rows + out_weight.shape[0], down_weight.shape[0]
    ]
    if up_parts == 3:
        rows = [2 * shard_rows] + rows[2:]
    spans, first = [], 0
    for count in rows:
        spans.append(slice(first, first + count))
        first += count
    sums, pieces, last_rows, token_low = attend_back_chip(
        heads_t, attended, agrad.reshape(width // HEAD, HEAD, length), log_total,
        cosine, sine, normal_t, shards, spans, output,
        wt, x_half, rgrad, gains, ctx, nfsdp, groups, seqs,
    )

    shard = [
        sums[n].reshape(-1, D)[: span.stop - span.start].astype(f32)
        for n, span in enumerate(spans)
    ]
    shard = jnp.concatenate(shard, 0)
    cuts = [shard[i * shard_rows : (i + 1) * shard_rows] for i in range(up_parts)]
    up_shard = jnp.concatenate(cuts, -1)
    offset = up_parts * shard_rows
    out_shard = shard[offset : offset + out_weight.shape[0]]
    down_shard = shard[offset + out_weight.shape[0] :]
    pieces = pieces.reshape(-1, 2, shard_rows, 3, 2 * HEAD)
    qkv_shard = jnp.transpose(pieces, (2, 3, 1, 0, 4)).reshape(shard_rows, 3 * D).astype(f32)
    attn_gain_grad = jnp.sum(qkv_weight.astype(f32) * qkv_shard, -1) / attention_gain.astype(f32)
    ffn_gain_grad = jnp.sum(up_weight.astype(f32) * up_shard, -1) / feedforward_gain.astype(f32)
    output = jnp.concatenate([first_rows, last_rows], 1)
    return (
        output,
        token_low.astype(f32),
        qkv_shard,
        out_shard,
        up_shard,
        down_shard,
        attn_gain_grad,
        ffn_gain_grad,
    )


def body(tokens, cotangent, qkv_weight, *others):
    ctx, dp = lax.axis_size("ctx"), lax.axis_size("dp")
    one_each = ctx == 2 * tokens.shape[0] and dp % 2 == 0 and ctx & (ctx - 1) == 0 and HEADS % 4 == 0
    aligned = tokens.shape[1] % 256 == 0 and 2 * qkv_weight.shape[0] % (16 * ctx) == 0
    chosen = chip_body if one_each and aligned else general_body
    return chosen(tokens, cotangent, qkv_weight, *others)


def solution(mesh):
    rows = P(("dp", "fsdp"), "ctx", None)
    weight = P(("dp", "fsdp"), None)
    gain = P(("dp", "fsdp"))
    return jax.shard_map(
        body,
        mesh=mesh,
        in_specs=(rows, rows, weight, weight, weight, weight, gain, gain),
        out_specs=(rows, rows, weight, weight, weight, weight, gain, gain),
        check_vma=False,
    )
```

```python
from functools import partial
import math

import jax
import jax.numpy as jnp
import numpy as np
from jax import lax
from jax.experimental import pallas as pl
from jax.experimental.pallas import tpu as pltpu
from jax.sharding import PartitionSpec as P

D = 768
HEADS = 12
HEAD = 64
FF = 1152
HALF = HEAD // 2

norm_eps = 1e-05
rope_base = 160000.0
score_scale = HEAD ** (-0.5)
score_base2 = score_scale * math.log2(math.e)
WEIGHT_AXES = ("dp", "fsdp")
f32 = jnp.float32
bf16 = jnp.bfloat16


def dot(left, right, left_dim=1, right_dim=0):
    return lax.dot_general(
        left, right, (((left_dim,), (right_dim,)), ((), ())), preferred_element_type=f32
    )


def layer_norm(values, norm_gain):
    centre = jnp.mean(values, -1, keepdims=True)
    centred = values - centre
    inverse = lax.rsqrt(jnp.mean(centred * centred, -1, keepdims=True) + norm_eps)
    normed = centred * inverse
    return (normed, inverse, normed * norm_gain)


def norm_back(upstream, normed, inverse, norm_gain):
    scaled = upstream * norm_gain
    return (
        scaled
        - jnp.mean(scaled, -1, keepdims=True)
        - normed * jnp.mean(scaled * normed, -1, keepdims=True)
    ) * inverse


def gated_gelu(inputs, gating):
    return jax.nn.gelu(inputs, approximate=False) * gating


def rope_rows(length):
    frequency = rope_base ** (-2.0 * jnp.arange(HALF, dtype=f32) / HEAD)
    angles = frequency[:, None] * jnp.arange(length, dtype=jnp.int32).astype(f32)[None, :]
    return (jnp.cos(angles), jnp.sin(angles))


def chunk_of(length, most):
    return most if length % most == 0 else length


def forward_kernel(q_ref, k_ref, v_ref, o_ref, log_ref, k_rows, v_wide):
    length = k_ref.shape[-1]
    chunk = chunk_of(length, 512)

    @pl.when(pl.program_id(1) == 0)
    def _():
        k_rows[...] = k_ref[0, 0].T
        v_wide[:HEAD, :] = v_ref[0, 0]
        v_wide[HEAD:, :] = jnp.ones((v_wide.shape[0] - HEAD, length), bf16)

    query = q_ref[0, 0]
    highest = None
    total = None
    for start in range(0, length, chunk):
        scores = dot(k_rows[start : start + chunk, :], query) * score_base2
        top = jnp.max(scores, 0, keepdims=True)
        new_high = top if highest is None else jnp.maximum(highest, top)
        weights = jnp.exp2(scores - new_high).astype(bf16)
        term = dot(v_wide[:, start : start + chunk], weights)
        total = term if total is None else total * jnp.exp2(highest - new_high) + term
        highest = new_high
    denominator = total[HEAD : HEAD + 1, :]
    o_ref[0, 0] = (total[:HEAD, :] / denominator).astype(bf16)
    log_ref[0] = highest + jnp.log2(denominator)


def attend(heads_t, block_len):
    _, count, _, length = heads_t.shape
    blocks = length // block_len
    return pl.pallas_call(
        forward_kernel,
        grid=(count, blocks),
        in_specs=[
            pl.BlockSpec((1, 1, HEAD, block_len), lambda h, c: (0, h, 0, c)),
            pl.BlockSpec((1, 1, HEAD, length), lambda h, c: (1, h, 0, 0)),
            pl.BlockSpec((1, 1, HEAD, length), lambda h, c: (2, h, 0, 0)),
        ],
        out_specs=[
            pl.BlockSpec((1, 1, HEAD, block_len), lambda h, c: (c, h, 0, 0)),
            pl.BlockSpec((1, 1, block_len), lambda h, c: (h, 0, c)),
        ],
        out_shape=[
            jax.ShapeDtypeStruct((blocks, count, HEAD, block_len), bf16),
            jax.ShapeDtypeStruct((count, 1, length), f32),
        ],
        scratch_shapes=[
            pltpu.VMEM((length, HEAD), bf16),
            pltpu.VMEM((HEAD + 16, length), bf16),
        ],
        compiler_params=pltpu.CompilerParams(vmem_limit_bytes=40 << 20),
        cost_estimate=pl.CostEstimate(
            flops=16 * count * length * length * HEAD,
            bytes_accessed=10 * count * length * HEAD,
            transcendentals=count * length * length,
        ),
    )(heads_t, heads_t, heads_t)


def rope_back(grad_t, cosine, sine):
    first, second = grad_t[:HALF, :], grad_t[HALF:, :]
    return (first * cosine + second * sine, second * cosine - first * sine)


def backward_kernel(
    q_ref, k_ref, v_ref, o_ref, up_ref, log_ref, cos_all, sin_all, cos_ref, sin_ref,
    dq_ref, dk_ref, dv_ref, q_rows, up_rows, up_cols, delta, dq_sum,
):
    step = pl.program_id(1)
    blocks, block_len = up_ref.shape[0], up_ref.shape[-1]
    length = q_ref.shape[-1]
    chunk = chunk_of(length, 512)

    @pl.when(step == 0)
    def _():
        q_rows[...] = q_ref[0, 0].T
        for number in range(blocks):
            place = slice(number * block_len, (number + 1) * block_len)
            upstream = up_ref[number, 0]
            up_cols[:, place] = upstream
            up_rows[place, :] = upstream.T
            delta[:, place] = jnp.sum(
                upstream.astype(f32) * o_ref[number, 0].astype(f32), 0, keepdims=True
            )
        dq_sum[...] = jnp.zeros_like(dq_sum)

    key_t = k_ref[0, 0]
    key = key_t.T
    value = v_ref[0, 0].T
    dk = None
    dv = None
    for start in range(0, length, chunk):
        place = slice(start, start + chunk)
        scores = dot(key, q_ref[0, 0, :, place]) * score_base2
        weights = jnp.exp2(scores - log_ref[0, :, place])
        weight_grad = dot(value, up_cols[:, place])
        score_grad = (weights * (weight_grad - delta[:, place])).astype(bf16)
        dv_term = dot(weights.astype(bf16), up_rows[place, :])
        dk_term = dot(score_grad, q_rows[place, :])
        dv = dv_term if dv is None else dv + dv_term
        dk = dk_term if dk is None else dk + dk_term
        dq_sum[:, place] += dot(key_t, score_grad)
    upper, lower = rope_back((dk * score_scale).T, cos_ref[...], sin_ref[...])
    dk_ref[0, :HALF, :] = upper.astype(bf16)
    dk_ref[0, HALF:, :] = lower.astype(bf16)
    dv_ref[0] = dv.T.astype(bf16)

    @pl.when(step == pl.num_programs(1) - 1)
    def _():
        upper, lower = rope_back(dq_sum[...] * score_scale, cos_all[...], sin_all[...])
        dq_ref[0, :HALF, :] = upper.astype(bf16)
        dq_ref[0, HALF:, :] = lower.astype(bf16)


def attend_back(heads_t, attended, upstream, log_total, cosine, sine):
    _, count, _, length = heads_t.shape
    blocks, _, _, block_len = attended.shape
    rows = chunk_of(length, 256)
    split = pl.BlockSpec((blocks, 1, HEAD, block_len), lambda h, k: (0, h, 0, 0))
    shape = jax.ShapeDtypeStruct((count, HEAD, length), bf16)
    return pl.pallas_call(
        backward_kernel,
        grid=(count, length // rows),
        in_specs=[
            pl.BlockSpec((1, 1, HEAD, length), lambda h, k: (0, h, 0, 0)),
            pl.BlockSpec((1, 1, HEAD, rows), lambda h, k: (1, h, 0, k)),
            pl.BlockSpec((1, 1, HEAD, rows), lambda h, k: (2, h, 0, k)),
            split,
            split,
            pl.BlockSpec((1, 1, length), lambda h, k: (h, 0, 0)),
            pl.BlockSpec((HALF, length), lambda h, k: (0, 0)),
            pl.BlockSpec((HALF, length), lambda h, k: (0, 0)),
            pl.BlockSpec((HALF, rows), lambda h, k: (0, k)),
            pl.BlockSpec((HALF, rows), lambda h, k: (0, k)),
        ],
        out_specs=[
            pl.BlockSpec((1, HEAD, length), lambda h, k: (h, 0, 0)),
            pl.BlockSpec((1, HEAD, rows), lambda h, k: (h, 0, k)),
            pl.BlockSpec((1, HEAD, rows), lambda h, k: (h, 0, k)),
        ],
        out_shape=[shape, shape, shape],
        scratch_shapes=[
            pltpu.VMEM((length, HEAD), bf16),
            pltpu.VMEM((length, HEAD), bf16),
            pltpu.VMEM((HEAD, length), bf16),
            pltpu.VMEM((1, length), f32),
            pltpu.VMEM((HEAD, length), f32),
        ],
        compiler_params=pltpu.CompilerParams(vmem_limit_bytes=40 << 20),
        cost_estimate=pl.CostEstimate(
            flops=40 * count * length * length * HEAD,
            bytes_accessed=16 * count * length * HEAD,
            transcendentals=count * length * length,
        ),
    )(heads_t, heads_t, heads_t, attended, upstream, log_total, cosine, sine, cosine, sine)


def gather_rows(shard):
    return lax.all_gather(shard, WEIGHT_AXES, axis=0, tiled=True)


def exchange(blocks):
    return lax.all_to_all(blocks, "ctx", 0, 0, tiled=True)


def general_body(
    tokens,
    cotangent,
    qkv_weight,
    out_weight,
    up_weight,
    down_weight,
    attention_gain,
    feedforward_gain,
):
    ctx = lax.axis_size("ctx")
    groups = lax.axis_size("dp") * lax.axis_size("fsdp")
    seq_count, block_len = (tokens.shape[0], tokens.shape[1])
    length = block_len * ctx
    sets = math.gcd(seq_count, ctx)
    each = seq_count // sets
    teams = ctx // sets
    own = -(-HEADS // teams)
    width = own * HEAD
    spare = teams * own - HEADS
    halves = 2 if own % 2 == 0 else 1
    part = own // halves
    shard_rows = qkv_weight.shape[0]
    row_count = seq_count * block_len

    moved = [
        exchange(jnp.repeat(tokens[turn::each], teams, axis=0)).reshape(length, D)
        for turn in range(each)
    ]

    by_head = qkv_weight.reshape(shard_rows, 3, D)
    if spare:
        by_head = jnp.pad(by_head, ((0, 0), (0, 0), (0, spare * HEAD)))
    team = lax.rem(lax.axis_index("ctx"), teams)
    own_columns = lax.dynamic_slice_in_dim(by_head, team * width, width, 2)
    gain_columns = jnp.pad(
        jnp.stack([attention_gain, feedforward_gain], -1), ((0, 0), (0, 126))
    )
    first_gather = gather_rows(
        jnp.concatenate([own_columns.reshape(shard_rows, 3 * width), gain_columns], -1)
    )
    qkv_own = first_gather[:, : 3 * width]
    attn_gain = first_gather[:, 3 * width].astype(f32)
    ffn_gain = first_gather[:, 3 * width + 1].astype(f32)
    out_whole = gather_rows(out_weight)
    up_whole = gather_rows(up_weight)
    down_whole = gather_rows(down_weight)
    cosine, sine = rope_rows(length)

    saved = []
    for turn in range(each):
        normal = layer_norm(moved[turn].astype(f32), attn_gain)[2].astype(bf16)
        by_part = qkv_own.reshape(D, 3, halves, part * HEAD)
        pieces = []
        for half in range(halves):
            weight = by_part[:, :, half].reshape(D, 3 * part * HEAD)
            projected = dot(weight, normal, 0, 1).reshape(3, part, 2, HALF, length)
            first, second = (projected[:2, :, 0], projected[:2, :, 1])
            turned = jnp.stack(
                [first * cosine - second * sine, second * cosine + first * sine], 2
            )
            heads_t = (
                jnp.concatenate([turned, projected[2:]], 0)
                .astype(bf16)
                .reshape(3, part, HEAD, length)
            )
            attended, log_total = attend(heads_t, block_len)
            pieces.append((heads_t, attended, log_total, exchange(attended)))
        saved.append((normal, pieces))

    columns = []
    for number in range(seq_count):
        chosen, turn = divmod(number, each)
        got = [
            piece[3].reshape(sets, teams, part, HEAD, block_len)[chosen]
            for piece in saved[turn][1]
        ]
        columns.append(jnp.concatenate(got, 1).reshape(teams * width, block_len)[:D])
    attended_t = jnp.concatenate(columns, 1)

    inputs = tokens.reshape(row_count, D).astype(f32)
    residual = inputs + dot(attended_t, out_whole, 0, 0)
    normed_b, inverse_b, scaled_b = layer_norm(residual, ffn_gain)
    normal_b = scaled_b.astype(bf16)
    widened = dot(normal_b, up_whole)
    hidden, hidden_back = jax.vjp(gated_gelu, widened[:, :FF], widened[:, FF:])
    hidden_low = hidden.astype(bf16)
    output = (residual + dot(hidden_low, down_whole)).astype(bf16)
    upstream = cotangent.reshape(row_count, D)
    hidden_grad = dot(upstream, down_whole, 1, 1)
    input_grad, gating_grad = hidden_back(hidden_grad)
    widened_grad = jnp.concatenate([input_grad, gating_grad], -1).astype(bf16)
    normal_b_grad = dot(widened_grad, up_whole, 1, 1)
    residual_grad = upstream.astype(f32) + norm_back(normal_b_grad, normed_b, inverse_b, ffn_gain)
    residual_low = residual_grad.astype(bf16)

    out_heads = out_whole
    if spare:
        out_heads = jnp.pad(out_heads, ((0, spare * HEAD), (0, 0)))
    out_heads = out_heads.reshape(teams, halves, part * HEAD, D)
    arrived = []
    for turn in range(each):
        for half in range(halves):
            weight = out_heads[:, half].reshape(teams * part * HEAD, D)
            sent = [
                dot(weight, residual_low[start : start + block_len], 1, 1).astype(bf16)
                for start in range(turn * block_len, row_count, each * block_len)
            ]
            arrived.append(exchange(jnp.stack(sent).reshape(ctx, part, HEAD, block_len)))

    down_grad = dot(hidden_low, upstream, 0, 0)
    up_grad = dot(normal_b, widened_grad, 0, 0)
    out_grad = dot(attended_t, residual_low)

    parts = [up_grad[:, start : start + D] for start in range(0, up_grad.shape[1], D)]
    parts += [down_grad, out_grad]
    packed = jnp.concatenate([item.astype(bf16).reshape(groups, -1, D) for item in parts], 1)
    shard = lax.psum_scatter(packed, WEIGHT_AXES, scatter_dimension=0, tiled=True)[0]
    shard = lax.psum(shard, "ctx").astype(f32)
    cuts = []
    offset = 0
    for item in parts:
        rows = item.shape[0] // groups
        cuts.append(shard[offset : offset + rows])
        offset += rows
    up_shard = jnp.concatenate(cuts[:-2], -1)
    down_shard, out_shard = cuts[-2:]

    back = []
    qkv_grad = 0.0
    for turn in range(each):
        normal, pieces = saved[turn]
        grads = []
        for half in range(halves):
            heads_t, attended, log_total, _ = pieces[half]
            grads.append(
                attend_back(
                    heads_t, attended, arrived[turn * halves + half], log_total, cosine, sine
                )
            )
        projected_grad = jnp.concatenate(
            [grads[half][which] for which in range(3) for half in range(halves)], 0
        ).reshape(3 * width, length)
        partial_grad = dot(projected_grad, qkv_own, 0, 1).astype(bf16)
        terms = exchange(partial_grad.reshape(ctx, block_len, D))
        back.append(terms.reshape(sets, teams, block_len, D).astype(f32).sum(1))
        qkv_grad = qkv_grad + dot(normal, projected_grad, 0, 1)
    normal_a_grad = jnp.stack(back, 1).reshape(row_count, D)
    normed_a, inverse_a, _ = layer_norm(inputs, attn_gain)
    token_grad = residual_grad + norm_back(normal_a_grad, normed_a, inverse_a, attn_gain)
    qkv_cut = lax.psum_scatter(
        qkv_grad.astype(bf16), WEIGHT_AXES, scatter_dimension=0, tiled=True
    )
    qkv_all = lax.all_gather(qkv_cut, "ctx", axis=0).astype(f32)
    qkv_all = qkv_all.reshape(sets, teams, shard_rows, 3, width).sum(0)
    qkv_shard = jnp.transpose(qkv_all, (1, 2, 0, 3)).reshape(shard_rows, 3, teams * width)
    qkv_shard = qkv_shard[:, :, :D].reshape(shard_rows, 3 * D)
    attn_gain_grad = jnp.sum(qkv_weight.astype(f32) * qkv_shard, -1) / attention_gain.astype(f32)
    ffn_gain_grad = jnp.sum(up_weight.astype(f32) * up_shard, -1) / feedforward_gain.astype(f32)
    return (
        output.reshape(seq_count, block_len, D),
        token_grad.reshape(seq_count, block_len, D),
        qkv_shard,
        out_shard,
        up_shard,
        down_shard,
        attn_gain_grad,
        ffn_gain_grad,
    )


MESH_ID = pl.DeviceIdType.MESH
VMEM_LIMIT = 60 << 20
vmem_spec = pl.BlockSpec(memory_space=pltpu.VMEM)
any_spec = pl.BlockSpec(memory_space=pl.ANY)


def here():
    dp = lax.axis_index("dp")
    return dp, lax.rem(dp, 2), dp // 2, lax.axis_index("ctx"), lax.axis_index("fsdp")


def params(number):
    return pltpu.CompilerParams(
        collective_id=number, has_side_effects=True, vmem_limit_bytes=VMEM_LIMIT
    )


def greet(partners):
    barrier = pltpu.get_barrier_semaphore()
    for partner in partners:
        pl.semaphore_signal(barrier, inc=1, device_id=partner, device_id_type=MESH_ID)
    pl.semaphore_wait(barrier, len(partners))


def remote(src, dst, send_sem, recv_sem, **device):
    return pltpu.make_async_remote_copy(
        src_ref=src, dst_ref=dst, send_sem=send_sem, recv_sem=recv_sem,
        device_id=device, device_id_type=MESH_ID,
    )


def near_order(place, count):
    def at(turn):
        block = place
        bit = 1
        while bit < count:
            flip = lax.rem(turn // bit, 2)
            block = block + flip * (bit - 2 * bit * lax.rem(place // bit, 2))
            bit *= 2
        return block
    return at


def prologue_kernel(
    ctx, nfsdp, groups, seqs,
    x_ref, w_ref, g_ref, cos_ref, sin_ref,
    heads_ref, normal_ref, half_ref, wt_ref, gain_ref,
    xbuf, wbuf, gbuf,
    send_x, recv_x, fwd_x, local_x, send_w, recv_w, local_w, send_g, recv_g, local_g,
):
    dp, core, x, z, y = here()
    sibling = dp + 1 - 2 * core
    block_len = x_ref.shape[1]
    shard_rows = w_ref.shape[0]
    width = wbuf.shape[1] // 3
    heads = width // HEAD
    me = dp * nfsdp + y
    lead = z // seqs == core
    others = []
    for j in range(1, groups):
        other = lax.rem(me + j, groups)
        others.append((other // nfsdp, lax.rem(other, nfsdp)))
    greet(
        [{"ctx": lax.rem(z + k, ctx)} for k in range(1, ctx)]
        + [{"dp": d, "fsdp": f} for d, f in others]
    )

    def column_copy(s):
        return remote(x_ref.at[s], xbuf.at[z], send_x.at[s], recv_x.at[z], ctx=core * seqs + s)

    def sibling_copy(s):
        return remote(x_ref.at[s], xbuf.at[z], send_x.at[s], recv_x.at[z], dp=sibling)

    for s in range(seqs):
        keep = core * seqs + s == z

        @pl.when(jnp.logical_not(keep))
        def _():
            column_copy(s).start()

        @pl.when(keep)
        def _():
            sibling_copy(s).start()
            own = pltpu.make_async_copy(x_ref.at[s], xbuf.at[z], local_x)
            own.start()
            own.wait()

    def weight_copy(j, part):
        d, f = others[j - 1]
        columns = pl.multiple_of(part * D + lax.rem(d, 2) * width, 128)
        return remote(
            w_ref.at[:, pl.ds(columns, width)],
            wbuf.at[pl.ds(pl.multiple_of(me * shard_rows, 16), shard_rows), pl.ds(part * width, width)],
            send_w.at[j - 1, part], recv_w.at[j - 1, part], dp=d, fsdp=f,
        )

    def gain_copy(j):
        d, f = others[j - 1]
        return remote(g_ref, gbuf.at[me], send_g.at[j - 1], recv_g.at[j - 1], dp=d, fsdp=f)

    for j in range(1, groups):
        gain_copy(j).start()
        for part in range(3):
            weight_copy(j, part).start()
    own = [pltpu.make_async_copy(g_ref, gbuf.at[me], local_g)]
    for part in range(3):
        columns = pl.multiple_of(part * D + core * width, 128)
        own.append(pltpu.make_async_copy(
            w_ref.at[:, pl.ds(columns, width)],
            wbuf.at[pl.ds(pl.multiple_of(me * shard_rows, 16), shard_rows), pl.ds(part * width, width)],
            local_w.at[part],
        ))
    for copy in own:
        copy.start()
    for copy in own:
        copy.wait()
    for j in range(1, groups):
        gain_copy(j).wait_recv()
        for part in range(3):
            weight_copy(j, part).wait_recv()

    gains = gbuf[0].astype(f32)
    for number in range(1, groups):
        gains = gains + gbuf[number].astype(f32)
    gain_ref[...] = gains
    wt_ref[...] = wbuf[...].T
    attn_gain = gains[0:1, :]
    order = near_order(z, ctx)

    def forward_copy(block):
        return remote(xbuf.at[block], xbuf.at[block], fwd_x.at[block], recv_x.at[block], dp=sibling)

    def turn(number, carry):
        block = order(number)

        @pl.when(jnp.logical_or(jnp.logical_not(lead), number > 0))
        def _():
            forward_copy(block).wait_recv()

        @pl.when(jnp.logical_and(lead, number > 0))
        def _():
            forward_copy(block).start()

        place = pl.ds(pl.multiple_of(block * block_len, 128), block_len)
        normal = layer_norm(xbuf[block].astype(f32), attn_gain)[2].astype(bf16)
        normal_ref[:, place] = normal.T
        cosine, sine = cos_ref[:, place], sin_ref[:, place]
        for part in range(3):
            projected = dot(wt_ref[part * width : (part + 1) * width, :], normal, 1, 1)
            for head in range(heads):
                first = projected[head * HEAD : head * HEAD + HALF, :]
                second = projected[head * HEAD + HALF : (head + 1) * HEAD, :]
                if part < 2:
                    first, second = (
                        first * cosine - second * sine, second * cosine + first * sine
                    )
                if part == 0:
                    first, second = first * score_base2, second * score_base2
                heads_ref[part, head, :HALF, place] = first.astype(bf16)
                heads_ref[part, head, HALF:, place] = second.astype(bf16)
        return carry

    lax.fori_loop(0, ctx, turn, 0)
    half_blocks = ctx // 2
    half_ref[...] = xbuf[pl.ds(core * half_blocks, half_blocks)].reshape(half_ref.shape)

    for s in range(seqs):
        sibling_copy(s).wait_send()
    for number in range(1, ctx):
        @pl.when(lead)
        def _():
            forward_copy(order(number)).wait_send()
    for j in range(1, groups):
        gain_copy(j).wait_send()
        for part in range(3):
            weight_copy(j, part).wait_send()


def prologue(tokens, qkv_weight, gains, cosine, sine, ctx, nfsdp, groups):
    seqs, block_len, _ = tokens.shape
    length = block_len * ctx
    width = D // 2
    shard_rows = qkv_weight.shape[0]
    dma = pltpu.SemaphoreType.DMA
    return pl.pallas_call(
        partial(prologue_kernel, ctx, nfsdp, groups, seqs),
        in_specs=[any_spec, any_spec, any_spec, vmem_spec, vmem_spec],
        out_specs=[vmem_spec] * 5,
        out_shape=[
            jax.ShapeDtypeStruct((3, width // HEAD, HEAD, length), bf16),
            jax.ShapeDtypeStruct((D, length), bf16),
            jax.ShapeDtypeStruct((length // 2, D), bf16),
            jax.ShapeDtypeStruct((3 * width, D), bf16),
            jax.ShapeDtypeStruct(gains.shape, f32),
        ],
        scratch_shapes=[
            pltpu.VMEM((ctx, block_len, D), bf16),
            pltpu.VMEM((groups * shard_rows, 3 * width), bf16),
            pltpu.VMEM((groups,) + gains.shape, bf16),
            dma((seqs,)), dma((ctx,)), dma((ctx,)), dma,
            dma((groups - 1, 3)), dma((groups - 1, 3)), dma((3,)),
            dma((groups - 1,)), dma((groups - 1,)), dma,
        ],
        compiler_params=params(1),
        name="prologue",
        cost_estimate=pl.CostEstimate(
            flops=6 * width * D * length, bytes_accessed=16 * length * D, transcendentals=0
        ),
    )(tokens, qkv_weight, gains, cosine, sine)


def column_partners(ctx):
    dp, core, x, z, y = here()
    found = [{"dp": dp + 1 - 2 * core}]
    for k in range(1, ctx):
        for c in range(2):
            found.append({"dp": 2 * x + c, "ctx": lax.rem(z + k, ctx)})
    return found


def to_halves(ctx, seqs, src, dst, send_sem, recv_sem, local_sem):
    dp, core, x, z, y = here()
    half = ctx // 2
    side, slot = z // half, lax.rem(z, half)

    def outgoing(s):
        return remote(
            src.at[s], dst.at[slot], send_sem.at[s], recv_sem.at[slot],
            dp=2 * x + side, ctx=core * seqs + s,
        )

    def stays(s):
        return jnp.logical_and(core * seqs + s == z, side == core)

    def own(s):
        return pltpu.make_async_copy(src.at[s], dst.at[slot], local_sem)

    def start():
        for s in range(seqs):
            @pl.when(stays(s))
            def _():
                own(s).start()

            @pl.when(jnp.logical_not(stays(s)))
            def _():
                outgoing(s).start()

    def finish():
        for s in range(seqs):
            @pl.when(stays(s))
            def _():
                own(s).wait()

            @pl.when(jnp.logical_not(stays(s)))
            def _():
                outgoing(s).wait_send()
        for i in range(half):
            mine = jnp.logical_and(z // seqs == core, core * half + i == z)

            @pl.when(jnp.logical_not(mine))
            def _():
                remote(
                    src.at[0], dst.at[i], send_sem.at[0], recv_sem.at[i], dp=dp
                ).wait_recv()

    return start, finish


def to_blocks(ctx, seqs, parts, src, dst, send_sem, recv_sem, local_sem):
    dp, core, x, z, y = here()
    half = ctx // 2
    side, slot = z // seqs, lax.rem(z, seqs)
    size = src.shape[1] // parts

    def outgoing(i, part):
        rows = slice(part * size, (part + 1) * size)
        return remote(
            src.at[i, rows], dst.at[slot, rows], send_sem.at[i, part], recv_sem.at[slot, part],
            dp=2 * x + side, ctx=core * half + i,
        )

    def stays(i):
        return jnp.logical_and(core * half + i == z, side == core)

    def own(i, part):
        rows = slice(part * size, (part + 1) * size)
        return pltpu.make_async_copy(src.at[i, rows], dst.at[slot, rows], local_sem.at[part])

    def start_one(i, part):
        @pl.when(stays(i))
        def _():
            own(i, part).start()

        @pl.when(jnp.logical_not(stays(i)))
        def _():
            outgoing(i, part).start()

    def finish():
        for part in range(parts):
            rows = slice(part * size, (part + 1) * size)
            for i in range(half):
                @pl.when(stays(i))
                def _():
                    own(i, part).wait()

                @pl.when(jnp.logical_not(stays(i)))
                def _():
                    outgoing(i, part).wait_send()
            for s in range(seqs):
                mine = jnp.logical_and(z // half == core, core * seqs + s == z)

                @pl.when(jnp.logical_not(mine))
                def _():
                    remote(
                        src.at[0, rows], dst.at[s, rows], send_sem.at[0, part],
                        recv_sem.at[s, part], dp=dp,
                    ).wait_recv()

    return start_one, finish


def block_sems(ctx, seqs, parts):
    dma = pltpu.SemaphoreType.DMA
    return [dma((ctx // 2, parts)), dma((seqs, parts)), dma((parts,))]


def attend_kernel(
    ctx, seqs, nfsdp, groups,
    q_ref, k_ref, v_ref, cot_ref, up_ref, o_ref, log_ref, all_ref, half_ref, whole_ref,
    k_rows, v_wide, done,
    send_c, recv_c, local_c, send_o, recv_o, local_o, send_u, recv_u, send_f, recv_f, local_u,
):
    head, step = pl.program_id(0), pl.program_id(1)
    heads, steps = pl.num_programs(0), pl.num_programs(1)
    dp, core, x, z, y = here()
    sibling = dp + 1 - 2 * core
    length = k_ref.shape[-1]
    chunk = chunk_of(length, 128)
    block = q_ref.shape[-1]
    half = length // 2
    start, finish = to_halves(ctx, seqs, cot_ref, half_ref, send_c, recv_c, local_c)
    mine, others = chips_of(nfsdp, groups)
    shard_rows = up_ref.shape[0]

    def rows_of(group):
        return pl.ds(pl.multiple_of(group * shard_rows, 16), shard_rows)

    own_rows = rows_of(dp * nfsdp + y)
    own_shard = pltpu.make_async_copy(up_ref, whole_ref.at[own_rows], local_u)
    shard_copies = [
        remote(up_ref, whole_ref.at[own_rows], send_u.at[j], recv_u.at[j], dp=2 * cx + core, fsdp=cy)
        for j, (_, cx, cy) in enumerate(others)
    ]
    twin_copy = remote(
        up_ref, whole_ref.at[own_rows], send_u.at[len(others)], recv_u.at[len(others)], dp=sibling
    )
    passed_on = []
    for j in range(len(others)):
        source = lax.rem(mine + len(others) - j, groups // 2)
        got = whole_ref.at[rows_of((2 * (source // nfsdp) + core) * nfsdp + lax.rem(source, nfsdp))]
        passed_on.append(remote(got, got, send_f.at[j], recv_f.at[j], dp=sibling))

    @pl.when(jnp.logical_and(head == 0, step == 0))
    def _():
        greet(column_partners(ctx) + plane_partners(nfsdp, groups))
        for each in shard_copies:
            each.start()
        start()
        own_shard.start()
        twin_copy.start()

    @pl.when(step == 0)
    def _():
        k_rows[...] = k_ref[0, 0].T
        v_wide[:HEAD, :] = v_ref[0, 0]
        v_wide[HEAD:, :] = jnp.ones((v_wide.shape[0] - HEAD, length), bf16)

    query = q_ref[0, 0]
    highest = None
    total = None
    coming = dot(k_rows[:chunk, :], query)
    for first in range(0, length, chunk):
        scores = coming
        after = first + chunk
        if after < length:
            coming = dot(k_rows[after : after + chunk, :], query)
        top = jnp.max(scores, 0, keepdims=True)
        new_high = top if highest is None else jnp.maximum(highest, top)
        weights = jnp.exp2(scores - new_high).astype(bf16)
        term = dot(v_wide[:, first:after], weights)
        total = term if total is None else total * jnp.exp2(highest - new_high) + term
        highest = new_high
    denominator = total[HEAD : HEAD + 1, :]
    result = (total[:HEAD, :] / denominator).astype(bf16)
    o_ref[0] = result
    done[head, :, pl.ds(pl.multiple_of(step * block, 128), block)] = result
    log_ref[0] = highest + jnp.log2(denominator)

    def own_copy(number):
        return pltpu.make_async_copy(
            done.at[number, :, pl.ds(pl.multiple_of(core * half, 128), half)],
            all_ref.at[core * heads + number], local_o.at[number],
        )

    def sibling_copy(number):
        return remote(
            done.at[number, :, pl.ds(pl.multiple_of((1 - core) * half, 128), half)],
            all_ref.at[core * heads + number], send_o.at[number], recv_o.at[number], dp=sibling,
        )

    @pl.when(step == steps - 1)
    def _():
        own_copy(head).start()
        sibling_copy(head).start()

    @pl.when(jnp.logical_and(head == heads - 1, step == steps - 1))
    def _():
        for each, further in zip(shard_copies, passed_on):
            each.wait()
            further.start()

        def settle(number, carry):
            own_copy(number).wait()
            sibling_copy(number).wait()
            return carry
        lax.fori_loop(0, heads, settle, 0)
        own_shard.wait()
        twin_copy.wait()
        for further in passed_on:
            further.wait()
        finish()


def attend_chip(heads_t, cotangent, up_weight, ctx, nfsdp, groups):
    _, count, _, length = heads_t.shape
    seqs, block_len, _ = cotangent.shape
    block = length
    dma = pltpu.SemaphoreType.DMA
    return pl.pallas_call(
        partial(attend_kernel, ctx, seqs, nfsdp, groups),
        grid=(count, length // block),
        in_specs=[
            pl.BlockSpec((1, 1, HEAD, block), lambda h, c: (0, h, 0, c)),
            pl.BlockSpec((1, 1, HEAD, length), lambda h, c: (1, h, 0, 0)),
            pl.BlockSpec((1, 1, HEAD, length), lambda h, c: (2, h, 0, 0)),
            any_spec,
            any_spec,
        ],
        out_specs=[
            pl.BlockSpec((1, HEAD, block), lambda h, c: (h, 0, c)),
            pl.BlockSpec((1, 1, block), lambda h, c: (h, 0, c)),
            any_spec,
            any_spec,
            any_spec,
        ],
        out_shape=[
            jax.ShapeDtypeStruct((count, HEAD, length), bf16),
            jax.ShapeDtypeStruct((count, 1, length), f32),
            jax.ShapeDtypeStruct((2 * count, HEAD, length // 2), bf16),
            jax.ShapeDtypeStruct((ctx // 2, block_len, D), bf16),
            jax.ShapeDtypeStruct((groups * up_weight.shape[0], up_weight.shape[1]), bf16),
        ],
        scratch_shapes=[
            pltpu.VMEM((length, HEAD), bf16),
            pltpu.VMEM((HEAD + 16, length), bf16),
            pltpu.VMEM((count, HEAD, length), bf16),
            dma((seqs,)), dma((ctx // 2,)), dma,
            dma((count,)), dma((count,)), dma((count,)),
            dma((groups // 2,)), dma((groups // 2,)),
            dma((groups // 2 - 1,)), dma((groups // 2 - 1,)), dma,
        ],
        compiler_params=params(2),
        name="attend",
        cost_estimate=pl.CostEstimate(
            flops=16 * count * length * length * HEAD,
            bytes_accessed=10 * count * length * HEAD,
            transcendentals=count * length * length,
        ),
    )(heads_t, heads_t, heads_t, cotangent, up_weight)


def ffn_kernel(
    ctx, seqs, nfsdp, groups, x_ref, att_ref, cot_ref, out_w, up_w, down_w, gain_ref,
    output_ref, rgrad_ref, agrad_ref, shard_ref, first_ref,
    normal_t, hidden_t, widened, low, cot_all, att_all, agrad, packed, twin, first_out,
    send_sem, recv_sem, local_sem, send_t, recv_t, *block_signals,
):
    step, steps = pl.program_id(0), pl.num_programs(0)
    dp, core, x, z, y = here()
    sibling = dp + 1 - 2 * core
    block = x_ref.shape[0]
    half = block * steps
    ff = down_w.shape[0]
    model = x_ref.shape[1]

    blocks = ctx // 2
    start_one, finish = to_blocks(ctx, seqs, 1, first_out, first_ref, *block_signals)

    @pl.when(step == 0)
    def _():
        greet(column_partners(ctx))

    row_block = lax.rem(step, blocks) * (steps // blocks) + step // blocks
    place = pl.ds(pl.multiple_of(row_block * block, 128), block)
    attended = att_ref[...]
    upstream = cot_ref[...]
    gain = gain_ref[1:2, :]
    residual = x_ref[...].astype(f32) + dot(attended.T, out_w[...])
    normed, inverse, scaled = layer_norm(residual, gain)
    normal = scaled.astype(bf16)
    wide = dot(normal, up_w[...])
    inputs, gating = wide[:, :ff], wide[:, ff:]
    phi_sum = 0.5 + 0.5 * lax.erf(inputs * math.sqrt(0.5))
    density = jnp.exp2(inputs * inputs * (-0.5 * math.log2(math.e))) * (1.0 / math.sqrt(2.0 * math.pi))
    gelu = inputs * phi_sum
    hidden = (gelu * gating).astype(bf16)
    result = (residual + dot(hidden, down_w[...])).astype(bf16)
    output_ref[0] = result
    for number in range(blocks):
        @pl.when(step == number)
        def _():
            first_out[number] = result
            start_one(number, 0)

    hidden_grad = dot(upstream, down_w[...], 1, 1)
    input_grad = (hidden_grad * gating * (phi_sum + inputs * density)).astype(bf16)
    gating_grad = (hidden_grad * gelu).astype(bf16)
    widened[place, :ff] = input_grad
    widened[place, ff:] = gating_grad
    normal_grad = dot(input_grad, up_w[:, :ff], 1, 1) + dot(gating_grad, up_w[:, ff:], 1, 1)
    residual_grad = upstream.astype(f32) + norm_back(normal_grad, normed, inverse, gain)
    rgrad_ref[...] = residual_grad
    residual_low = residual_grad.astype(bf16)
    agrad[:, place] = dot(out_w[...], residual_low, 1, 1).astype(bf16)
    normal_t[:, place] = normal.T
    hidden_t[:, place] = hidden.T
    low[place, :] = residual_low
    cot_all[place, :] = upstream
    att_all[:, place] = attended

    def agrad_copies():
        width = agrad.shape[0] // 2
        mine = pl.ds(pl.multiple_of(core * half, 128), half)
        return (
            pltpu.make_async_copy(
                agrad.at[pl.ds(pl.multiple_of(core * width, 16), width), :],
                agrad_ref.at[:, mine], local_sem,
            ),
            remote(
                agrad.at[pl.ds(pl.multiple_of((1 - core) * width, 16), width), :],
                agrad_ref.at[:, mine], send_sem, recv_sem, dp=sibling,
            ),
        )

    @pl.when(step == steps - 1)
    def _():
        for copy in agrad_copies():
            copy.start()
        chips = groups // 2
        pieces = [
            (normal_t, widened.at[:, pl.ds(first, model)]) for first in range(0, 2 * ff, model)
        ]
        pieces += [(att_all, low), (hidden_t, cot_all)]
        spans = []
        offset = 0

        def group_of(chip, c):
            return (2 * (chip // nfsdp) + c) * nfsdp + chip % nfsdp

        def twin_copy(number, chip):
            rows = spans[number]
            return remote(
                packed.at[group_of(chip, 0) + (1 - core) * nfsdp, rows], twin.at[chip, rows],
                send_t.at[number, chip], recv_t.at[number, chip], dp=sibling,
            )

        for number, (left, right) in enumerate(pieces):
            grad = dot(left[...], right[...])
            rows = grad.shape[0] // groups
            spans.append(slice(offset, offset + rows))
            packed[:, spans[-1], :] = grad.astype(bf16).reshape(groups, rows, model)
            offset += rows
            for chip in range(chips):
                twin_copy(number, chip).start()
        for number, rows in enumerate(spans):
            for chip in range(chips):
                twin_copy(number, chip).wait()
                mine = packed[group_of(chip, 0) + core * nfsdp, rows].astype(f32)
                shard_ref[chip, rows] = (mine + twin[chip, rows].astype(f32)).astype(bf16)
        for copy in agrad_copies():
            copy.wait()
        finish()


def feed_forward(x, attended, cotangent, out_w, up_w, down_w, gains, nfsdp, groups, ctx, seqs):
    half = x.shape[0]
    ff = down_w.shape[0]
    blocks = ctx // 2
    block = half // blocks // 2
    chips, pieces = groups // 2, 2 * ff // D + 2
    rows = (2 * ff // D * D + ff + D) // groups
    dma = pltpu.SemaphoreType.DMA

    def whole(array):
        return pl.BlockSpec(array.shape, lambda i: (0,) * array.ndim, pipeline_mode=pl.Buffered(1))

    def turned(i):
        return i % blocks * 2 + i // blocks

    by_rows = pl.BlockSpec((block, D), lambda i: (turned(i), 0))
    return pl.pallas_call(
        partial(ffn_kernel, ctx, seqs, nfsdp, groups),
        grid=(half // block,),
        in_specs=[
            by_rows,
            pl.BlockSpec((D, block), lambda i: (0, turned(i))),
            by_rows,
            whole(out_w), whole(up_w), whole(down_w), whole(gains),
        ],
        out_specs=[
            pl.BlockSpec((1, block, D), lambda i: (jnp.maximum(i - blocks, 0), 0, 0)),
            by_rows,
            any_spec,
            vmem_spec,
            any_spec,
        ],
        out_shape=[
            jax.ShapeDtypeStruct((blocks, block, D), bf16),
            jax.ShapeDtypeStruct((half, D), f32),
            jax.ShapeDtypeStruct((D // 2, 2 * half), bf16),
            jax.ShapeDtypeStruct((chips, rows, D), bf16),
            jax.ShapeDtypeStruct((seqs, block, D), bf16),
        ],
        scratch_shapes=[
            pltpu.VMEM((D, half), bf16),
            pltpu.VMEM((ff, half), bf16),
            pltpu.VMEM((half, 2 * ff), bf16),
            pltpu.VMEM((half, D), bf16),
            pltpu.VMEM((half, D), bf16),
            pltpu.VMEM((D, half), bf16),
            pltpu.VMEM((D, half), bf16),
            pltpu.VMEM((groups, rows, D), bf16),
            pltpu.VMEM((chips, rows, D), bf16),
            pltpu.VMEM((blocks, block, D), bf16),
            dma, dma, dma, dma((pieces, chips)), dma((pieces, chips)),
            *block_sems(ctx, seqs, 1),
        ],
        compiler_params=params(3),
        name="feed_forward",
        cost_estimate=pl.CostEstimate(
            flops=6 * half * D * (3 * ff + D), bytes_accessed=32 << 20,
            transcendentals=2 * half * ff,
        ),
    )(x, attended, cotangent, out_w, up_w, down_w, gains)


def chips_of(nfsdp, groups):
    dp, core, x, z, y = here()
    chips = groups // 2
    mine = x * nfsdp + y
    found = []
    for j in range(1, chips):
        other = lax.rem(mine + j, chips)
        found.append((other, other // nfsdp, lax.rem(other, nfsdp)))
    return mine, found


def plane_partners(nfsdp, groups):
    dp, core, x, z, y = here()
    return [
        {"dp": 2 * cx + c, "fsdp": cy}
        for _, cx, cy in chips_of(nfsdp, groups)[1] for c in range(2)
    ]


def z_sum(ctx, sent, got, final, sems):
    z = lax.axis_index("ctx")
    send_a, recv_a, send_b, recv_b = sems

    def piece(k):
        to = lax.rem(z + k, ctx)
        return remote(sent.at[to], got.at[k - 1], send_a.at[k - 1], recv_a.at[k - 1], ctx=to)

    def result(k):
        to = lax.rem(z + k, ctx)
        return remote(final.at[z], final.at[z], send_b.at[k - 1], recv_b.at[k - 1], ctx=to)

    def start():
        for k in range(1, ctx):
            piece(k).start()

    def middle():
        for k in range(1, ctx):
            piece(k).wait()
        total = sent[z].astype(f32)
        for k in range(1, ctx):
            total = total + got[k - 1].astype(f32)
        final[z] = total.astype(bf16)
        for k in range(1, ctx):
            result(k).start()

    def finish():
        for k in range(1, ctx):
            result(k).wait()

    return start, middle, finish


def z_sems(ctx):
    return [pltpu.SemaphoreType.DMA((ctx - 1,))] * 4


def column_sum(ctx, nfsdp, groups, src, got, zsent, zgot, final, sems):
    dp, core, x, z, y = here()
    mine, others = chips_of(nfsdp, groups)
    send_q, recv_q = sems[:2]
    z_start, z_middle, z_finish = z_sum(ctx, zsent, zgot, final, sems[2:])
    places = [(x, y)] + [(cx, cy) for _, cx, cy in others]
    chips = len(places)

    def copy(j, way):
        cx, cy = places[j]
        c = core if way == 0 else 1 - core
        return remote(
            src.at[(2 * cx + c) * nfsdp + cy], got.at[way, j],
            send_q.at[way, j], recv_q.at[way, j], dp=2 * cx + c, fsdp=cy,
        )

    pairs = [(j, way) for way in range(2) for j in range(chips) if (j, way) != (0, 0)]

    def send():
        for pair in pairs:
            copy(*pair).start()

    def plane():
        for pair in pairs:
            copy(*pair).wait()
        rows, columns = src.shape[1], src.shape[2]
        per = ctx // 2
        for way in range(2):
            owner = core if way == 0 else 1 - core
            total = (src[dp * nfsdp + y] if way == 0 else got[1, 0]).astype(f32)
            for j in range(1, chips):
                total = total + got[way, j].astype(f32)
            zsent[pl.ds(owner * per, per)] = total.astype(bf16).reshape(per, rows // per, columns)
        z_start()

    return send, plane, z_middle, z_finish


def column_scratch(ctx, groups, rows, columns):
    chips, per = groups // 2, 2 * rows // ctx
    dma = pltpu.SemaphoreType.DMA
    buffers = [
        pltpu.VMEM((2, chips, rows, columns), bf16),
        pltpu.VMEM((ctx, per, columns), bf16),
        pltpu.VMEM((ctx - 1, per, columns), bf16),
        pltpu.VMEM((ctx, per, columns), bf16),
    ]
    return buffers, [dma((2, chips))] * 2 + z_sems(ctx)


def plane_sum(ctx, nfsdp, groups, spans, own, got, zsent, zgot, final, sems):
    dp, core, x, z, y = here()
    mine, others = chips_of(nfsdp, groups)
    send_q, recv_q = sems[:2]
    per = zsent.shape[2]
    z_stages = [
        z_sum(
            ctx, zsent.at[n], zgot.at[n], final.at[n],
            [sems[k].at[n] for k in range(2, 6)],
        )
        for n in range(len(spans))
    ]

    def copy(number, j):
        chip, cx, cy = others[j]
        rows = spans[number]
        return remote(
            own.at[chip, rows], got.at[j, rows], send_q.at[number, j], recv_q.at[number, j],
            dp=2 * cx + core, fsdp=cy,
        )

    def begin(number):
        for j in range(len(others)):
            copy(number, j).start()

    def plane(number):
        rows = spans[number]
        for j in range(len(others)):
            copy(number, j).wait()
        total = own[mine, rows].astype(f32)
        for j in range(len(others)):
            total = total + got[j, rows].astype(f32)
        low = total.astype(bf16)
        count = low.shape[0]
        for k in range(ctx):
            first, last = min(k * per, count), min((k + 1) * per, count)
            if last > first:
                zsent[number, k, : last - first, :] = low[first:last, :]
            if last - first < per:
                zsent[number, k, last - first :, :] = jnp.zeros(
                    (per - last + first, low.shape[1]), bf16
                )
        z_stages[number][0]()

    def middle(number):
        z_stages[number][1]()

    def finish():
        for stage in z_stages:
            stage[2]()

    return begin, plane, middle, finish


def plane_scratch(ctx, groups, spans):
    chips, count = groups // 2, len(spans)
    most = max(span.stop - span.start for span in spans)
    per = -(-most // (16 * ctx)) * 16
    dma = pltpu.SemaphoreType.DMA
    buffers = [
        pltpu.VMEM((chips - 1, spans[-1].stop, D), bf16),
        pltpu.VMEM((count, ctx, per, D), bf16),
        pltpu.VMEM((count, ctx - 1, per, D), bf16),
        pltpu.VMEM((count, ctx, per, D), bf16),
    ]
    return buffers, [dma((count, chips - 1))] * 2 + [dma((count, ctx - 1))] * 4


def attend_back_kernel(
    ctx, nfsdp, groups, seqs, spans, parts,
    q_ref, k_ref, v_ref, o_ref, up_ref, log_ref, cos_all, sin_all, cos_ref, sin_ref,
    normal_ref, shard_ref, out_ref, wt_ref, x_ref, rgrad_ref, gain_ref,
    sums_ref, qkv_ref, output_ref, token_ref,
    q_rows, up_rows, up_cols, delta, dq_sum, dproj, pair_proj, fresh,
    dn_send, dn_recv, tg_send, *scratch,
):
    head, step = pl.program_id(0), pl.program_id(1)
    heads, steps = pl.num_programs(0), pl.num_programs(1)
    dp, core, x, z, y = here()
    sibling = dp + 1 - 2 * core
    length = q_ref.shape[-1]
    rows = k_ref.shape[-1]
    chunk = chunk_of(length, 256)
    pairs = fresh.shape[0]
    total_steps = pairs * 2 * (length // rows)
    last = total_steps - 1
    now = head * steps + step

    def take(count):
        nonlocal scratch
        taken, scratch = scratch[:count], scratch[count:]
        return taken

    send_n, recv_n = take(2)
    begin, plane, middle, plane_finish = plane_sum(
        ctx, nfsdp, groups, spans, shard_ref, *(bufs := take(4)), take(6)
    )
    out_start, out_finish = to_blocks(ctx, seqs, 1, out_ref, output_ref, *take(3))
    token_start, token_finish = to_blocks(ctx, seqs, parts, tg_send, token_ref, *take(3))
    columns, finals = [], []
    for p in range(pairs):
        column_bufs = take(4)
        finals.append(column_bufs[3])
        columns.append(column_sum(
            ctx, nfsdp, groups, fresh.at[p], *column_bufs, take(6)
        ))

    @pl.when(now == 0)
    def _():
        greet(column_partners(ctx) + plane_partners(nfsdp, groups))
        begin(0)

    @pl.when(step == 0)
    def _():
        q_rows[...] = q_ref[0, 0].T
        upstream = up_ref[0]
        up_cols[...] = upstream
        up_rows[...] = upstream.T
        delta[...] = jnp.sum(
            upstream.astype(f32) * o_ref[0].astype(f32), 0, keepdims=True
        )
        dq_sum[...] = jnp.zeros_like(dq_sum)

    key_t = k_ref[0, 0]
    key = key_t.T
    value = v_ref[0, 0].T
    dk = None
    dv = None
    for start in range(0, length, chunk):
        place = slice(start, start + chunk)
        scores = dot(key, q_ref[0, 0, :, place])
        weights = jnp.exp2(scores - log_ref[0, :, place])
        weight_grad = dot(value, up_cols[:, place])
        score_grad = (weights * (weight_grad - delta[:, place])).astype(bf16)
        dv_term = dot(weights.astype(bf16), up_rows[place, :])
        dk_term = dot(score_grad, q_rows[place, :])
        dv = dv_term if dv is None else dv + dv_term
        dk = dk_term if dk is None else dk + dk_term
        dq_sum[:, place] += dot(key_t, score_grad)
    block = pl.ds(pl.multiple_of(step * rows, 128), rows)
    upper, lower = rope_back((dk * math.log(2.0)).T, cos_ref[...], sin_ref[...])
    dproj[1, head, :HALF, block] = upper.astype(bf16)
    dproj[1, head, HALF:, block] = lower.astype(bf16)
    dproj[2, head, :, block] = dv.T.astype(bf16)

    @pl.when(step == steps - 1)
    def _():
        upper, lower = rope_back(dq_sum[...] * score_scale, cos_all[...], sin_all[...])
        dproj[0, head, :HALF, :] = upper.astype(bf16)
        dproj[0, head, HALF:, :] = lower.astype(bf16)
        for part in range(3):
            first = pl.multiple_of(part * 2 * HEAD + lax.rem(head, 2) * HEAD, HEAD)
            pair_proj[pl.ds(first, HEAD), :] = dproj[part, head]

    @pl.when(jnp.logical_and(step == steps - 1, lax.rem(head, 2) == 1))
    def _():
        grad = dot(normal_ref[...], pair_proj[...], 1, 1).astype(bf16)
        fresh[head // 2] = grad.reshape(fresh.shape[1:])

    events = {}

    def at(turn, what, *args):
        events.setdefault(total_steps * turn // 12, []).append(partial(what, *args))

    count = len(spans)
    for number in range(1, count):
        at(number * 5 // count, begin, number)
    for number in range(count):
        at(2 + 6 * number // count, plane, number)
    for number in range(count):
        at(5 + 6 * number // count, middle, number)
    for i in range(ctx // 2):
        at(3 + 3 * i, out_start, i, 0)
    for p in range(pairs - 1):
        done = 12 * (p + 1) // pairs - 1
        for number, what in enumerate(columns[p][:3]):
            at(min(done + (0, 3 - (p > 0), 5 - 2 * (p > 0))[number], 10), what)
    for when, things in sorted(events.items()):
        @pl.when(now == when)
        def _():
            for thing in things:
                thing()

    half = x_ref.shape[0]
    blocks = tg_send.shape[0]
    block_len = half // blocks
    size = block_len // parts

    def dn_rows(first):
        place = pl.ds(pl.multiple_of(first, 128), size)
        grads = dproj[:, :, :, place].reshape(wt_ref.shape[0], size)
        return dot(grads, wt_ref[...], 0, 0)

    def sibling_copy(number):
        return remote(
            dn_send.at[number], dn_recv.at[number], send_n.at[number], recv_n.at[number],
            dp=sibling,
        )

    def sibling_part(number):
        dn_send[number] = dn_rows((1 - core) * half + number * size).astype(bf16)
        sibling_copy(number).start()

    def own_part(number):
        first = number * size
        place = slice(first, first + size)
        gain = gain_ref[0:1, :]
        grad = dn_rows(core * half + first)
        sibling_copy(number).wait()
        grad = grad + dn_recv[number].astype(f32)
        normed, inverse, _ = layer_norm(x_ref[place, :].astype(f32), gain)
        token = rgrad_ref[place, :] + norm_back(grad, normed, inverse, gain)
        i, part = number // parts, number % parts
        tg_send[i, part * size : (part + 1) * size, :] = token.astype(bf16)

    @pl.when(now == last)
    def _():
        ending = columns[pairs - 1]
        ending[0]()
        parts_all = blocks * parts
        early_parts = parts_all // 2
        for number in range(parts_all):
            sibling_part(number)
            if 0 < number <= early_parts:
                own_part(number - 1)
                token_start((number - 1) // parts, (number - 1) % parts)
        ending[1]()
        for number in range(early_parts, parts_all):
            own_part(number)
            if number < parts_all - 1:
                token_start(number // parts, number % parts)
        ending[2]()
        token_start(blocks - 1, parts - 1)
        out_finish()
        plane_finish()
        sums_ref[...] = bufs[3][...]
        for p in range(pairs):
            columns[p][3]()
            qkv_ref[p] = finals[p][...]
        token_finish()


def attend_back_chip(
    heads_t, attended, upstream, log_total, cosine, sine, normal_t, shards, spans, output,
    wt, x, rgrad, gains, ctx, nfsdp, groups, seqs,
):
    _, count, _, length = heads_t.shape
    rows = chunk_of(length, 1024)
    pairs = count // 2
    half = length // 2
    block_len = length // ctx
    parts = 2 if block_len % 256 == 0 else 1
    size = block_len // parts
    shard_rows = normal_t.shape[0] // groups
    plane_bufs, plane_signals = plane_scratch(ctx, groups, spans)
    column_bufs, column_signals = column_scratch(ctx, groups, shard_rows, 6 * HEAD)
    full = pl.BlockSpec((1, HEAD, length), lambda h, k: (h, 0, 0))
    table = pl.BlockSpec((HALF, length), lambda h, k: (0, 0), pipeline_mode=pl.Buffered(1))
    table_part = pl.BlockSpec((HALF, rows), lambda h, k: (0, k))
    dma = pltpu.SemaphoreType.DMA

    def whole(array):
        return pl.BlockSpec(
            array.shape, lambda h, k: (0,) * array.ndim, pipeline_mode=pl.Buffered(1)
        )

    return pl.pallas_call(
        partial(attend_back_kernel, ctx, nfsdp, groups, seqs, spans, parts),
        grid=(count, length // rows),
        in_specs=[
            pl.BlockSpec((1, 1, HEAD, length), lambda h, k: (0, h, 0, 0)),
            pl.BlockSpec((1, 1, HEAD, rows), lambda h, k: (1, h, 0, k)),
            pl.BlockSpec((1, 1, HEAD, rows), lambda h, k: (2, h, 0, k)),
            full,
            full,
            pl.BlockSpec((1, 1, length), lambda h, k: (h, 0, 0)),
            table,
            table,
            table_part,
            table_part,
            whole(normal_t), whole(shards), any_spec, whole(wt), whole(x), whole(rgrad),
            whole(gains),
        ],
        out_specs=[vmem_spec, vmem_spec, any_spec, any_spec],
        out_shape=[
            jax.ShapeDtypeStruct(plane_bufs[3].shape, bf16),
            jax.ShapeDtypeStruct((pairs, ctx, 2 * shard_rows // ctx, 6 * HEAD), bf16),
            jax.ShapeDtypeStruct((seqs,) + output.shape[1:], bf16),
            jax.ShapeDtypeStruct((seqs, block_len, D), bf16),
        ],
        scratch_shapes=[
            pltpu.VMEM((length, HEAD), bf16),
            pltpu.VMEM((length, HEAD), bf16),
            pltpu.VMEM((HEAD, length), bf16),
            pltpu.VMEM((1, length), f32),
            pltpu.VMEM((HEAD, length), f32),
            pltpu.VMEM((3, count, HEAD, length), bf16),
            pltpu.VMEM((6 * HEAD, length), bf16),
            pltpu.VMEM((pairs, groups, shard_rows, 6 * HEAD), bf16),
            pltpu.VMEM((half // size, size, D), bf16),
            pltpu.VMEM((half // size, size, D), bf16),
            pltpu.VMEM((ctx // 2, block_len, D), bf16),
            dma((half // size,)), dma((half // size,)),
            *plane_bufs, *plane_signals,
            *block_sems(ctx, seqs, 1), *block_sems(ctx, seqs, parts),
            *(column_bufs + column_signals) * pairs,
        ],
        compiler_params=params(4),
        name="attend_back",
        cost_estimate=pl.CostEstimate(
            flops=40 * count * length * length * HEAD,
            bytes_accessed=16 * count * length * HEAD,
            transcendentals=count * length * length,
        ),
    )(
        heads_t, heads_t, heads_t, attended, upstream, log_total,
        cosine, sine, cosine, sine, normal_t, shards, output, wt, x, rgrad, gains,
    )


def chip_body(
    tokens,
    cotangent,
    qkv_weight,
    out_weight,
    up_weight,
    down_weight,
    attention_gain,
    feedforward_gain,
):
    ctx, nfsdp = lax.axis_size("ctx"), lax.axis_size("fsdp")
    groups = lax.axis_size("dp") * nfsdp
    seqs, block_len, _ = tokens.shape
    length = block_len * ctx
    width = D // 2
    shard_rows = qkv_weight.shape[0]
    me = lax.axis_index("dp") * nfsdp + lax.axis_index("fsdp")
    gain_rows = lax.dynamic_update_slice(
        jnp.zeros((16, D), bf16), jnp.stack([attention_gain, feedforward_gain]),
        (0, me * shard_rows),
    )
    frequency = np.float32(rope_base) ** (np.arange(HALF, dtype=np.float32) * np.float32(-2 / HEAD))
    angles = frequency[:, None] * np.arange(length, dtype=np.float32)[None, :]
    cosine, sine = jnp.asarray(np.cos(angles)), jnp.asarray(np.sin(angles))
    out_whole = gather_rows(out_weight)
    down_whole = gather_rows(down_weight)
    heads_t, normal_t, x_half, wt, gains = prologue(
        tokens, qkv_weight, gain_rows, cosine, sine, ctx, nfsdp, groups
    )
    attended, log_total, att_all, cot_half, up_whole = attend_chip(
        heads_t, cotangent, up_weight, ctx, nfsdp, groups
    )
    output, rgrad, agrad, shards, first_rows = feed_forward(
        x_half, att_all.reshape(D, length // 2), cot_half.reshape(length // 2, D),
        out_whole, up_whole, down_whole, gains, nfsdp, groups, ctx, seqs,
    )
    up_parts = up_weight.shape[1] // D
    rows = [shard_rows] * (up_parts - 1) + [
        shard_rows + out_weight.shape[0], down_weight.shape[0]
    ]
    if up_parts == 3:
        rows = [2 * shard_rows] + rows[2:]
    spans, first = [], 0
    for count in rows:
        spans.append(slice(first, first + count))
        first += count
    sums, pieces, last_rows, token_low = attend_back_chip(
        heads_t, attended, agrad.reshape(width // HEAD, HEAD, length), log_total,
        cosine, sine, normal_t, shards, spans, output,
        wt, x_half, rgrad, gains, ctx, nfsdp, groups, seqs,
    )

    shard = [
        sums[n].reshape(-1, D)[: span.stop - span.start].astype(f32)
        for n, span in enumerate(spans)
    ]
    shard = jnp.concatenate(shard, 0)
    cuts = [shard[i * shard_rows : (i + 1) * shard_rows] for i in range(up_parts)]
    up_shard = jnp.concatenate(cuts, -1)
    offset = up_parts * shard_rows
    out_shard = shard[offset : offset + out_weight.shape[0]]
    down_shard = shard[offset + out_weight.shape[0] :]
    pieces = pieces.reshape(-1, 2, shard_rows, 3, 2 * HEAD)
    qkv_shard = jnp.transpose(pieces, (2, 3, 1, 0, 4)).reshape(shard_rows, 3 * D).astype(f32)
    attn_gain_grad = jnp.sum(qkv_weight.astype(f32) * qkv_shard, -1) / attention_gain.astype(f32)
    ffn_gain_grad = jnp.sum(up_weight.astype(f32) * up_shard, -1) / feedforward_gain.astype(f32)
    output = jnp.concatenate([first_rows, last_rows], 1)
    return (
        output,
        token_low.astype(f32),
        qkv_shard,
        out_shard,
        up_shard,
        down_shard,
        attn_gain_grad,
        ffn_gain_grad,
    )


def body(tokens, cotangent, qkv_weight, *others):
    ctx, dp = lax.axis_size("ctx"), lax.axis_size("dp")
    one_each = ctx == 2 * tokens.shape[0] and dp % 2 == 0 and ctx & (ctx - 1) == 0 and HEADS % 4 == 0
    aligned = tokens.shape[1] % 256 == 0 and 2 * qkv_weight.shape[0] % (16 * ctx) == 0
    chosen = chip_body if one_each and aligned else general_body
    return chosen(tokens, cotangent, qkv_weight, *others)


def solution(mesh):
    rows = P(("dp", "fsdp"), "ctx", None)
    weight = P(("dp", "fsdp"), None)
    gain = P(("dp", "fsdp"))
    return jax.shard_map(
        body,
        mesh=mesh,
        in_specs=(rows, rows, weight, weight, weight, weight, gain, gain),
        out_specs=(rows, rows, weight, weight, weight, weight, gain, gain),
        check_vma=False,
    )
```
